32 devices in a mesh: lat: 4 (over y, core), lon: 8 (over z, x).
Axes of the slice: x: 2, y: 2, z: 4, core: 2. Of those that a mesh axis runs over, the one named last changes fastest.
Arguments:
- ensemble: bfloat16 [8, 4, 16, 384, 128], P(None, None, 'lat', 'lon'), may hold values from -5 to 5
- vert_loc: float32 [128, 128], replicated, may hold values from -0.5 to 0.5
- static_vert: float32 [128, 128], replicated, may hold values from -0.5 to 0.5
- inst_vert: float32 [16, 128], replicated, may hold values from -0.5 to 0.5
- inst_err: float32 [16], replicated, may hold values from 0.5 to 2
- obs_dest: int32 [8192, 1], P(('lat', 'lon')), may hold values from 0 to 31; in each aligned block of 256 rows (0 to 255, 256 to 511, ...) at most 16 rows name the same one
- obs_patch: int32 [8192], P(('lat', 'lon')), may hold values from 0 to 47
- obs_window: int32 [8192], P(('lat', 'lon')), may hold values from 0 to 3
- obs_inst: int32 [8192], P(('lat', 'lon')), may hold values from 0 to 15
- obs_hweight: float32 [4, 8192], P(None, ('lat', 'lon')), may hold values from 0 to 0.5
- innovation: float32 [8192], P(('lat', 'lon')), may hold values from -6 to 6
- obs_count: int32 [32], P(('lat', 'lon')), may hold values from 128 to 256, as said below
Outputs:
- static_control: float32 [16, 384, 128], P('lat', 'lon')
- member_control: float32 [8, 16, 384, 128], P(None, 'lat', 'lon')
- obs_equivalent: float32 [8192], P(('lat', 'lon'))
The draws below stay inside these ranges and needn't reach their ends.
Inputs may be any that keep to these rules, and one draw needn't show every extreme that they name: `obs_dest`: index of the tile in lat+lon order (lat slowest) that holds the row's patch; within the rows of one shard no tile is named more than 16 times. `obs_patch`: patch p of a tile covers its latitude rows 2 (p // 24) and the next, and its longitude columns 2 (p % 24) and the next. `obs_count`: some shard uses all 256 rows in every draw; rows at or past a shard's count are unused.
All inputs are finite; a program needn't handle non-finite values.
Results may differ from the reference program's by a relative error of at most 0.0003.
Values sent between devices are 32-bit elements; how exact they have to be, the bound alone decides.
No kernel may reach another device: no remote copies, remote signals or barrier semaphores. Data moves between devices by JAX's collectives and lax.ppermute only.
A program may use at most 64 MiB of HBM per device.

```python
import math
import jax
import jax.numpy as jnp
import numpy as np
from jax import lax

CLAT = 4
CLON = 48
OBS_DEV = 256
MEM = 8
WIN = 4
NINST = 16
ITERS = 2
VL = 128
OWNERS = 32
NLAT = 16
NLON = 384
NOBS = 8192
CAP = 16
PATCH_DEV = 48
N_LON = 8


def draw_obs_count(key, part):
    counts = jax.random.randint(key, (OWNERS,), OBS_DEV // 2, OBS_DEV + 1)
    fullest = jax.random.randint(jax.random.fold_in(key, 7), (), 0, OWNERS)
    return counts.at[fullest].set(OBS_DEV).astype(jnp.int32)


def with_ends(values, own_key, low, high):
    dims = values.shape
    place = [jax.random.randint(jax.random.fold_in(own_key, axis), (), 0, dims[axis]) for axis in range(len(dims))]
    values = values.at[tuple(place)].set(low)
    longest = dims.index(max(dims))
    place[longest] = (place[longest] + 1) % dims[longest]
    return values.at[tuple(place)].set(high)


def block_levels(rng, extent, split, low, largest):
    def one(dim, blocks):
        heights = jax.random.uniform(jax.random.fold_in(jax.random.fold_in(rng, 6), dim), (blocks,), jnp.float32, low / len(split), largest / len(split))
        return jnp.repeat(jnp.exp(heights), extent[dim] // blocks).reshape((-1,) + (1,) * (len(extent) - dim - 1))

    factor_of = one(*split[0])
    for cut in split[1:]:
        factor_of = factor_of * one(*cut)
    return factor_of


def deal_out(key, own, number, rows, amount, top, bound, skew):
    ranking = jax.random.permutation(key, amount)
    crowded, usual = shares(amount, rows * top, bound, skew, True), shares(amount, rows * top, bound, skew, False)
    places = jnp.arange(amount)

    def named(lengths, turn):
        used = int((lengths > 0).sum())
        fixed = max(1, used // 4)
        shifted = fixed + (places - fixed + turn * (used - fixed)) % max(1, amount - fixed)
        return jnp.zeros((amount,), jnp.int32).at[ranking[jnp.where(places < fixed, places, shifted)]].set(jnp.asarray(lengths, jnp.int32))

    lengths = jnp.where(number % 4 == 0, named(crowded, number // 4), named(usual, number - number // 4 - 1))
    mixed = jax.random.permutation(jax.random.fold_in(own, 3), amount)
    giver, receiver = mixed[0:amount // 2 * 2:2], mixed[1:amount // 2 * 2:2]
    margin = jnp.minimum(lengths[giver] - 1, bound - lengths[receiver]) // 2
    margin = jnp.where((giver == ranking[0]) | (receiver == ranking[0]) | (lengths[receiver] == 0), 0, jnp.maximum(margin, 0))
    shifted = jax.random.randint(jax.random.fold_in(own, 4), (amount // 2,), 0, 1 << 20) % (margin + 1)
    lengths = lengths.at[giver].add(-shifted).at[receiver].add(shifted)
    labels = jnp.searchsorted(jnp.cumsum(lengths), jnp.arange(rows * top), side="right").astype(jnp.int32)
    table = labels.reshape(top, rows).T
    table = table[jax.random.permutation(jax.random.fold_in(own, 1), rows)]
    turn = jax.random.randint(jax.random.fold_in(own, 2), (rows, 1), 0, top)
    return jnp.take_along_axis(table, (jnp.arange(top)[None, :] + turn) % top, axis=1)


def shares(number_of, total, reach, slope, full):
    portions = [(1 << 20) // math.isqrt(standing ** slope) + 1 for standing in range(1, number_of + 1)]
    largest = reach if full else min(reach, max(-(-total // number_of), total * portions[0] // sum(portions)))
    least = 1 if total - largest >= number_of - 1 else 0
    given, surplus = [largest] + [least] * (number_of - 1), total - largest - least * (number_of - 1)
    while surplus > 0:
        free = [i for i in range(1, number_of) if given[i] < largest] or [i for i in range(1, number_of) if given[i] < reach]
        mass, left = sum([portions[i] for i in free]), surplus
        for i in free:
            more = min(reach - given[i], max(1, left * portions[i] // mass), surplus)
            given[i] = given[i] + more
            surplus = surplus - more
    return np.array(given)


def bell_draw(own_key, shape, scale, reach, split=(), kind=jnp.bfloat16):
    values = jax.random.normal(own_key, shape, jnp.float32) * scale
    if len(split) > 0:
        values = block_levels(own_key, shape, split, -0.22, 0.18) * values
    return jnp.clip(values, min=-reach, max=reach).astype(kind)


def setup_inputs(seed: int = 0) -> dict:
    streams_of = jax.random.split(jax.random.key(seed), 13)
    ensemble = bell_draw(streams_of[0], (MEM, WIN, NLAT, NLON, VL), 0.35, 5.0, ((2, 4), (3, 8)))
    vert_loc = bell_draw(streams_of[1], (VL, VL), VL ** -0.5, 0.5, (), jnp.float32)
    static_vert = bell_draw(streams_of[2], (VL, VL), VL ** -0.5, 0.5, (), jnp.float32)
    inst_vert = bell_draw(streams_of[3], (NINST, VL), VL ** -0.5, 0.5, (), jnp.float32)
    inst_err = jnp.clip(jnp.exp(jax.random.uniform(streams_of[4], (NINST,), jnp.float32, math.log(0.5), math.log(2.0))), 0.5, 2.0)
    obs_dest_keys = jax.random.split(jax.random.fold_in(streams_of[5], 1), NOBS // OBS_DEV)
    obs_dest_turns = jax.random.permutation(jax.random.fold_in(streams_of[5], 3), NOBS // OBS_DEV)
    obs_dest = jax.vmap(lambda own, number: deal_out(jax.random.fold_in(streams_of[5], 2), own, number, OBS_DEV, OWNERS, 1, CAP, 2))(obs_dest_keys, obs_dest_turns).reshape((NOBS, 1))
    obs_patch = with_ends(jax.random.randint(streams_of[6], (NOBS,), 0, PATCH_DEV), jax.random.fold_in(streams_of[6], 1), 0, PATCH_DEV - 1).astype(jnp.int32)
    obs_window = with_ends(jax.random.randint(streams_of[7], (NOBS,), 0, WIN), jax.random.fold_in(streams_of[7], 1), 0, WIN - 1).astype(jnp.int32)
    obs_inst = with_ends(jax.random.randint(streams_of[8], (NOBS,), 0, NINST), jax.random.fold_in(streams_of[8], 1), 0, NINST - 1).astype(jnp.int32)
    obs_hweight = jnp.clip(0.5 * jax.random.uniform(streams_of[9], (4, NOBS), jnp.float32) ** block_levels(streams_of[9], (4, NOBS), ((1, 32),), -0.2, 0.2), 0.0, 0.5)
    innovation = bell_draw(streams_of[10], (NOBS,), 1.0, 6.0, ((0, 32),), jnp.float32)
    obs_count = draw_obs_count(jax.random.fold_in(streams_of[12], 71), 0)
    return {"ensemble": ensemble, "vert_loc": vert_loc, "static_vert": static_vert, "inst_vert": inst_vert, "inst_err": inst_err, "obs_dest": obs_dest, "obs_patch": obs_patch, "obs_window": obs_window, "obs_inst": obs_inst, "obs_hweight": obs_hweight, "innovation": innovation, "obs_count": obs_count}


SMOOTH = 0.15
BETA_STATIC = 0.5
BETA_ENSEMBLE = 0.85


def level_product(values, matrix):
    flat = values.reshape(-1, values.shape[-1])
    result = jnp.dot(flat, matrix, precision=lax.Precision.HIGHEST, preferred_element_type=jnp.float32)
    return result.reshape(values.shape[:-1] + (matrix.shape[1],))


def smooth_once(grid_field):
    widths = [(0, 0)] * (grid_field.ndim - 3) + [(1, 1), (0, 0), (0, 0)]
    padded = jnp.pad(grid_field, widths)
    northern = padded[..., :-2, :, :]
    southern = padded[..., 2:, :, :]
    eastern = jnp.roll(grid_field, -1, axis=grid_field.ndim - 2)
    western = jnp.roll(grid_field, 1, axis=grid_field.ndim - 2)
    return (1.0 - 4.0 * SMOOTH) * grid_field + SMOOTH * (northern + southern + eastern + western)


def spread(grid_field):
    return smooth_once(smooth_once(grid_field))


def combine(former, scale, latter):
    return (former[0] + scale * latter[0], former[1] + scale * latter[1])


def local_dot(former, latter):
    return jnp.sum(former[0] * latter[0]) + jnp.sum(former[1] * latter[1])


def reference(ensemble, vert_loc, static_vert, inst_vert, inst_err, obs_dest, obs_patch, obs_window, obs_inst, obs_hweight, innovation, obs_count):
    destination = obs_dest[:, 0]
    lat_start = (destination // N_LON) * CLAT + 2 * (obs_patch // (CLON // 2))
    lon_start = (destination % N_LON) * CLON + 2 * (obs_patch % (CLON // 2))
    row_index = jnp.arange(innovation.shape[0], dtype=jnp.int32)
    active = ((row_index % OBS_DEV) < obs_count[row_index // OBS_DEV]).astype(jnp.float32)
    hweights = obs_hweight * active[None, :]
    inverse_var = 1.0 / (inst_err[obs_inst] * inst_err[obs_inst])

    def forward(control):
        static_part = BETA_STATIC * level_product(spread(control[0]), static_vert)

        def add_member(summed, member_pair):
            member_weights, perturbation = member_pair
            localized = level_product(spread(member_weights), vert_loc)
            return summed + perturbation.astype(jnp.float32) * localized[None], None

        initial = jnp.zeros(ensemble.shape[1:], jnp.float32)
        summed, unused = lax.scan(add_member, initial, (control[1], ensemble))
        return static_part[None] + BETA_ENSEMBLE * summed

    def observe(increment):
        projected = level_product(increment, inst_vert.T)
        image = jnp.zeros(innovation.shape, jnp.float32)
        for corner in range(4):
            image = image + hweights[corner] * projected[obs_window, lat_start + corner // 2, lon_start + corner % 2, obs_inst]
        return image

    def gradient(weights):
        table = jnp.zeros(ensemble.shape[1:4] + (inst_vert.shape[0],), jnp.float32)
        for corner in range(4):
            table = table.at[obs_window, lat_start + corner // 2, lon_start + corner % 2, obs_inst].add(hweights[corner] * weights)
        return level_product(table, inst_vert)

    def adjoint(grad_field):
        static_part = BETA_STATIC * spread(level_product(jnp.sum(grad_field, axis=0), static_vert.T))

        def one_member(unused, perturbation):
            localized = jnp.sum(perturbation.astype(jnp.float32) * grad_field, axis=0)
            return unused, BETA_ENSEMBLE * spread(level_product(localized, vert_loc.T))

        unused, member_part = lax.scan(one_member, jnp.zeros((), jnp.float32), ensemble)
        return static_part, member_part

    def hessian(direction):
        obs_image = observe(forward(direction))
        back_field = adjoint(gradient(inverse_var * obs_image))
        return obs_image, combine(direction, 1.0, back_field)

    residual = adjoint(gradient(inverse_var * innovation))
    solution = (jnp.zeros_like(residual[0]), jnp.zeros_like(residual[1]))
    equivalent = jnp.zeros(innovation.shape, jnp.float32)
    direction = residual
    norm_now = local_dot(residual, residual)
    for iteration in range(ITERS):
        obs_image, image = hessian(direction)
        step_size = norm_now / local_dot(direction, image)
        solution = combine(solution, step_size, direction)
        equivalent = equivalent + step_size * obs_image
        residual = combine(residual, -step_size, image)
        norm_next = local_dot(residual, residual)
        direction = combine(residual, norm_next / norm_now, direction)
        norm_now = norm_next
    return solution[0], solution[1], equivalent
```

```python
import functools

import jax
import jax.numpy as jnp
from jax import lax
from jax.experimental import pallas as pl
from jax.experimental.pallas import tpu as pltpu
from jax.sharding import PartitionSpec as P

SMOOTH = 0.15
CENTER = 1.0 - 4.0 * SMOOTH
BETA_STATIC = 0.5
BETA_ENSEMBLE = 0.85
HALO = 4
LANES = 128
HIGHEST = lax.Precision.HIGHEST
F32 = jnp.float32

ANY = pl.BlockSpec(memory_space=pl.ANY)
VMEM = pl.BlockSpec(memory_space=pltpu.VMEM)
SMEM = pl.BlockSpec(memory_space=pltpu.SMEM)
PARAMS = pltpu.CompilerParams(vmem_limit_bytes=48 * 1024 * 1024)


def dot(left, right, dims=((1,), (0,))):
    return lax.dot_general(
        left, right, (dims, ((), ())), precision=HIGHEST, preferred_element_type=F32
    )


def iota(shape, dim):
    return lax.broadcasted_iota(jnp.int32, shape, dim)


def pack_kernel(
    slots, patches, dest_col, dest, patch, window, inst, hweight, innov, count, send, lane, feat
):
    owners = send.shape[0]
    rows = dest.shape[1]
    me = lax.axis_index("lat") * lax.axis_size("lon") + lax.axis_index("lon")
    base = lax.rem(me, LANES // slots) * slots
    destination = dest[...]
    earlier = (dest_col[...] == destination) & (iota((rows, rows), 0) < iota((rows, rows), 1))
    ranking = jnp.sum(jnp.where(earlier, 1.0, 0.0), axis=0, keepdims=True).astype(jnp.int32)
    position = ranking + base
    lane[...] = position
    active = (iota((1, rows), 1) < count[0]).astype(F32)
    feat[...] = jnp.zeros_like(feat)
    feat[0:1] = (window[...] * patches + patch[...]).astype(F32)
    feat[1:2] = inst[...].astype(F32)
    feat[2:6] = hweight[...] * active
    feat[6:7] = innov[...]
    chosen = iota((owners, 8, rows), 0) == destination.reshape(1, 1, rows)
    spread_out = jnp.where(chosen, feat[...][None], 0.0).reshape(owners * 8, rows)
    at_lane = (iota((LANES, rows), 0) == position).astype(F32)
    send[...] = dot(spread_out, at_lane, ((1,), (1,))).reshape(owners, 8, LANES)


def prepare_kernel(vert_loc, static_vert, squares):
    squares[0] = BETA_ENSEMBLE**2 * dot(vert_loc[...], vert_loc[...], ((0,), (0,)))
    squares[1] = BETA_STATIC**2 * dot(static_vert[...], static_vert[...], ((0,), (0,)))


def fill_weights(feat, weights, windows, rows_lat, rows_lon):
    slots = feat.shape[1]
    cell = feat[0:1].astype(jnp.int32)
    half = iota((rows_lon, slots), 0) >> 1
    odd = (iota((rows_lon, slots), 0) & 1) == 1
    corner = [jnp.where(odd, feat[3 + 2 * q : 4 + 2 * q], feat[2 + 2 * q : 3 + 2 * q]) for q in range(2)]
    per_window = rows_lat // 2 * (rows_lon // 2)
    for t in range(windows):
        for a in range(rows_lat):
            first = t * per_window + a // 2 * (rows_lon // 2)
            row = (t * rows_lat + a) * rows_lon
            weights[row : row + rows_lon] = jnp.where(half == cell - first, corner[a % 2], 0.0)


def adjoint_fields(amount, weights, ivert, ens, grad, fields, edge_a, edge_b):
    members, windows, rows_lat, rows_lon, levels = ens.shape
    block = rows_lat * rows_lon
    scaled = ivert[...] * amount
    for t in range(windows):
        rows = slice(t * block, (t + 1) * block)
        grad[rows] = dot(weights[rows], scaled, ((1,), (1,)))
    even = lax.rem(lax.axis_index("lon"), 2) == 0
    upper = iota((8, levels), 0) >= 4

    def put(k, a, value):
        fields[k, a] = value
        east = jnp.where(upper, value[rows_lon - 8 :], 0.0)
        west = jnp.where(upper, 0.0, value[:8])
        edge_a[k, a] = jnp.where(even, east, west)
        edge_b[k, a] = jnp.where(even, west, east)

    for a in range(rows_lat):
        parts = [grad[
            (t * rows_lat + a) * rows_lon : (t * rows_lat + a + 1) * rows_lon
        ] for t in range(windows)]
        for k in range(members):
            total = ens[k, 0, a].astype(F32) * parts[0]
            for t in range(1, windows):
                total = total + ens[k, t, a].astype(F32) * parts[t]
            put(k, a, total)
        total = parts[0]
        for t in range(1, windows):
            total = total + parts[t]
        put(members, a, total)


def first_kernel(
    slots,
    recv,
    inst_vert,
    inst_err,
    ens_hbm,
    feat,
    ivert,
    fields,
    edge_a,
    edge_b,
    ens,
    weights,
    grad,
    sem,
):
    copy = pltpu.make_async_copy(ens_hbm, ens, sem)
    copy.start()
    members, windows, rows_lat, rows_lon, levels = ens.shape
    owners = recv.shape[0]
    per = LANES // slots
    for g in range(owners // per):
        feat[:, g * LANES : (g + 1) * LANES] = jnp.sum(recv[g * per : (g + 1) * per], axis=0)
    instruments = inst_vert.shape[0]
    total = feat.shape[1]
    onehot = (iota((instruments, total), 0) == feat[1:2].astype(jnp.int32)).astype(F32)
    ivert[...] = dot(inst_vert[...].T, onehot)
    inverse = jnp.broadcast_to(1.0 / (inst_err[...] * inst_err[...]), (8, instruments))
    rinv = dot(inverse, onehot)[0:1]
    feat[6:7] = feat[6:7] * rinv
    feat[7:8] = rinv
    fill_weights(feat, weights, windows, rows_lat, rows_lon)
    copy.wait()
    adjoint_fields(feat[6:7], weights, ivert, ens, grad, fields, edge_a, edge_b)


def halo_copies(own, lat_a, lat_b, cross, corner_a, corner_b, field, sems):
    rows_lat, rows_lon = own.shape[1:3]
    odd = lax.rem(lax.axis_index("lat"), 2)
    south = HALO + rows_lat
    row_a = south * (1 - odd)
    row_b = south * odd
    far_a = (rows_lat - HALO) * odd
    far_b = (rows_lat - HALO) * (1 - odd)
    main = pl.ds(0, rows_lon)
    side = pl.ds(rows_lon, 8)
    mid = pl.ds(HALO, rows_lat)
    plan = (
        (own, field.at[:, mid, main]),
        (cross, field.at[:, mid, side]),
        (lat_a.at[:, pl.ds(far_a, HALO)], field.at[:, pl.ds(row_a, HALO), main]),
        (lat_b.at[:, pl.ds(far_b, HALO)], field.at[:, pl.ds(row_b, HALO), main]),
        (corner_a.at[:, pl.ds(far_a, HALO)], field.at[:, pl.ds(row_a, HALO), side]),
        (corner_b.at[:, pl.ds(far_b, HALO)], field.at[:, pl.ds(row_b, HALO), side]),
    )
    return [pltpu.make_async_copy(s, d, sems.at[n]) for n, (s, d) in enumerate(plan)]


def smooth_power(field, powers, out, order):
    count, rows, width, levels = field.shape
    rows_lat = rows - 2 * HALO
    rows_lon = width - 8
    lat = lax.axis_index("lat")
    north = (lat > 0).astype(F32)
    south = (lat < lax.axis_size("lat") - 1).astype(F32)
    factor = {2: (2.0, 1.0), 4: (4.0, 6.0, 4.0, 1.0)}[order]

    def one(k, carry):
        for c in range(width // 8):
            cols = slice(8 * c, 8 * c + 8)
            low = HALO - order
            line = {i: field[k, i, cols] for i in range(low, rows - low)}
            for m in range(1, order + 1):
                fresh = {}
                for i in range(low + m, rows - low - m):
                    value = line[i - 1] + line[i + 1]
                    if i < HALO:
                        value = value * north
                    if i >= HALO + rows_lat:
                        value = value * south
                    fresh[i] = value
                line = fresh
                for i in range(rows_lat):
                    powers[m - 1, i, cols] = line[HALO + i]
        for i in range(rows_lat):
            value = field[k, HALO + i]
            for m in range(1, order + 1):
                ring = pltpu.roll(value, 1, 0) + pltpu.roll(value, width - 1, 0)
                value = CENTER * value + SMOOTH * ring
                value = value + (factor[m - 1] * SMOOTH**m) * powers[m - 1, i]
            out[k, i] = value[:rows_lon]
        return carry

    lax.fori_loop(0, count, one, 0)


def observe(field, powers, smooth, mixed, squares, ivert, weights, ens, ens_copy):
    members, windows, rows_lat, rows_lon, levels = ens.shape
    block = rows_lat * rows_lon
    smooth_power(field, powers, smooth, 4)
    shape = (rows_lat, rows_lon, levels)
    for k in range(members + 1):
        square = squares[0] if k < members else squares[1]
        mixed[k] = dot(smooth[k].reshape(block, levels), square).reshape(shape)
    ens_copy.wait()
    slots = weights.shape[1]
    image = jnp.zeros((8, slots), F32)
    for t in range(windows):
        lines = []
        for a in range(rows_lat):
            total = mixed[members, a]
            for k in range(members):
                total = total + ens[k, t, a].astype(F32) * mixed[k, a]
            lines.append(total)
        increment = jnp.stack(lines).reshape(block, levels)
        seen = dot(increment, ivert[...]) * weights[t * block : (t + 1) * block]
        image = image + jnp.sum(seen.reshape(block // 8, 8, slots), axis=0)
    return jnp.sum(image, axis=0, keepdims=True)


def middle_kernel(
    own, lat_a, lat_b, cross, corner_a, corner_b, ens_hbm, feat, ivert, squares,
    image, fields, edge_a, edge_b,
    ens, field, powers, smooth, mixed, weights, grad, sem, sems,
):
    copies = halo_copies(own, lat_a, lat_b, cross, corner_a, corner_b, field, sems)
    for copy in copies:
        copy.start()
    ens_copy = pltpu.make_async_copy(ens_hbm, ens, sem)
    ens_copy.start()
    members, windows, rows_lat, rows_lon, levels = ens.shape
    fill_weights(feat, weights, windows, rows_lat, rows_lon)
    for copy in copies:
        copy.wait()
    seen = observe(field, powers, smooth, mixed, squares, ivert, weights, ens, ens_copy)
    scaled = seen * feat[7:8]
    image[...] = jnp.zeros_like(image)
    image[0:1] = seen
    image[1:2] = scaled
    adjoint_fields(scaled, weights, ivert, ens, grad, fields, edge_a, edge_b)


def last_kernel(
    slots,
    own, lat_a, lat_b, cross, corner_a, corner_b, ens_hbm, feat, ivert, squares, image,
    send,
    ens, field, powers, smooth, mixed, weights, terms, sem, sems,
):
    copies = halo_copies(own, lat_a, lat_b, cross, corner_a, corner_b, field, sems)
    for copy in copies:
        copy.start()
    ens_copy = pltpu.make_async_copy(ens_hbm, ens, sem)
    ens_copy.start()
    members, windows, rows_lat, rows_lon, levels = ens.shape
    fill_weights(feat, weights, windows, rows_lat, rows_lon)
    for copy in copies:
        copy.wait()
    second = observe(field, powers, smooth, mixed, squares, ivert, weights, ens, ens_copy)
    start = feat[6:7]
    rinv = feat[7:8]
    first = image[0:1]
    scaled = image[1:2]
    norm = jnp.sum(start * first, axis=1, keepdims=True)
    curve = norm + jnp.sum(first * scaled, axis=1, keepdims=True)
    guess = jnp.where(curve > 0.0, norm / jnp.where(curve > 0.0, curve, 1.0), 1.0)
    guess = jnp.clip(guess, 0.0, 1.0)
    ahead = start + scaled
    ahead_image = first + second
    rest = start - guess * ahead
    rest_image = first - guess * ahead_image
    products = (
        start * first,
        first * scaled,
        rest * rest_image,
        rest * ahead_image + ahead * rest_image,
        ahead * ahead_image,
        rest_image * rinv * rest_image,
        2.0 * rest_image * rinv * ahead_image,
        ahead_image * rinv * ahead_image,
        2.0 * rest_image * scaled,
        2.0 * ahead_image * scaled,
        start * rest_image + rest * first,
        start * ahead_image + ahead * first,
    )
    terms[...] = jnp.zeros_like(terms)
    for n, value in enumerate(products):
        terms[n : n + 1] = value
    sums = jnp.sum(terms[...], axis=1, keepdims=True)
    square = (16, LANES)
    line = jnp.sum(
        jnp.where(iota(square, 0) == iota(square, 1), sums, 0.0), axis=0, keepdims=True
    )
    owners = send.shape[0]
    per = LANES // slots
    row = iota((8, LANES), 0)
    for g in range(owners // per):
        lanes = slice(g * LANES, (g + 1) * LANES)
        block = jnp.where(row == 0, first[:, lanes], 0.0)
        block = jnp.where(row == 1, second[:, lanes], block)
        block = jnp.where(row == 2, line, block)
        block = jnp.where(row == 3, guess, block)
        send[g * per : (g + 1) * per] = jnp.broadcast_to(block[None], (per, 8, LANES))


def control_kernel(
    own, lat_a, lat_b, cross, corner_a, corner_b, vert_loc, static_vert,
    control,
    field, powers, smooth, sems,
):
    copies = halo_copies(own, lat_a, lat_b, cross, corner_a, corner_b, field, sems)
    for copy in copies:
        copy.start()
    for copy in copies:
        copy.wait()
    smooth_power(field, powers, smooth, 2)
    count, rows_lat, rows_lon, levels = smooth.shape
    for k in range(count):
        scale, matrix = (BETA_ENSEMBLE, vert_loc) if k < count - 1 else (BETA_STATIC, static_vert)
        value = dot(smooth[k].reshape(rows_lat * rows_lon, levels), matrix[...], ((1,), (1,)))
        control[k] = (scale * value).reshape(rows_lat, rows_lon, levels)


def final_kernel(recv, dest, lane, early, late, static, member, equivalent):
    owners = recv.shape[0]
    rows = dest.shape[1]
    blocks = recv[...]
    line = blocks[:, 2:3]
    sums = jnp.sum(line, axis=0)

    def pick(values, n):
        return values[:, n : n + 1]

    norm = pick(sums, 0)
    step = norm / (norm + pick(sums, 1))
    off = blocks[:, 3:4] - step[None]
    linear = jnp.sum(off * line, axis=0)
    square = jnp.sum(off * off * line, axis=0)
    norm_next = jnp.maximum(pick(sums, 2) + pick(linear, 3) + pick(square, 4), 0.0)
    beta = norm_next / norm
    bend = pick(sums, 5) + pick(linear, 6) + pick(square, 7)
    bend = bend + beta * (pick(sums, 8) + pick(linear, 9)) + beta * beta * pick(sums, 1)
    length = norm_next + beta * (pick(sums, 10) + pick(linear, 11)) + beta * beta * norm
    curve = length + bend
    step_next = jnp.where(curve > 0.0, norm_next / jnp.where(curve > 0.0, curve, 1.0), 0.0)
    step_next = jnp.minimum(step_next, 1.0)
    near = step + step_next * ((1.0 - step) + beta)
    far = -step_next * step
    members = member.shape[0]
    for k in range(members):
        member[k] = near[None] * early[k] + far[None] * late[k]
    static[...] = near[None] * early[members] + far[None] * late[members]
    kind = iota((owners, 8, rows), 1)
    factor = jnp.where(kind == 0, near[None], jnp.where(kind == 1, far[None], 0.0))
    chosen = iota((owners, 8, rows), 0) == dest[...].reshape(1, 1, rows)
    picked = jnp.where(chosen, factor, 0.0).reshape(owners * 8, rows)
    table = dot(blocks.reshape(owners * 8, LANES), picked, ((0,), (0,)))
    equivalent[...] = jnp.sum(
        jnp.where(iota((LANES, rows), 0) == lane[...], table, 0.0), axis=0, keepdims=True
    )


def shape(*dims):
    return jax.ShapeDtypeStruct(dims, F32)


def swaps(count, ring):
    inner = [(i, i ^ 1) for i in range(count)]
    outer = []
    for i in range(1, count - 1, 2):
        outer += [(i, i + 1), (i + 1, i)]
    if ring:
        outer += [(count - 1, 0), (0, count - 1)]
    return inner, outer


def body(
    ensemble,
    vert_loc,
    static_vert,
    inst_vert,
    inst_err,
    obs_dest,
    obs_patch,
    obs_window,
    obs_inst,
    obs_hweight,
    innovation,
    obs_count,
):
    members, windows, rows_lat, rows_lon, levels = ensemble.shape
    lat_count = lax.axis_size("lat")
    lon_count = lax.axis_size("lon")
    owners = lat_count * lon_count
    rows = innovation.shape[0]
    slots = 2 * rows // owners
    total = owners * slots
    patches = rows_lat // 2 * (rows_lon // 2)
    count = members + 1
    width = rows_lon + 8
    lat_inner, lat_outer = swaps(lat_count, False)
    lon_inner, lon_outer = swaps(lon_count, True)
    tile = shape(count, rows_lat, rows_lon, levels)
    edge = shape(count, rows_lat, 8, levels)

    def line(values):
        return values.reshape(1, rows)

    dest = line(obs_dest)
    send, lane = pl.pallas_call(
        functools.partial(pack_kernel, slots, patches),
        out_shape=(shape(owners, 8, LANES), jax.ShapeDtypeStruct((1, rows), jnp.int32)),
        in_specs=[VMEM] * 7 + [SMEM],
        out_specs=(VMEM, VMEM),
        scratch_shapes=[pltpu.VMEM((8, rows), F32)],
        compiler_params=PARAMS,
        name="pack",
    )(
        obs_dest,
        dest,
        line(obs_patch),
        line(obs_window),
        line(obs_inst),
        obs_hweight,
        line(innovation),
        obs_count,
    )
    squares = pl.pallas_call(
        prepare_kernel,
        out_shape=shape(2, levels, levels),
        compiler_params=PARAMS,
        name="prepare",
    )(vert_loc, static_vert)

    def exchange(blocks):
        return lax.all_to_all(blocks, ("lat", "lon"), split_axis=0, concat_axis=0, tiled=True)

    recv = exchange(send)
    ens_scratch = pltpu.VMEM(ensemble.shape, ensemble.dtype)
    field_scratch = pltpu.VMEM((count, rows_lat + 2 * HALO, width, levels), F32)
    tile_scratch = pltpu.VMEM(tile.shape, F32)
    weight_scratch = pltpu.VMEM((windows * rows_lat * rows_lon, total), F32)
    grad_scratch = pltpu.VMEM((windows * rows_lat * rows_lon, levels), F32)

    def powers(order):
        return pltpu.VMEM((order, rows_lat, width, levels), F32)

    feat, ivert, fields, edge_a, edge_b = pl.pallas_call(
        functools.partial(first_kernel, slots),
        out_shape=(shape(8, total), shape(levels, total), tile, edge, edge),
        in_specs=[VMEM, VMEM, VMEM, ANY],
        out_specs=(VMEM,) * 5,
        scratch_shapes=[ens_scratch, weight_scratch, grad_scratch, pltpu.SemaphoreType.DMA],
        compiler_params=PARAMS,
        name="first",
    )(recv, inst_vert, inst_err.reshape(1, -1), ensemble)

    def halo(fields, edge_a, edge_b):
        lat_b = lax.ppermute(fields, "lat", lat_outer)
        side_a = lax.ppermute(edge_a, "lon", lon_inner)
        side_b = lax.ppermute(edge_b, "lon", lon_outer)
        lat_a = lax.ppermute(fields, "lat", lat_inner)
        cross = side_a + side_b
        corner_b = lax.ppermute(cross, "lat", lat_outer)
        corner_a = lax.ppermute(cross, "lat", lat_inner)
        return (fields, lat_a, lat_b, cross, corner_a, corner_b)

    def control(parts):
        return pl.pallas_call(
            control_kernel,
            out_shape=tile,
            in_specs=[ANY] * 6 + [VMEM] * 2,
            out_specs=VMEM,
            scratch_shapes=[
                field_scratch,
                powers(2),
                tile_scratch,
                pltpu.SemaphoreType.DMA((6,)),
            ],
            compiler_params=PARAMS,
            name="control",
        )(*parts, vert_loc, static_vert)

    parts = halo(fields, edge_a, edge_b)
    work = [ens_scratch, field_scratch, powers(4), tile_scratch, tile_scratch, weight_scratch]
    sems = [pltpu.SemaphoreType.DMA, pltpu.SemaphoreType.DMA((6,))]
    image, fields, edge_a, edge_b = pl.pallas_call(
        middle_kernel,
        out_shape=(shape(8, total), tile, edge, edge),
        in_specs=[ANY] * 7 + [VMEM] * 3,
        out_specs=(VMEM,) * 4,
        scratch_shapes=work + [grad_scratch] + sems,
        compiler_params=PARAMS,
        name="middle",
    )(*parts, ensemble, feat, ivert, squares)
    early = control(parts)
    parts = halo(fields, edge_a, edge_b)
    send = pl.pallas_call(
        functools.partial(last_kernel, slots),
        out_shape=shape(owners, 8, LANES),
        in_specs=[ANY] * 7 + [VMEM] * 4,
        out_specs=VMEM,
        scratch_shapes=work + [pltpu.VMEM((16, total), F32)] + sems,
        compiler_params=PARAMS,
        name="last",
    )(*parts, ensemble, feat, ivert, squares, image)
    late = control(parts)
    recv = exchange(send)
    static, member, equivalent = pl.pallas_call(
        final_kernel,
        out_shape=(
            shape(rows_lat, rows_lon, levels),
            shape(members, rows_lat, rows_lon, levels),
            shape(1, rows),
        ),
        compiler_params=PARAMS,
        name="final",
    )(recv, dest, lane, early, late)
    return static, member, equivalent.reshape(rows)


def solution(mesh):
    return jax.shard_map(
        body,
        mesh=mesh,
        in_specs=(
            P(None, None, "lat", "lon", None),
            P(),
            P(),
            P(),
            P(),
            P(("lat", "lon"), None),
            P(("lat", "lon")),
            P(("lat", "lon")),
            P(("lat", "lon")),
            P(None, ("lat", "lon")),
            P(("lat", "lon")),
            P(("lat", "lon")),
        ),
        out_specs=(P("lat", "lon", None), P(None, "lat", "lon", None), P(("lat", "lon"))),
        check_vma=False,
    )
```

```python
import functools

import jax
import jax.numpy as jnp
from jax import lax
from jax.experimental import pallas as pl
from jax.experimental.pallas import tpu as pltpu
from jax.sharding import PartitionSpec as P


SMOOTH = 0.15
CENTER = 1.0 - 4.0 * SMOOTH
BETA_STATIC = 0.5
BETA_ENSEMBLE = 0.85
HALO = 4
FOLD = 3
LANES = 128
HIGHEST = lax.Precision.HIGHEST
F32 = jnp.float32

ANY = pl.BlockSpec(memory_space=pl.ANY)
HBM = pl.BlockSpec(memory_space=pltpu.HBM)
VMEM = pl.BlockSpec(memory_space=pltpu.VMEM)
SMEM = pl.BlockSpec(memory_space=pltpu.SMEM)
PARAMS = pltpu.CompilerParams(vmem_limit_bytes=32 * 1024 * 1024)
DMA = pltpu.SemaphoreType.DMA


def dot(left, right, dims=((1,), (0,))):
    return lax.dot_general(
        left, right, (dims, ((), ())), precision=HIGHEST, preferred_element_type=F32
    )


def iota(shape, dim):
    return lax.broadcasted_iota(jnp.int32, shape, dim)


def fetch(sources, targets, sems):
    copies = [
        pltpu.make_async_copy(source, target, sems.at[n])
        for n, (source, target) in enumerate(zip(sources, targets))
    ]
    for copy in copies:
        copy.start()
    return copies


def wait_all(copies):
    for copy in copies:
        copy.wait()


def pack_kernel(
    slots, patches,
    dest_hbm, patch_hbm, window_hbm, inst_hbm, hweight_hbm, innov_hbm, count,
    send, lane_hbm,
    dest, patch, window, inst, hweight, innov, feat, lane, sems,
):
    wait_all(
        fetch(
            (dest_hbm, patch_hbm, window_hbm, inst_hbm, hweight_hbm, innov_hbm),
            (dest, patch, window, inst, hweight, innov),
            sems,
        )
    )
    owners = send.shape[0]
    rows = dest.shape[1]
    me = lax.axis_index("lat") * lax.axis_size("lon") + lax.axis_index("lon")
    base = lax.rem(me, LANES // slots) * slots
    destination = dest[...]
    row, col = iota((rows, rows), 0), iota((rows, rows), 1)
    upright = jnp.sum(
        jnp.where(row == col, destination.astype(F32), 0.0), axis=1, keepdims=True
    ).astype(jnp.int32)
    earlier = (upright == destination) & (row < col)
    ranking = jnp.sum(jnp.where(earlier, 1.0, 0.0), axis=0, keepdims=True).astype(jnp.int32)
    position = ranking + base
    lane[...] = position
    lane_copy = pltpu.make_async_copy(lane, lane_hbm, sems.at[6])
    lane_copy.start()
    active = (iota((1, rows), 1) < count[0]).astype(F32)
    feat[...] = jnp.zeros_like(feat)
    feat[0:1] = (window[...] * patches + patch[...]).astype(F32)
    feat[1:2] = inst[...].astype(F32)
    feat[2:6] = hweight[...] * active
    feat[6:7] = innov[...]
    chosen = iota((owners, 8, rows), 0) == destination.reshape(1, 1, rows)
    spread_out = jnp.where(chosen, feat[...][None], 0.0).reshape(owners * 8, rows)
    at_lane = (iota((LANES, rows), 0) == position).astype(F32)
    send[...] = dot(spread_out, at_lane, ((1,), (1,))).reshape(owners, 8, LANES)
    lane_copy.wait()


def prepare_kernel(vert_loc, static_vert, squares):
    squares[0] = BETA_ENSEMBLE**2 * dot(vert_loc[...], vert_loc[...], ((0,), (0,)))
    squares[1] = BETA_STATIC**2 * dot(static_vert[...], static_vert[...], ((0,), (0,)))


def fill_weights(feat, weights, windows, rows_lat, rows_lon):
    slots = feat.shape[1]
    cell = feat[0:1].astype(jnp.int32)
    half = iota((rows_lon, slots), 0) >> 1
    odd = (iota((rows_lon, slots), 0) & 1) == 1
    corner = [jnp.where(odd, feat[3 + 2 * q : 4 + 2 * q], feat[2 + 2 * q : 3 + 2 * q]) for q in range(2)]
    per_window = rows_lat // 2 * (rows_lon // 2)
    for t in range(windows):
        for a in range(rows_lat):
            first = t * per_window + a // 2 * (rows_lon // 2)
            row = (t * rows_lat + a) * rows_lon
            weights[row : row + rows_lon] = jnp.where(half == cell - first, corner[a % 2], 0.0)


def adjoint_fields(amount, weights, ivert, ens, ens_copies, grad, outs):
    fields, edge_a, edge_b = outs
    members, windows, rows_lat, rows_lon, _ = ens.shape
    block = rows_lat * rows_lon
    scaled = ivert[...] * amount
    for t in range(windows):
        rows = slice(t * block, (t + 1) * block)
        grad[rows] = dot(weights[rows], scaled, ((1,), (1,)))
    even = lax.rem(lax.axis_index("lon"), 2) == 0

    def part(t, a):
        first = (t * rows_lat + a) * rows_lon
        return grad[first : first + rows_lon]

    for k in range(members + 1):
        if k < members and ens_copies:
            ens_copies[k].wait()
        for a in range(rows_lat):
            total = part(0, a) if k == members else ens[k, 0, a].astype(F32) * part(0, a)
            for t in range(1, windows):
                term = part(t, a) if k == members else ens[k, t, a].astype(F32) * part(t, a)
                total = total + term
            fields[k, a] = total
            east = total[rows_lon - HALO :]
            west = total[:HALO]
            edge_a[k, a] = jnp.where(even, east, west)
            edge_b[k, a] = jnp.where(even, west, east)


def first_kernel(
    slots,
    recv, inst_vert_hbm, inst_err_hbm, ens_hbm,
    feat, ivert, fields, edge_a, edge_b,
    inst_vert, inst_err, ens, weights, grad, sems,
):
    members = ens.shape[0]
    copies = fetch(
        [inst_vert_hbm, inst_err_hbm] + [ens_hbm.at[k] for k in range(members)],
        [inst_vert, inst_err] + [ens.at[k] for k in range(members)],
        sems,
    )
    members, windows, rows_lat, rows_lon, _ = ens.shape
    owners = recv.shape[0]
    per = LANES // slots
    for g in range(owners // per):
        feat[:, g * LANES : (g + 1) * LANES] = jnp.sum(recv[g * per : (g + 1) * per], axis=0)
    wait_all(copies[:2])
    instruments = inst_vert.shape[0]
    total = feat.shape[1]
    onehot = (iota((instruments, total), 0) == feat[1:2].astype(jnp.int32)).astype(F32)
    ivert[...] = dot(inst_vert[...].T, onehot)
    inverse = jnp.broadcast_to(1.0 / (inst_err[...] * inst_err[...]), (8, instruments))
    rinv = dot(inverse, onehot)[0:1]
    feat[6:7] = feat[6:7] * rinv
    feat[7:8] = rinv
    fill_weights(feat, weights, windows, rows_lat, rows_lon)
    outs = (fields, edge_a, edge_b)
    adjoint_fields(feat[6:7], weights, ivert, ens, copies[2:], grad, outs)


def halo_copies(own, lat_a, lat_b, cross, corner_a, corner_b, field, sems):
    rows_lat, rows_lon = own.shape[1:3]
    odd = lax.rem(lax.axis_index("lat"), 2)
    south = HALO + rows_lat
    row_a = south * (1 - odd)
    row_b = south * odd
    far_a = (rows_lat - HALO) * odd
    far_b = (rows_lat - HALO) * (1 - odd)
    main = pl.ds(0, rows_lon)
    side = pl.ds(rows_lon, 8)
    mid = pl.ds(HALO, rows_lat)
    plan = (
        (own, field.at[:, mid, main]),
        (cross, field.at[:, mid, side]),
        (lat_a.at[:, pl.ds(far_a, HALO)], field.at[:, pl.ds(row_a, HALO), main]),
        (lat_b.at[:, pl.ds(far_b, HALO)], field.at[:, pl.ds(row_b, HALO), main]),
        (corner_a.at[:, pl.ds(far_a, HALO)], field.at[:, pl.ds(row_a, HALO), side]),
        (corner_b.at[:, 0], field.at[:, row_b + (HALO - 1) * (1 - odd), side]),
        (corner_b.at[:, 1], field.at[:, row_b + (HALO - 2) * (1 - odd) + odd, side]),
    )
    unused = row_b + (HALO - 1) * odd
    field[:, pl.ds(unused, 1), rows_lon:] = jnp.zeros_like(field[:, pl.ds(unused, 1), rows_lon:])
    return [pltpu.make_async_copy(s, d, sems.at[n]) for n, (s, d) in enumerate(plan)]


def unfold_corner(field, rows_lon):
    odd = lax.rem(lax.axis_index("lat"), 2)
    row_b = (field.shape[1] - HALO) * odd
    second = row_b + (HALO - 2) * (1 - odd) + odd
    third = row_b + (HALO - 3) * (1 - odd) + 2 * odd
    for k in range(field.shape[0]):
        field[k, third, rows_lon:] = pltpu.roll(field[k, second, rows_lon:], 8 - FOLD, 0)


def sides_kernel(part_a, part_b, cross, folded):
    count, rows_lat, _, levels = part_a.shape
    even = lax.rem(lax.axis_index("lon"), 2) == 0
    odd = lax.rem(lax.axis_index("lat"), 2) == 1
    index = iota((8, levels), 0)
    inner = (index == FOLD - 1) | (index == FOLD)
    for k in range(count):
        rows = []
        for a in range(rows_lat):
            first = jnp.where(even, part_a[k, a], part_b[k, a])
            second = jnp.where(even, part_b[k, a], part_a[k, a])
            rows.append(jnp.concatenate([first, second], axis=0))
            cross[k, a] = rows[a]
        near = [jnp.where(odd, rows[rows_lat - 1 - r], rows[r]) for r in range(HALO - 1)]
        folded[k, 0] = near[0]
        folded[k, 1] = jnp.where(inner, pltpu.roll(near[2], FOLD, 0), near[1])


def keep_copy(field, kept, sems):
    inner = pl.ds(HALO // 2, field.shape[1] - HALO)
    return pltpu.make_async_copy(field.at[:, inner], kept, sems.at[7])


def smooth_power(field, powers, out, order):
    count, rows, width, _ = field.shape
    rows_lat = rows - 2 * order
    rows_lon = width - 8
    lat = lax.axis_index("lat")
    north = (lat > 0).astype(F32)
    south = (lat < lax.axis_size("lat") - 1).astype(F32)
    factor = {2: (2.0, 1.0), 4: (4.0, 6.0, 4.0, 1.0)}[order]

    def one(k, carry):
        for c in range(width // 8):
            cols = slice(8 * c, 8 * c + 8)
            line = {i: field[k, i, cols] for i in range(rows)}
            for m in range(1, order + 1):
                fresh = {}
                for i in range(m, rows - m):
                    value = line[i - 1] + line[i + 1]
                    if i < order:
                        value = value * north
                    if i >= order + rows_lat:
                        value = value * south
                    fresh[i] = value
                line = fresh
                for i in range(rows_lat):
                    powers[m - 1, i, cols] = line[order + i]
        for i in range(rows_lat):
            value = field[k, order + i]
            for m in range(1, order + 1):
                ring = pltpu.roll(value, 1, 0) + pltpu.roll(value, width - 1, 0)
                value = CENTER * value + SMOOTH * ring
                value = value + (factor[m - 1] * SMOOTH**m) * powers[m - 1, i]
            out[k, i] = value[:rows_lon]
        return carry

    lax.fori_loop(0, count, one, 0)


def observe(field, powers, smooth, mixed, squares, ivert, weights, ens, ens_copy):
    members, windows, rows_lat, rows_lon, levels = ens.shape
    block = rows_lat * rows_lon
    smooth_power(field, powers, smooth, 4)
    shape = (rows_lat, rows_lon, levels)
    for k in range(members + 1):
        square = squares[0] if k < members else squares[1]
        mixed[k] = dot(smooth[k].reshape(block, levels), square).reshape(shape)
    ens_copy.wait()
    slots = weights.shape[1]
    image = jnp.zeros((8, slots), F32)
    for t in range(windows):
        lines = []
        for a in range(rows_lat):
            total = mixed[members, a]
            for k in range(members):
                total = total + ens[k, t, a].astype(F32) * mixed[k, a]
            lines.append(total)
        increment = jnp.stack(lines).reshape(block, levels)
        seen = dot(increment, ivert[...]) * weights[t * block : (t + 1) * block]
        image = image + jnp.sum(seen.reshape(block // 8, 8, slots), axis=0)
    return jnp.sum(image, axis=0, keepdims=True)


def middle_kernel(
    own, lat_a, lat_b, cross, corner_a, corner_b, ens_hbm, feat, ivert, squares,
    image, kept, fields, edge_a, edge_b,
    ens, field, powers, smooth, mixed, weights, grad, sem, sems,
):
    copies = halo_copies(own, lat_a, lat_b, cross, corner_a, corner_b, field, sems)
    for copy in copies:
        copy.start()
    ens_copy = pltpu.make_async_copy(ens_hbm, ens, sem)
    ens_copy.start()
    _, windows, rows_lat, rows_lon, _ = ens.shape
    fill_weights(feat, weights, windows, rows_lat, rows_lon)
    wait_all(copies)
    unfold_corner(field, rows_lon)
    keep = keep_copy(field, kept, sems)
    keep.start()
    seen = observe(field, powers, smooth, mixed, squares, ivert, weights, ens, ens_copy)
    scaled = seen * feat[7:8]
    image[...] = jnp.zeros_like(image)
    image[0:1] = seen
    image[1:2] = scaled
    outs = (fields, edge_a, edge_b)
    adjoint_fields(scaled, weights, ivert, ens, (), grad, outs)
    keep.wait()


def last_kernel(
    slots,
    own, lat_a, lat_b, cross, corner_a, corner_b, ens_hbm, early, feat, ivert, squares, image,
    send, kept,
    ens, field, powers, smooth, mixed, weights, terms, sem, sems,
):
    copies = halo_copies(own, lat_a, lat_b, cross, corner_a, corner_b, field, sems)
    for copy in copies:
        copy.start()
    ens_copy = pltpu.make_async_copy(ens_hbm, ens, sem)
    ens_copy.start()
    _, windows, rows_lat, rows_lon, _ = ens.shape
    fill_weights(feat, weights, windows, rows_lat, rows_lon)
    wait_all(copies)
    unfold_corner(field, rows_lon)
    keep = keep_copy(field, kept, sems)
    keep.start()
    second = observe(field, powers, smooth, mixed, squares, ivert, weights, ens, ens_copy)
    start = feat[6:7]
    rinv = feat[7:8]
    first = image[0:1]
    scaled = image[1:2]
    norm = jnp.sum(start * first, axis=1, keepdims=True)
    curve = norm + jnp.sum(first * scaled, axis=1, keepdims=True)
    guess = jnp.where(curve > 0.0, norm / jnp.where(curve > 0.0, curve, 1.0), 1.0)
    guess = jnp.clip(guess, 0.0, 1.0)
    ahead = start + scaled
    ahead_image = first + second
    rest = start - guess * ahead
    rest_image = first - guess * ahead_image
    products = (
        start * first,
        first * scaled,
        rest * rest_image,
        rest * ahead_image + ahead * rest_image,
        ahead * ahead_image,
        rest_image * rinv * rest_image,
        2.0 * rest_image * rinv * ahead_image,
        ahead_image * rinv * ahead_image,
        2.0 * rest_image * scaled,
        2.0 * ahead_image * scaled,
        start * rest_image + rest * first,
        start * ahead_image + ahead * first,
    )
    terms[...] = jnp.zeros_like(terms)
    for n, value in enumerate(products):
        terms[n : n + 1] = value
    sums = jnp.sum(terms[...], axis=1, keepdims=True)
    square = (16, LANES)
    line = jnp.sum(
        jnp.where(iota(square, 0) == iota(square, 1), sums, 0.0), axis=0, keepdims=True
    )
    owners = send.shape[0]
    per = LANES // slots
    row = iota((8, LANES), 0)
    for g in range(owners // per):
        lanes = slice(g * LANES, (g + 1) * LANES)
        block = jnp.where(row == 0, first[:, lanes], 0.0)
        block = jnp.where(row == 1, second[:, lanes], block)
        block = jnp.where(row == 2, line, block)
        block = jnp.where(row == 3, guess, block)
        send[g * per : (g + 1) * per] = jnp.broadcast_to(block[None], (per, 8, LANES))
    keep.wait()


def control_kernel(
    kept, vert_hbm, static_hbm,
    control,
    field, powers, smooth, result, vert_loc, static_vert, sems, out_sems,
):
    copies = fetch((vert_hbm, static_hbm, kept), (vert_loc, static_vert, field), sems)
    wait_all(copies)
    count, rows_lat, rows_lon, levels = smooth.shape
    smooth_power(field, powers, smooth, 2)
    stores = []
    for k in range(count):
        member = k < count - 1
        scale, matrix = (BETA_ENSEMBLE, vert_loc) if member else (BETA_STATIC, static_vert)
        value = dot(smooth[k].reshape(rows_lat * rows_lon, levels), matrix[...], ((1,), (1,)))
        result[k] = (scale * value).reshape(rows_lat, rows_lon, levels)
        stores.append(pltpu.make_async_copy(result.at[k], control.at[k], out_sems.at[k]))
        stores[k].start()
    wait_all(stores)


def final_kernel(
    recv, dest_hbm, lane_hbm, early_hbm, late_hbm,
    static_hbm, member_hbm, equivalent,
    dest, lane, early, late, result, sems, field_sems,
):
    small = fetch((dest_hbm, lane_hbm), (dest, lane), sems)
    count = early.shape[0]
    large = []
    for k in range(count):
        large.append(
            fetch(
                (early_hbm.at[k], late_hbm.at[k]), (early.at[k], late.at[k]), field_sems.at[k]
            )
        )
    owners = recv.shape[0]
    rows = dest.shape[1]
    blocks = recv[...]
    line = blocks[:, 2:3]
    sums = jnp.sum(line, axis=0)

    def pick(values, n):
        return values[:, n : n + 1]

    norm = pick(sums, 0)
    step = norm / (norm + pick(sums, 1))
    off = blocks[:, 3:4] - step[None]
    linear = jnp.sum(off * line, axis=0)
    square = jnp.sum(off * off * line, axis=0)
    norm_next = jnp.maximum(pick(sums, 2) + pick(linear, 3) + pick(square, 4), 0.0)
    beta = norm_next / norm
    bend = pick(sums, 5) + pick(linear, 6) + pick(square, 7)
    bend = bend + beta * (pick(sums, 8) + pick(linear, 9)) + beta * beta * pick(sums, 1)
    length = norm_next + beta * (pick(sums, 10) + pick(linear, 11)) + beta * beta * norm
    curve = length + bend
    step_next = jnp.where(curve > 0.0, norm_next / jnp.where(curve > 0.0, curve, 1.0), 0.0)
    step_next = jnp.minimum(step_next, 1.0)
    near = step + step_next * ((1.0 - step) + beta)
    far = -step_next * step
    stores = []
    for k in range(count):
        wait_all(large[k])
        result[k] = near[None] * early[k] + far[None] * late[k]
        target = member_hbm.at[k] if k < count - 1 else static_hbm
        stores.append(pltpu.make_async_copy(result.at[k], target, field_sems.at[k, 2]))
        stores[k].start()
    wait_all(small)
    kind = iota((owners, 8, rows), 1)
    factor = jnp.where(kind == 0, near[None], jnp.where(kind == 1, far[None], 0.0))
    chosen = iota((owners, 8, rows), 0) == dest[...].reshape(1, 1, rows)
    picked = jnp.where(chosen, factor, 0.0).reshape(owners * 8, rows)
    table = dot(blocks.reshape(owners * 8, LANES), picked, ((0,), (0,)))
    equivalent[...] = jnp.sum(
        jnp.where(iota((LANES, rows), 0) == lane[...], table, 0.0), axis=0, keepdims=True
    )
    wait_all(stores)


def shape(*dims):
    return jax.ShapeDtypeStruct(dims, F32)


def stay(*values):
    return [pltpu.with_memory_space_constraint(value, pltpu.HBM) for value in values]


def swaps(count, ring):
    inner = [(i, i ^ 1) for i in range(count)]
    outer = []
    for i in range(1, count - 1, 2):
        outer += [(i, i + 1), (i + 1, i)]
    if ring:
        outer += [(count - 1, 0), (0, count - 1)]
    return inner, outer


def body(
    ensemble,
    vert_loc,
    static_vert,
    inst_vert,
    inst_err,
    obs_dest,
    obs_patch,
    obs_window,
    obs_inst,
    obs_hweight,
    innovation,
    obs_count,
):
    members, windows, rows_lat, rows_lon, levels = ensemble.shape
    lat_count = lax.axis_size("lat")
    lon_count = lax.axis_size("lon")
    owners = lat_count * lon_count
    rows = innovation.shape[0]
    slots = 2 * rows // owners
    total = owners * slots
    patches = rows_lat // 2 * (rows_lon // 2)
    count = members + 1
    width = rows_lon + 8
    lat_inner, lat_outer = swaps(lat_count, False)
    lon_inner, lon_outer = swaps(lon_count, True)
    tile = shape(count, rows_lat, rows_lon, levels)
    edge = shape(count, rows_lat, HALO, levels)

    def line(values):
        return values.reshape(1, rows)

    dest = line(obs_dest)
    row_scratch = pltpu.VMEM((1, rows), jnp.int32)
    send, lane = pl.pallas_call(
        functools.partial(pack_kernel, slots, patches),
        out_shape=(shape(owners, 8, LANES), pltpu.HBM((1, rows), jnp.int32)),
        in_specs=[HBM] * 6 + [SMEM],
        out_specs=(VMEM, HBM),
        scratch_shapes=[row_scratch] * 4
        + [
            pltpu.VMEM(obs_hweight.shape, F32),
            pltpu.VMEM((1, rows), F32),
            pltpu.VMEM((8, rows), F32),
            row_scratch,
            DMA((7,)),
        ],
        compiler_params=PARAMS,
        name="pack",
    )(
        *stay(
            dest,
            line(obs_patch),
            line(obs_window),
            line(obs_inst),
            obs_hweight,
            line(innovation),
        ),
        obs_count,
    )
    squares = pl.pallas_call(
        prepare_kernel,
        out_shape=shape(2, levels, levels),
        compiler_params=PARAMS,
        name="prepare",
    )(vert_loc, static_vert)

    def exchange(blocks):
        return lax.all_to_all(blocks, ("lat", "lon"), split_axis=0, concat_axis=0, tiled=True)

    recv = exchange(send)
    ens_scratch = pltpu.VMEM(ensemble.shape, ensemble.dtype)
    field_scratch = pltpu.VMEM((count, rows_lat + 2 * HALO, width, levels), F32)
    tile_scratch = pltpu.VMEM(tile.shape, F32)
    weight_scratch = pltpu.VMEM((windows * rows_lat * rows_lon, total), F32)
    grad_scratch = pltpu.VMEM((windows * rows_lat * rows_lon, levels), F32)

    def powers(order):
        return pltpu.VMEM((order, rows_lat, width, levels), F32)

    feat, ivert, *outs = pl.pallas_call(
        functools.partial(first_kernel, slots),
        out_shape=(shape(8, total), shape(levels, total), tile, edge, edge),
        in_specs=[VMEM, HBM, HBM, HBM],
        out_specs=(VMEM,) * 5,
        scratch_shapes=[
            pltpu.VMEM(inst_vert.shape, F32),
            pltpu.VMEM((1, inst_err.shape[0]), F32),
            ens_scratch,
            weight_scratch,
            grad_scratch,
            DMA((2 + members,)),
        ],
        compiler_params=PARAMS,
        name="first",
    )(recv, *stay(inst_vert, inst_err.reshape(1, -1), ensemble))

    def sides(part_a, part_b):
        return pl.pallas_call(
            sides_kernel,
            out_shape=(
                shape(count, rows_lat, 8, levels),
                shape(count, 2, 8, levels),
            ),
            in_specs=[VMEM] * 2,
            out_specs=(VMEM,) * 2,
            compiler_params=PARAMS,
            name="sides",
        )(part_a, part_b)

    def halo(fields, edge_a, edge_b):
        lat_b = lax.ppermute(fields, "lat", lat_outer)
        side_a = lax.ppermute(edge_a, "lon", lon_inner)
        side_b = lax.ppermute(edge_b, "lon", lon_outer)
        lat_a = lax.ppermute(fields, "lat", lat_inner)
        cross, folded = sides(side_a, side_b)
        corner_b = lax.ppermute(folded, "lat", lat_outer)
        corner_a = lax.ppermute(cross, "lat", lat_inner)
        return (fields, lat_a, lat_b, cross, corner_a, corner_b)

    def control(kept):
        return pl.pallas_call(
            control_kernel,
            out_shape=pltpu.HBM(tile.shape, F32),
            in_specs=[HBM] * 3,
            out_specs=HBM,
            scratch_shapes=[
                pltpu.VMEM(kept_shape.shape, F32),
                powers(2),
                tile_scratch,
                tile_scratch,
                matrix_scratch,
                matrix_scratch,
                DMA((3,)),
                DMA((count,)),
            ],
            compiler_params=PARAMS,
            name="control",
        )(*stay(kept, vert_loc, static_vert))

    parts = halo(*outs)
    matrix_scratch = pltpu.VMEM(vert_loc.shape, F32)
    work = [ens_scratch, field_scratch, powers(4), tile_scratch, tile_scratch, weight_scratch]
    sems = [DMA, DMA((8,))]
    kept_shape = pltpu.HBM((count, rows_lat + HALO, width, levels), F32)
    image, kept, *outs = pl.pallas_call(
        middle_kernel,
        out_shape=(shape(8, total), kept_shape, tile, edge, edge),
        in_specs=[ANY] * 6 + [HBM] + [VMEM] * 3,
        out_specs=(VMEM, HBM) + (VMEM,) * 3,
        scratch_shapes=work + [grad_scratch] + sems,
        compiler_params=PARAMS,
        name="middle",
    )(*parts, *stay(ensemble), feat, ivert, squares)
    early = control(kept)
    parts = halo(*outs)
    send, kept = pl.pallas_call(
        functools.partial(last_kernel, slots),
        out_shape=(shape(owners, 8, LANES), kept_shape),
        in_specs=[ANY] * 6 + [HBM] * 2 + [VMEM] * 4,
        out_specs=(VMEM, HBM),
        scratch_shapes=work + [pltpu.VMEM((16, total), F32)] + sems,
        compiler_params=PARAMS,
        name="last",
    )(*parts, *stay(ensemble, early), feat, ivert, squares, image)
    recv = exchange(send)
    late = control(kept)
    static, member, equivalent = pl.pallas_call(
        final_kernel,
        out_shape=(
            shape(rows_lat, rows_lon, levels),
            shape(members, rows_lat, rows_lon, levels),
            shape(1, rows),
        ),
        in_specs=[VMEM] + [HBM] * 4,
        out_specs=(HBM, HBM, VMEM),
        scratch_shapes=[
            row_scratch,
            row_scratch,
            tile_scratch,
            tile_scratch,
            tile_scratch,
            DMA((2,)),
            DMA((count, 3)),
        ],
        compiler_params=PARAMS,
        name="final",
    )(recv, *stay(dest, lane, early, late))
    return static, member, equivalent.reshape(rows)


def solution(mesh):
    return jax.shard_map(
        body,
        mesh=mesh,
        in_specs=(
            P(None, None, "lat", "lon", None),
            P(),
            P(),
            P(),
            P(),
            P(("lat", "lon"), None),
            P(("lat", "lon")),
            P(("lat", "lon")),
            P(("lat", "lon")),
            P(None, ("lat", "lon")),
            P(("lat", "lon")),
            P(("lat", "lon")),
        ),
        out_specs=(P("lat", "lon", None), P(None, "lat", "lon", None), P(("lat", "lon"))),
        check_vma=False,
    )
```

```python
import functools

import jax
import jax.numpy as jnp
from jax import lax
from jax.experimental import pallas as pl
from jax.experimental.pallas import tpu as pltpu
from jax.sharding import PartitionSpec as P


SMOOTH = 0.15
CENTER = 1.0 - 4.0 * SMOOTH
BETA_STATIC = 0.5
BETA_ENSEMBLE = 0.85
HALO = 4
FOLD = 3
LANES = 128
HIGHEST = lax.Precision.HIGHEST
F32 = jnp.float32
BF16 = jnp.bfloat16

ANY = pl.BlockSpec(memory_space=pl.ANY)
HBM = pl.BlockSpec(memory_space=pltpu.HBM)
VMEM = pl.BlockSpec(memory_space=pltpu.VMEM)
SMEM = pl.BlockSpec(memory_space=pltpu.SMEM)
PARAMS = pltpu.CompilerParams(vmem_limit_bytes=32 * 1024 * 1024)
DMA = pltpu.SemaphoreType.DMA


def dot(left, right, dims=((1,), (0,))):
    return lax.dot_general(
        left, right, (dims, ((), ())), precision=HIGHEST, preferred_element_type=F32
    )


def iota(shape, dim):
    return lax.broadcasted_iota(jnp.int32, shape, dim)


def halves(value):
    high = value.astype(BF16)
    return high, (value - high.astype(F32)).astype(BF16)


def fetch(sources, targets, sems):
    copies = [
        pltpu.make_async_copy(source, target, sems.at[n])
        for n, (source, target) in enumerate(zip(sources, targets))
    ]
    for copy in copies:
        copy.start()
    return copies


def wait_all(copies):
    for copy in copies:
        copy.wait()


def short_dot(left, right, dims=((1,), (0,))):
    return lax.dot_general(left, right, (dims, ((), ())), preferred_element_type=F32)


def pack_kernel(
    slots, patches,
    dest_hbm, patch_hbm, window_hbm, inst_hbm, hweight_hbm, innov_hbm, count,
    send, lane_hbm,
    dest, patch, window, inst, hweight, innov, feat, lane, sems,
):
    wait_all(
        fetch(
            (dest_hbm, patch_hbm, window_hbm, inst_hbm, hweight_hbm, innov_hbm),
            (dest, patch, window, inst, hweight, innov),
            sems,
        )
    )
    owners = send.shape[0]
    rows = dest.shape[1]
    me = lax.axis_index("lat") * lax.axis_size("lon") + lax.axis_index("lon")
    base = lax.rem(me, LANES // slots) * slots
    destination = dest[...]
    row, col = iota((rows, rows), 0), iota((rows, rows), 1)
    upright = jnp.sum(
        jnp.where(row == col, destination.astype(F32), 0.0), axis=1, keepdims=True
    ).astype(jnp.int32)
    earlier = (upright == destination) & (row < col)
    ranking = jnp.sum(jnp.where(earlier, 1.0, 0.0), axis=0, keepdims=True).astype(jnp.int32)
    position = ranking + base
    lane[...] = position
    lane_copy = pltpu.make_async_copy(lane, lane_hbm, sems.at[6])
    lane_copy.start()
    active = (iota((1, rows), 1) < count[0]).astype(F32)
    feat[...] = jnp.zeros_like(feat)
    feat[0:1] = (window[...] * patches + patch[...]).astype(F32)
    feat[1:2] = inst[...].astype(F32)
    feat[2:6] = hweight[...] * active
    feat[6:7] = innov[...]
    chosen = iota((owners, 8, rows), 0) == destination.reshape(1, 1, rows)
    spread_out = jnp.where(chosen, feat[...][None], 0.0).reshape(owners * 8, rows)
    at_lane = (iota((LANES, rows), 0) == position).astype(F32)
    send[...] = dot(spread_out, at_lane, ((1,), (1,))).reshape(owners, 8, LANES)
    lane_copy.wait()


def prepare_kernel(vert_loc, static_vert, squares):
    levels = vert_loc.shape[0]
    squares[...] = jnp.zeros_like(squares)
    for n, (scale, matrix) in enumerate(((BETA_ENSEMBLE, vert_loc), (BETA_STATIC, static_vert))):
        high, low = halves(scale**2 * dot(matrix[...], matrix[...], ((0,), (0,))))
        squares[n, :levels, :levels] = high
        squares[n, :levels, levels:] = low
        squares[n, levels:, :levels] = high


def fill_weights(feat, weights, high_weights, low_weights, windows, rows_lat, rows_lon):
    slots = feat.shape[1]
    cell = feat[0:1].astype(jnp.int32)
    half = iota((rows_lon, slots), 0) >> 1
    odd = (iota((rows_lon, slots), 0) & 1) == 1
    corner = [
        jnp.where(odd, feat[3 + 2 * q : 4 + 2 * q], feat[2 + 2 * q : 3 + 2 * q]) for q in range(2)
    ]
    per_window = rows_lat // 2 * (rows_lon // 2)
    for t in range(windows):
        for a in range(rows_lat):
            first = t * per_window + a // 2 * (rows_lon // 2)
            row = (t * rows_lat + a) * rows_lon
            rows = slice(row, row + rows_lon)
            value = jnp.where(half == cell - first, corner[a % 2], 0.0)
            weights[rows] = value
            high_weights[rows], low_weights[rows] = halves(value)


def adjoint_fields(amount, high_weights, low_weights, ivert, ens, ens_copies, grad, outs):
    fields, edge_a, edge_b = outs
    members, windows, rows_lat, rows_lon, levels = ens.shape
    block = rows_lat * rows_lon
    high, low = halves(ivert[...] * amount)
    both = jnp.concatenate([high, low], axis=0)
    for t in range(windows):
        rows = slice(t * block, (t + 1) * block)
        pair = short_dot(high_weights[rows], both, ((1,), (1,)))
        rest = short_dot(low_weights[rows], high, ((1,), (1,)))
        grad[rows] = pair[:, :levels] + pair[:, levels:] + rest
    even = lax.rem(lax.axis_index("lon"), 2) == 0

    def part(t, a):
        first = (t * rows_lat + a) * rows_lon
        return grad[first : first + rows_lon]

    for k in range(members + 1):
        if k < members and ens_copies:
            ens_copies[k].wait()
        for a in range(rows_lat):
            total = part(0, a) if k == members else ens[k, 0, a].astype(F32) * part(0, a)
            for t in range(1, windows):
                term = part(t, a) if k == members else ens[k, t, a].astype(F32) * part(t, a)
                total = total + term
            fields[k, a] = total
            east = total[rows_lon - HALO :]
            west = total[:HALO]
            edge_a[k, a] = jnp.where(even, east, west)
            edge_b[k, a] = jnp.where(even, west, east)


def first_kernel(
    slots,
    recv, inst_vert_hbm, inst_err_hbm, ens_hbm,
    feat, ivert, fields, edge_a, edge_b,
    inst_vert, inst_err, ens, weights, high_weights, low_weights, grad, sems,
):
    members = ens.shape[0]
    copies = fetch(
        [inst_vert_hbm, inst_err_hbm] + [ens_hbm.at[k] for k in range(members)],
        [inst_vert, inst_err] + [ens.at[k] for k in range(members)],
        sems,
    )
    members, windows, rows_lat, rows_lon, _ = ens.shape
    owners = recv.shape[0]
    per = LANES // slots
    for g in range(owners // per):
        feat[:, g * LANES : (g + 1) * LANES] = jnp.sum(recv[g * per : (g + 1) * per], axis=0)
    wait_all(copies[:2])
    instruments = inst_vert.shape[0]
    total = feat.shape[1]
    onehot = (iota((instruments, total), 0) == feat[1:2].astype(jnp.int32)).astype(F32)
    ivert[...] = dot(inst_vert[...].T, onehot)
    inverse = jnp.broadcast_to(1.0 / (inst_err[...] * inst_err[...]), (8, instruments))
    rinv = dot(inverse, onehot)[0:1]
    feat[6:7] = feat[6:7] * rinv
    feat[7:8] = rinv
    fill_weights(feat, weights, high_weights, low_weights, windows, rows_lat, rows_lon)
    outs = (fields, edge_a, edge_b)
    adjoint_fields(feat[6:7], high_weights, low_weights, ivert, ens, copies[2:], grad, outs)


def halo_copies(own, lat_a, lat_b, cross, corner_a, corner_b, field, sems):
    rows_lat, rows_lon = own.shape[1:3]
    odd = lax.rem(lax.axis_index("lat"), 2)
    south = HALO + rows_lat
    row_a = south * (1 - odd)
    row_b = south * odd
    far_a = (rows_lat - HALO) * odd
    far_b = (rows_lat - HALO) * (1 - odd)
    main = pl.ds(0, rows_lon)
    side = pl.ds(rows_lon, 8)
    mid = pl.ds(HALO, rows_lat)
    plan = (
        (own, field.at[:, mid, main]),
        (cross, field.at[:, mid, side]),
        (lat_a.at[:, pl.ds(far_a, HALO)], field.at[:, pl.ds(row_a, HALO), main]),
        (lat_b.at[:, pl.ds(far_b, HALO)], field.at[:, pl.ds(row_b, HALO), main]),
        (corner_a.at[:, pl.ds(far_a, HALO)], field.at[:, pl.ds(row_a, HALO), side]),
        (corner_b.at[:, 0], field.at[:, row_b + (HALO - 1) * (1 - odd), side]),
        (corner_b.at[:, 1], field.at[:, row_b + (HALO - 2) * (1 - odd) + odd, side]),
    )
    unused = row_b + (HALO - 1) * odd
    field[:, pl.ds(unused, 1), rows_lon:] = jnp.zeros_like(field[:, pl.ds(unused, 1), rows_lon:])
    return [pltpu.make_async_copy(s, d, sems.at[n]) for n, (s, d) in enumerate(plan)]


def unfold_corner(field, rows_lon):
    odd = lax.rem(lax.axis_index("lat"), 2)
    row_b = (field.shape[1] - HALO) * odd
    second = row_b + (HALO - 2) * (1 - odd) + odd
    third = row_b + (HALO - 3) * (1 - odd) + 2 * odd
    for k in range(field.shape[0]):
        field[k, third, rows_lon:] = pltpu.roll(field[k, second, rows_lon:], 8 - FOLD, 0)


def sides_kernel(part_a, part_b, cross, folded):
    count, rows_lat, _, levels = part_a.shape
    even = lax.rem(lax.axis_index("lon"), 2) == 0
    odd = lax.rem(lax.axis_index("lat"), 2) == 1
    index = iota((8, levels), 0)
    inner = (index == FOLD - 1) | (index == FOLD)
    for k in range(count):
        rows = []
        for a in range(rows_lat):
            first = jnp.where(even, part_a[k, a], part_b[k, a])
            second = jnp.where(even, part_b[k, a], part_a[k, a])
            rows.append(jnp.concatenate([first, second], axis=0))
            cross[k, a] = rows[a]
        near = [jnp.where(odd, rows[rows_lat - 1 - r], rows[r]) for r in range(HALO - 1)]
        folded[k, 0] = near[0]
        folded[k, 1] = jnp.where(inner, pltpu.roll(near[2], FOLD, 0), near[1])


def keep_copy(field, kept, sems):
    inner = pl.ds(HALO // 2, field.shape[1] - HALO)
    return pltpu.make_async_copy(field.at[:, inner], kept, sems.at[7])


def smooth_power(field, powers, out, order):
    count, rows, width, _ = field.shape
    rows_lat = rows - 2 * order
    rows_lon = width - 8
    lat = lax.axis_index("lat")
    north = (lat > 0).astype(F32)
    south = (lat < lax.axis_size("lat") - 1).astype(F32)
    factor = {2: (2.0, 1.0), 4: (4.0, 6.0, 4.0, 1.0)}[order]

    def one(k, carry):
        for c in range(width // 8):
            cols = slice(8 * c, 8 * c + 8)
            line = {i: field[k, i, cols] for i in range(rows)}
            for m in range(1, order + 1):
                fresh = {}
                for i in range(m, rows - m):
                    value = line[i - 1] + line[i + 1]
                    if i < order:
                        value = value * north
                    if i >= order + rows_lat:
                        value = value * south
                    fresh[i] = value
                line = fresh
                for i in range(rows_lat):
                    powers[m - 1, i, cols] = line[order + i]
        for i in range(rows_lat):
            value = field[k, order + i]
            for m in range(1, order + 1):
                ring = pltpu.roll(value, 1, 0) + pltpu.roll(value, width - 1, 0)
                value = CENTER * value + SMOOTH * ring
                value = value + (factor[m - 1] * SMOOTH**m) * powers[m - 1, i]
            out[k, i] = value[:rows_lon]
        return carry

    lax.fori_loop(0, count, one, 0, unroll=count)


def observe(field, powers, smooth, mixed, squares, ivert, weights, ens, ens_copy):
    members, windows, rows_lat, rows_lon, levels = ens.shape
    block = rows_lat * rows_lon
    smooth_power(field, powers, smooth, 4)
    shape = (rows_lat, rows_lon, levels)
    for k in range(members + 1):
        square = squares[0] if k < members else squares[1]
        pair = jnp.concatenate(halves(smooth[k].reshape(block, levels)), axis=1)
        product = short_dot(pair, square)
        mixed[k] = (product[:, :levels] + product[:, levels:]).reshape(shape)
    ens_copy.wait()
    slots = weights.shape[1]
    image = jnp.zeros((8, slots), F32)
    high, low = halves(ivert[...])
    rows_of = jnp.concatenate([high, high, low], axis=0)
    for t in range(windows):
        lines = []
        for a in range(rows_lat):
            total = mixed[members, a]
            for k in range(members):
                total = total + ens[k, t, a].astype(F32) * mixed[k, a]
            lines.append(total)
        increment = jnp.stack(lines).reshape(block, levels)
        high, low = halves(increment)
        seen = short_dot(jnp.concatenate([high, low, high], axis=1), rows_of)
        seen = seen * weights[t * block : (t + 1) * block]
        image = image + jnp.sum(seen.reshape(block // 8, 8, slots), axis=0)
    return jnp.sum(image, axis=0, keepdims=True)


def middle_kernel(
    own, lat_a, lat_b, cross, corner_a, corner_b, ens_hbm, feat, ivert, squares,
    image, kept, fields, edge_a, edge_b,
    ens, field, powers, smooth, mixed, weights, high_weights, low_weights, grad, sem, sems,
):
    copies = halo_copies(own, lat_a, lat_b, cross, corner_a, corner_b, field, sems)
    for copy in copies:
        copy.start()
    ens_copy = pltpu.make_async_copy(ens_hbm, ens, sem)
    ens_copy.start()
    _, windows, rows_lat, rows_lon, _ = ens.shape
    fill_weights(feat, weights, high_weights, low_weights, windows, rows_lat, rows_lon)
    wait_all(copies)
    unfold_corner(field, rows_lon)
    keep = keep_copy(field, kept, sems)
    keep.start()
    seen = observe(field, powers, smooth, mixed, squares, ivert, weights, ens, ens_copy)
    scaled = seen * feat[7:8]
    image[...] = jnp.zeros_like(image)
    image[0:1] = seen
    image[1:2] = scaled
    outs = (fields, edge_a, edge_b)
    adjoint_fields(scaled, high_weights, low_weights, ivert, ens, (), grad, outs)
    keep.wait()


def last_kernel(
    slots,
    own, lat_a, lat_b, cross, corner_a, corner_b, ens_hbm, feat, ivert, squares, image,
    send, kept,
    ens, field, powers, smooth, mixed, weights, high_weights, low_weights, terms, sem, sems,
):
    copies = halo_copies(own, lat_a, lat_b, cross, corner_a, corner_b, field, sems)
    for copy in copies:
        copy.start()
    ens_copy = pltpu.make_async_copy(ens_hbm, ens, sem)
    ens_copy.start()
    _, windows, rows_lat, rows_lon, _ = ens.shape
    fill_weights(feat, weights, high_weights, low_weights, windows, rows_lat, rows_lon)
    wait_all(copies)
    unfold_corner(field, rows_lon)
    keep = keep_copy(field, kept, sems)
    keep.start()
    second = observe(field, powers, smooth, mixed, squares, ivert, weights, ens, ens_copy)
    start = feat[6:7]
    rinv = feat[7:8]
    first = image[0:1]
    scaled = image[1:2]
    norm = jnp.sum(start * first, axis=1, keepdims=True)
    curve = norm + jnp.sum(first * scaled, axis=1, keepdims=True)
    guess = jnp.where(curve > 0.0, norm / jnp.where(curve > 0.0, curve, 1.0), 1.0)
    guess = jnp.clip(guess, 0.0, 1.0)
    ahead = start + scaled
    ahead_image = first + second
    rest = start - guess * ahead
    rest_image = first - guess * ahead_image
    products = (
        start * first,
        first * scaled,
        rest * rest_image,
        rest * ahead_image + ahead * rest_image,
        ahead * ahead_image,
        rest_image * rinv * rest_image,
        2.0 * rest_image * rinv * ahead_image,
        ahead_image * rinv * ahead_image,
        2.0 * rest_image * scaled,
        2.0 * ahead_image * scaled,
        start * rest_image + rest * first,
        start * ahead_image + ahead * first,
    )
    terms[...] = jnp.zeros_like(terms)
    for n, value in enumerate(products):
        terms[n : n + 1] = value
    sums = jnp.sum(terms[...], axis=1, keepdims=True)
    square = (16, LANES)
    line = jnp.sum(
        jnp.where(iota(square, 0) == iota(square, 1), sums, 0.0), axis=0, keepdims=True
    )
    owners = send.shape[0]
    per = LANES // slots
    row = iota((8, LANES), 0)
    for g in range(owners // per):
        lanes = slice(g * LANES, (g + 1) * LANES)
        block = jnp.where(row == 0, first[:, lanes], 0.0)
        block = jnp.where(row == 1, second[:, lanes], block)
        block = jnp.where(row == 2, line, block)
        block = jnp.where(row == 3, guess, block)
        send[g * per : (g + 1) * per] = jnp.broadcast_to(block[None], (per, 8, LANES))
    keep.wait()


def control_kernel(
    kept_early, kept_late, vert_hbm, static_hbm,
    early, late,
    fields, powers, smooth, vert_loc, static_vert, sems,
):
    copies = fetch(
        (vert_hbm, static_hbm, kept_early, kept_late),
        (vert_loc, static_vert, fields.at[0], fields.at[1]),
        sems,
    )
    wait_all(copies[:2])
    count, rows_lat, rows_lon, levels = smooth.shape
    blocks = []
    for scale, matrix in ((BETA_ENSEMBLE, vert_loc), (BETA_STATIC, static_vert)):
        high, low = halves(scale * matrix[...])
        upper = jnp.concatenate([high, high], axis=1)
        lower = jnp.concatenate([low, jnp.zeros_like(low)], axis=1)
        blocks.append(jnp.concatenate([upper, lower], axis=0))
    for n, control in enumerate((early, late)):
        copies[2 + n].wait()
        smooth_power(fields.at[n], powers, smooth, 2)
        for k in range(count):
            pair = jnp.concatenate(halves(smooth[k].reshape(rows_lat * rows_lon, levels)), axis=1)
            product = short_dot(pair, blocks[k // (count - 1)], ((1,), (1,)))
            product = product[:, :levels] + product[:, levels:]
            control[k] = product.reshape(rows_lat, rows_lon, levels)


def final_kernel(
    recv, early, late, dest_hbm, lane_hbm,
    static_hbm, member_hbm, equivalent_hbm,
    dest, lane, equivalent, result, sems, out_sems,
):
    small = fetch((dest_hbm, lane_hbm), (dest, lane), sems)
    count = early.shape[0]
    owners = recv.shape[0]
    rows = dest.shape[1]
    blocks = recv[...]
    line = blocks[:, 2:3]
    sums = jnp.sum(line, axis=0)

    def pick(values, n):
        return values[:, n : n + 1]

    norm = pick(sums, 0)
    step = norm / (norm + pick(sums, 1))
    off = blocks[:, 3:4] - step[None]
    linear = jnp.sum(off * line, axis=0)
    square = jnp.sum(off * off * line, axis=0)
    norm_next = jnp.maximum(pick(sums, 2) + pick(linear, 3) + pick(square, 4), 0.0)
    beta = norm_next / norm
    bend = pick(sums, 5) + pick(linear, 6) + pick(square, 7)
    bend = bend + beta * (pick(sums, 8) + pick(linear, 9)) + beta * beta * pick(sums, 1)
    length = norm_next + beta * (pick(sums, 10) + pick(linear, 11)) + beta * beta * norm
    curve = length + bend
    step_next = jnp.where(curve > 0.0, norm_next / jnp.where(curve > 0.0, curve, 1.0), 0.0)
    step_next = jnp.minimum(step_next, 1.0)
    near = step + step_next * ((1.0 - step) + beta)
    far = -step_next * step
    stores = []
    for k in range(count):
        result[k] = near[None] * early[k] + far[None] * late[k]
        target = member_hbm.at[k] if k < count - 1 else static_hbm
        stores.append(pltpu.make_async_copy(result.at[k], target, out_sems.at[k]))
        stores[k].start()
    wait_all(small)
    kind = iota((owners, 8, rows), 1)
    factor = jnp.where(kind == 0, near[None], jnp.where(kind == 1, far[None], 0.0))
    chosen = iota((owners, 8, rows), 0) == dest[...].reshape(1, 1, rows)
    picked = jnp.where(chosen, factor, 0.0).reshape(owners * 8, rows)
    table = dot(blocks.reshape(owners * 8, LANES), picked, ((0,), (0,)))
    equivalent[...] = jnp.sum(
        jnp.where(iota((LANES, rows), 0) == lane[...], table, 0.0), axis=0, keepdims=True
    )
    stores.append(pltpu.make_async_copy(equivalent, equivalent_hbm, out_sems.at[count]))
    stores[count].start()
    wait_all(stores)


def shape(*dims):
    return jax.ShapeDtypeStruct(dims, F32)


def stay(*values):
    return [pltpu.with_memory_space_constraint(value, pltpu.HBM) for value in values]


def swaps(count, ring):
    inner = [(i, i ^ 1) for i in range(count)]
    outer = []
    for i in range(1, count - 1, 2):
        outer += [(i, i + 1), (i + 1, i)]
    if ring:
        outer += [(count - 1, 0), (0, count - 1)]
    return inner, outer


def body(
    ensemble,
    vert_loc,
    static_vert,
    inst_vert,
    inst_err,
    obs_dest,
    obs_patch,
    obs_window,
    obs_inst,
    obs_hweight,
    innovation,
    obs_count,
):
    members, windows, rows_lat, rows_lon, levels = ensemble.shape
    lat_count = lax.axis_size("lat")
    lon_count = lax.axis_size("lon")
    owners = lat_count * lon_count
    rows = innovation.shape[0]
    slots = 2 * rows // owners
    total = owners * slots
    patches = rows_lat // 2 * (rows_lon // 2)
    count = members + 1
    width = rows_lon + 8
    lat_inner, lat_outer = swaps(lat_count, False)
    lon_inner, lon_outer = swaps(lon_count, True)
    tile = shape(count, rows_lat, rows_lon, levels)
    edge = shape(count, rows_lat, HALO, levels)

    def line(values):
        return values.reshape(1, rows)

    dest = line(obs_dest)
    row_scratch = pltpu.VMEM((1, rows), jnp.int32)
    send, lane = pl.pallas_call(
        functools.partial(pack_kernel, slots, patches),
        out_shape=(shape(owners, 8, LANES), pltpu.HBM((1, rows), jnp.int32)),
        in_specs=[HBM] * 6 + [SMEM],
        out_specs=(VMEM, HBM),
        scratch_shapes=[row_scratch] * 4
        + [
            pltpu.VMEM(obs_hweight.shape, F32),
            pltpu.VMEM((1, rows), F32),
            pltpu.VMEM((8, rows), F32),
            row_scratch,
            DMA((7,)),
        ],
        compiler_params=PARAMS,
        name="pack",
    )(
        *stay(
            dest,
            line(obs_patch),
            line(obs_window),
            line(obs_inst),
            obs_hweight,
            line(innovation),
        ),
        obs_count,
    )
    squares = pl.pallas_call(
        prepare_kernel,
        out_shape=jax.ShapeDtypeStruct((2, 2 * levels, 2 * levels), BF16),
        compiler_params=PARAMS,
        name="prepare",
    )(vert_loc, static_vert)

    def exchange(blocks):
        return lax.all_to_all(blocks, ("lat", "lon"), split_axis=0, concat_axis=0, tiled=True)

    recv = exchange(send)
    ens_scratch = pltpu.VMEM(ensemble.shape, ensemble.dtype)
    field_scratch = pltpu.VMEM((count, rows_lat + 2 * HALO, width, levels), F32)
    tile_scratch = pltpu.VMEM(tile.shape, F32)
    weight_scratch = pltpu.VMEM((windows * rows_lat * rows_lon, total), F32)
    half_scratch = pltpu.VMEM(weight_scratch.shape, BF16)
    grad_scratch = pltpu.VMEM((windows * rows_lat * rows_lon, levels), F32)

    def powers(order):
        return pltpu.VMEM((order, rows_lat, width, levels), F32)

    feat, ivert, *outs = pl.pallas_call(
        functools.partial(first_kernel, slots),
        out_shape=(shape(8, total), shape(levels, total), tile, edge, edge),
        in_specs=[VMEM, HBM, HBM, HBM],
        out_specs=(VMEM,) * 5,
        scratch_shapes=[
            pltpu.VMEM(inst_vert.shape, F32),
            pltpu.VMEM((1, inst_err.shape[0]), F32),
            ens_scratch,
            weight_scratch,
            half_scratch,
            half_scratch,
            grad_scratch,
            DMA((2 + members,)),
        ],
        compiler_params=PARAMS,
        name="first",
    )(recv, *stay(inst_vert, inst_err.reshape(1, -1), ensemble))

    def sides(part_a, part_b):
        return pl.pallas_call(
            sides_kernel,
            out_shape=(
                shape(count, rows_lat, 8, levels),
                shape(count, 2, 8, levels),
            ),
            in_specs=[VMEM] * 2,
            out_specs=(VMEM,) * 2,
            compiler_params=PARAMS,
            name="sides",
        )(part_a, part_b)

    def halo(fields, edge_a, edge_b):
        lat_b = lax.ppermute(fields, "lat", lat_outer)
        side_a = lax.ppermute(edge_a, "lon", lon_inner)
        side_b = lax.ppermute(edge_b, "lon", lon_outer)
        lat_a = lax.ppermute(fields, "lat", lat_inner)
        cross, folded = sides(side_a, side_b)
        corner_b = lax.ppermute(folded, "lat", lat_outer)
        corner_a = lax.ppermute(cross, "lat", lat_inner)
        return (fields, lat_a, lat_b, cross, corner_a, corner_b)

    parts = halo(*outs)
    matrix_scratch = pltpu.VMEM(vert_loc.shape, F32)
    work = [ens_scratch, field_scratch, powers(4), tile_scratch, tile_scratch, weight_scratch]
    work += [half_scratch] * 2
    sems = [DMA, DMA((8,))]
    kept_shape = pltpu.HBM((count, rows_lat + HALO, width, levels), F32)
    image, kept_early, *outs = pl.pallas_call(
        middle_kernel,
        out_shape=(shape(8, total), kept_shape, tile, edge, edge),
        in_specs=[ANY] * 6 + [HBM] + [VMEM] * 3,
        out_specs=(VMEM, HBM) + (VMEM,) * 3,
        scratch_shapes=work + [grad_scratch] + sems,
        compiler_params=PARAMS,
        name="middle",
    )(*parts, *stay(ensemble), feat, ivert, squares)
    parts = halo(*outs)
    send, kept_late = pl.pallas_call(
        functools.partial(last_kernel, slots),
        out_shape=(shape(owners, 8, LANES), kept_shape),
        in_specs=[ANY] * 6 + [HBM] + [VMEM] * 4,
        out_specs=(VMEM, HBM),
        scratch_shapes=work + [pltpu.VMEM((16, total), F32)] + sems,
        compiler_params=PARAMS,
        name="last",
    )(*parts, *stay(ensemble), feat, ivert, squares, image)
    recv = exchange(send)
    early, late = pl.pallas_call(
        control_kernel,
        out_shape=(tile, tile),
        in_specs=[HBM] * 4,
        out_specs=(VMEM,) * 2,
        scratch_shapes=[
            pltpu.VMEM((2,) + kept_shape.shape, F32),
            powers(2),
            tile_scratch,
            matrix_scratch,
            matrix_scratch,
            DMA((4,)),
        ],
        compiler_params=PARAMS,
        name="control",
    )(*stay(kept_early, kept_late, vert_loc, static_vert))
    static, member, equivalent = pl.pallas_call(
        final_kernel,
        out_shape=(
            shape(rows_lat, rows_lon, levels),
            shape(members, rows_lat, rows_lon, levels),
            shape(1, rows),
        ),
        in_specs=[VMEM] * 3 + [HBM] * 2,
        out_specs=(HBM,) * 3,
        scratch_shapes=[
            row_scratch,
            row_scratch,
            pltpu.VMEM((1, rows), F32),
            tile_scratch,
            DMA((2,)),
            DMA((count + 1,)),
        ],
        compiler_params=PARAMS,
        name="final",
    )(recv, early, late, *stay(dest, lane))
    return static, member, equivalent.reshape(rows)


def solution(mesh):
    return jax.shard_map(
        body,
        mesh=mesh,
        in_specs=(
            P(None, None, "lat", "lon", None),
            P(),
            P(),
            P(),
            P(),
            P(("lat", "lon"), None),
            P(("lat", "lon")),
            P(("lat", "lon")),
            P(("lat", "lon")),
            P(None, ("lat", "lon")),
            P(("lat", "lon")),
            P(("lat", "lon")),
        ),
        out_specs=(P("lat", "lon", None), P(None, "lat", "lon", None), P(("lat", "lon"))),
        check_vma=False,
    )
```

```python
import functools

import jax
import jax.numpy as jnp
from jax import lax
from jax.experimental import pallas as pl
from jax.experimental.pallas import tpu as pltpu
from jax.sharding import PartitionSpec as P


SMOOTH = 0.15
CENTER = 1.0 - 4.0 * SMOOTH
BETA_STATIC = 0.5
BETA_ENSEMBLE = 0.85
HALO = 4
FOLD = 3
GUESS = 12
LANES = 128
HIGHEST = lax.Precision.HIGHEST
F32 = jnp.float32
BF16 = jnp.bfloat16

ANY = pl.BlockSpec(memory_space=pl.ANY)
HBM = pl.BlockSpec(memory_space=pltpu.HBM)
VMEM = pl.BlockSpec(memory_space=pltpu.VMEM)
SMEM = pl.BlockSpec(memory_space=pltpu.SMEM)
PARAMS = pltpu.CompilerParams(vmem_limit_bytes=32 * 1024 * 1024)
DMA = pltpu.SemaphoreType.DMA


def dot(left, right, dims=((1,), (0,))):
    return lax.dot_general(
        left, right, (dims, ((), ())), precision=HIGHEST, preferred_element_type=F32
    )


def iota(shape, dim):
    return lax.broadcasted_iota(jnp.int32, shape, dim)


def halves(value):
    high = value.astype(BF16)
    return high, (value - high.astype(F32)).astype(BF16)


def thirds(value):
    high = value.astype(BF16)
    rest = value - high.astype(F32)
    middle = rest.astype(BF16)
    return high, middle, (rest - middle.astype(F32)).astype(BF16)


def within(value, length):
    return (value >= 0) & (value < length)


def fetch(sources, targets, sems):
    copies = [
        pltpu.make_async_copy(source, target, sems.at[n])
        for n, (source, target) in enumerate(zip(sources, targets))
    ]
    for copy in copies:
        copy.start()
    return copies


def wait_all(copies):
    for copy in copies:
        copy.wait()


def short_dot(left, right, dims=((1,), (0,))):
    return lax.dot_general(left, right, (dims, ((), ())), preferred_element_type=F32)


def pack_kernel(
    slots, patches,
    dest_hbm, patch_hbm, window_hbm, inst_hbm, hweight_hbm, innov_hbm, count,
    send, lane_hbm,
    dest, patch, window, inst, hweight, innov, feat, lane, table, sems,
):
    wait_all(
        fetch(
            (dest_hbm, patch_hbm, window_hbm, inst_hbm, hweight_hbm, innov_hbm),
            (dest, patch, window, inst, hweight, innov),
            sems,
        )
    )
    owners = send.shape[0]
    rows = dest.shape[1]
    destination = dest[...]
    row, col = iota((rows, rows), 0), iota((rows, rows), 1)
    upright = jnp.sum(
        jnp.where(row == col, destination.astype(F32), 0.0), axis=1, keepdims=True
    ).astype(jnp.int32)
    earlier = (upright == destination) & (row < col)
    ranking = jnp.sum(jnp.where(earlier, 1.0, 0.0), axis=0, keepdims=True).astype(jnp.int32)
    lane[...] = ranking
    lane_copy = pltpu.make_async_copy(lane, lane_hbm, sems.at[6])
    lane_copy.start()
    active = (iota((1, rows), 1) < count[0]).astype(F32)
    feat[0:1] = (window[...] * patches + patch[...]).astype(F32)
    feat[1:2] = inst[...].astype(F32)
    feat[2:6] = hweight[...] * active
    feat[6:7] = innov[...]
    table[...] = jnp.zeros_like(table)
    here = iota((slots, rows), 0) == ranking
    for f in range(7):
        table[f * slots : (f + 1) * slots] = jnp.where(here, feat[f : f + 1], 0.0)
    chosen = (iota((owners, rows), 0) == destination).astype(F32).astype(BF16)
    send[...] = short_dot(
        jnp.concatenate([chosen] * 3, axis=1),
        jnp.concatenate(thirds(table[...]), axis=1),
        ((1,), (1,)),
    )
    lane_copy.wait()


def prepare_kernel(vert_loc, static_vert, squares):
    levels = vert_loc.shape[0]
    squares[...] = jnp.zeros_like(squares)
    for n, (scale, matrix) in enumerate(((BETA_ENSEMBLE, vert_loc), (BETA_STATIC, static_vert))):
        high, low = halves(scale**2 * dot(matrix[...], matrix[...], ((0,), (0,))))
        squares[n, :levels, :levels] = high
        squares[n, :levels, levels:] = low
        squares[n, levels:, :levels] = high


def fill_weights(feat, weights, high_weights, low_weights, windows, rows_lat, rows_lon):
    slots = feat.shape[1]
    cell = feat[0:1].astype(jnp.int32)
    half = iota((rows_lon, slots), 0) >> 1
    odd = (iota((rows_lon, slots), 0) & 1) == 1
    corner = [
        jnp.where(odd, feat[3 + 2 * q : 4 + 2 * q], feat[2 + 2 * q : 3 + 2 * q]) for q in range(2)
    ]
    per_window = rows_lat // 2 * (rows_lon // 2)
    for t in range(windows):
        for a in range(rows_lat):
            first = t * per_window + a // 2 * (rows_lon // 2)
            row = (t * rows_lat + a) * rows_lon
            rows = slice(row, row + rows_lon)
            value = jnp.where(half == cell - first, corner[a % 2], 0.0)
            weights[rows] = value
            high_weights[rows], low_weights[rows] = halves(value)


def adjoint_fields(amount, high_weights, low_weights, ivert, ens, ens_copies, grad, outs):
    fields, edge_a, edge_b = outs
    members, windows, rows_lat, rows_lon, levels = ens.shape
    block = rows_lat * rows_lon
    high, low = halves(ivert[...] * amount)
    both = jnp.concatenate([high, low], axis=0)
    for t in range(windows):
        rows = slice(t * block, (t + 1) * block)
        pair = short_dot(high_weights[rows], both, ((1,), (1,)))
        rest = short_dot(low_weights[rows], high, ((1,), (1,)))
        grad[rows] = pair[:, :levels] + pair[:, levels:] + rest
    even = lax.rem(lax.axis_index("lon"), 2) == 0

    def part(t, a):
        first = (t * rows_lat + a) * rows_lon
        return grad[first : first + rows_lon]

    for k in range(members + 1):
        if k < members and ens_copies:
            ens_copies[k].wait()
        for a in range(rows_lat):
            total = part(0, a) if k == members else ens[k, 0, a].astype(F32) * part(0, a)
            for t in range(1, windows):
                term = part(t, a) if k == members else ens[k, t, a].astype(F32) * part(t, a)
                total = total + term
            fields[k, a] = total
            east = total[rows_lon - HALO :]
            west = total[:HALO]
            edge_a[k, a] = jnp.where(even, east, west)
            edge_b[k, a] = jnp.where(even, west, east)


def first_kernel(
    slots,
    recv, inst_vert_hbm, inst_err_hbm, ens_hbm,
    feat, ivert, fields, edge_a, edge_b,
    inst_vert, inst_err, ens, weights, high_weights, low_weights, grad, sems,
):
    members = ens.shape[0]
    copies = fetch(
        [inst_vert_hbm, inst_err_hbm] + [ens_hbm.at[k] for k in range(members)],
        [inst_vert, inst_err] + [ens.at[k] for k in range(members)],
        sems,
    )
    members, windows, rows_lat, rows_lon, _ = ens.shape
    owners = recv.shape[0]
    total = feat.shape[1]
    source = iota((owners, total), 1) - iota((owners, total), 0) * slots
    mine = within(source, slots).astype(F32).astype(BF16)
    lines = short_dot(
        jnp.concatenate(thirds(recv[...]), axis=0),
        jnp.concatenate([mine] * 3, axis=0),
        ((0,), (0,)),
    )
    same = (iota((LANES, total), 0) & (slots - 1)) == (iota((LANES, total), 1) & (slots - 1))
    lines = jnp.where(same, lines, 0.0)
    for f in range(8):
        feat[f : f + 1] = jnp.sum(lines[f * slots : (f + 1) * slots], axis=0, keepdims=True)
    wait_all(copies[:2])
    instruments = inst_vert.shape[0]
    onehot = (iota((instruments, total), 0) == feat[1:2].astype(jnp.int32)).astype(F32)
    ivert[...] = dot(inst_vert[...].T, onehot)
    inverse = jnp.broadcast_to(1.0 / (inst_err[...] * inst_err[...]), (8, instruments))
    rinv = dot(inverse, onehot)[0:1]
    feat[6:7] = feat[6:7] * rinv
    feat[7:8] = rinv
    fill_weights(feat, weights, high_weights, low_weights, windows, rows_lat, rows_lon)
    outs = (fields, edge_a, edge_b)
    adjoint_fields(feat[6:7], high_weights, low_weights, ivert, ens, copies[2:], grad, outs)


def halo_copies(own, lat_a, lat_b, cross, corner_a, corner_b, field, sems):
    rows_lat, rows_lon = own.shape[1:3]
    odd = lax.rem(lax.axis_index("lat"), 2)
    south = HALO + rows_lat
    row_a = south * (1 - odd)
    row_b = south * odd
    far_a = (rows_lat - HALO) * odd
    far_b = (rows_lat - HALO) * (1 - odd)
    main = pl.ds(0, rows_lon)
    side = pl.ds(rows_lon, 8)
    mid = pl.ds(HALO, rows_lat)
    plan = (
        (own, field.at[:, mid, main]),
        (cross, field.at[:, mid, side]),
        (lat_a.at[:, pl.ds(far_a, HALO)], field.at[:, pl.ds(row_a, HALO), main]),
        (lat_b.at[:, pl.ds(far_b, HALO)], field.at[:, pl.ds(row_b, HALO), main]),
        (corner_a.at[:, pl.ds(far_a, HALO)], field.at[:, pl.ds(row_a, HALO), side]),
        (corner_b.at[:, 0], field.at[:, row_b + (HALO - 1) * (1 - odd), side]),
        (corner_b.at[:, 1], field.at[:, row_b + (HALO - 2) * (1 - odd) + odd, side]),
    )
    unused = row_b + (HALO - 1) * odd
    field[:, pl.ds(unused, 1), rows_lon:] = jnp.zeros_like(field[:, pl.ds(unused, 1), rows_lon:])
    return [pltpu.make_async_copy(s, d, sems.at[n]) for n, (s, d) in enumerate(plan)]


def unfold_corner(field, rows_lon):
    odd = lax.rem(lax.axis_index("lat"), 2)
    row_b = (field.shape[1] - HALO) * odd
    second = row_b + (HALO - 2) * (1 - odd) + odd
    third = row_b + (HALO - 3) * (1 - odd) + 2 * odd
    for k in range(field.shape[0]):
        field[k, third, rows_lon:] = pltpu.roll(field[k, second, rows_lon:], 8 - FOLD, 0)


def sides_kernel(part_a, part_b, cross, folded):
    count, rows_lat, _, levels = part_a.shape
    even = lax.rem(lax.axis_index("lon"), 2) == 0
    odd = lax.rem(lax.axis_index("lat"), 2) == 1
    index = iota((8, levels), 0)
    inner = (index == FOLD - 1) | (index == FOLD)
    for k in range(count):
        rows = []
        for a in range(rows_lat):
            first = jnp.where(even, part_a[k, a], part_b[k, a])
            second = jnp.where(even, part_b[k, a], part_a[k, a])
            rows.append(jnp.concatenate([first, second], axis=0))
            cross[k, a] = rows[a]
        near = [jnp.where(odd, rows[rows_lat - 1 - r], rows[r]) for r in range(HALO - 1)]
        folded[k, 0] = near[0]
        folded[k, 1] = jnp.where(inner, pltpu.roll(near[2], FOLD, 0), near[1])


def keep_copy(field, kept, sems):
    inner = pl.ds(HALO // 2, field.shape[1] - HALO)
    return pltpu.make_async_copy(field.at[:, inner], kept, sems.at[7])


def smooth_power(field, powers, out, order, twice=None):
    count, rows, width, _ = field.shape
    rows_lat = rows - 2 * order
    rows_lon = width - 8
    lat = lax.axis_index("lat")
    north = (lat > 0).astype(F32)
    south = (lat < lax.axis_size("lat") - 1).astype(F32)
    factor = {2: (2.0, 1.0), 4: (4.0, 6.0, 4.0, 1.0)}[order]

    def one(k, carry):
        for c in range(width // 8):
            cols = slice(8 * c, 8 * c + 8)
            line = {i: field[k, i, cols] for i in range(rows)}
            for m in range(1, order + 1):
                fresh = {}
                for i in range(m, rows - m):
                    value = line[i - 1] + line[i + 1]
                    if i < order:
                        value = value * north
                    if i >= order + rows_lat:
                        value = value * south
                    fresh[i] = value
                line = fresh
                for i in range(rows_lat):
                    powers[m - 1, i, cols] = line[order + i]

        def step(value):
            ring = pltpu.roll(value, 1, 0) + pltpu.roll(value, width - 1, 0)
            return CENTER * value + SMOOTH * ring

        for i in range(rows_lat):
            value = field[k, order + i]
            for m in range(1, order + 1):
                value = step(value)
                if m == 1 and twice is not None:
                    other = step(value + (2.0 * SMOOTH) * powers[0, i])
                    other = other + SMOOTH**2 * powers[1, i]
                    twice[k, i] = other[:rows_lon]
                value = value + (factor[m - 1] * SMOOTH**m) * powers[m - 1, i]
            out[k, i] = value[:rows_lon]
        return carry

    lax.fori_loop(0, count, one, 0, unroll=count)


def observe(field, powers, smooth, mixed, squares, ivert, weights, ens, ens_copy, twice=None):
    members, windows, rows_lat, rows_lon, levels = ens.shape
    block = rows_lat * rows_lon
    smooth_power(field, powers, smooth, 4, twice)
    shape = (rows_lat, rows_lon, levels)
    for k in range(members + 1):
        square = squares[0] if k < members else squares[1]
        pair = jnp.concatenate(halves(smooth[k].reshape(block, levels)), axis=1)
        product = short_dot(pair, square)
        mixed[k] = (product[:, :levels] + product[:, levels:]).reshape(shape)
    ens_copy.wait()
    slots = weights.shape[1]
    image = jnp.zeros((8, slots), F32)
    high, low = halves(ivert[...])
    rows_of = jnp.concatenate([high, high, low], axis=0)
    for t in range(windows):
        lines = []
        for a in range(rows_lat):
            total = mixed[members, a]
            for k in range(members):
                total = total + ens[k, t, a].astype(F32) * mixed[k, a]
            lines.append(total)
        increment = jnp.stack(lines).reshape(block, levels)
        high, low = halves(increment)
        seen = short_dot(jnp.concatenate([high, low, high], axis=1), rows_of)
        seen = seen * weights[t * block : (t + 1) * block]
        image = image + jnp.sum(seen.reshape(block // 8, 8, slots), axis=0)
    return jnp.sum(image, axis=0, keepdims=True)


def middle_kernel(
    own, lat_a, lat_b, cross, corner_a, corner_b, ens_hbm, feat, ivert, squares,
    image, kept, fields, edge_a, edge_b,
    ens, field, powers, smooth, mixed, weights, high_weights, low_weights, grad, sem, sems,
):
    copies = halo_copies(own, lat_a, lat_b, cross, corner_a, corner_b, field, sems)
    for copy in copies:
        copy.start()
    ens_copy = pltpu.make_async_copy(ens_hbm, ens, sem)
    ens_copy.start()
    _, windows, rows_lat, rows_lon, _ = ens.shape
    fill_weights(feat, weights, high_weights, low_weights, windows, rows_lat, rows_lon)
    wait_all(copies)
    unfold_corner(field, rows_lon)
    keep = keep_copy(field, kept, sems)
    keep.start()
    seen = observe(field, powers, smooth, mixed, squares, ivert, weights, ens, ens_copy)
    scaled = seen * feat[7:8]
    image[...] = jnp.zeros_like(image)
    image[0:1] = seen
    image[1:2] = scaled
    outs = (fields, edge_a, edge_b)
    adjoint_fields(scaled, high_weights, low_weights, ivert, ens, (), grad, outs)
    keep.wait()


def last_kernel(
    slots,
    own, lat_a, lat_b, cross, corner_a, corner_b, ens_hbm, vert_hbm, static_hbm,
    feat, ivert, squares, image,
    send, late,
    ens, field, powers, smooth, mixed, weights, high_weights, low_weights, terms, twice,
    vert_loc, static_vert, sem, sems,
):
    copies = halo_copies(own, lat_a, lat_b, cross, corner_a, corner_b, field, sems)
    for copy in copies:
        copy.start()
    ens_copy = pltpu.make_async_copy(ens_hbm, ens, sem)
    ens_copy.start()
    _, windows, rows_lat, rows_lon, _ = ens.shape
    fill_weights(feat, weights, high_weights, low_weights, windows, rows_lat, rows_lon)
    matrices = fetch((vert_hbm, static_hbm), (vert_loc, static_vert), sems.at[pl.ds(8, 2)])
    wait_all(copies)
    unfold_corner(field, rows_lon)
    second = observe(field, powers, smooth, mixed, squares, ivert, weights, ens, ens_copy, twice)
    wait_all(matrices)
    to_control(twice, vert_loc, static_vert, late)
    start = feat[6:7]
    rinv = feat[7:8]
    first = image[0:1]
    scaled = image[1:2]
    norm = jnp.sum(start * first, axis=1, keepdims=True)
    curve = norm + jnp.sum(first * scaled, axis=1, keepdims=True)
    guess = jnp.where(curve > 0.0, norm / jnp.where(curve > 0.0, curve, 1.0), 1.0)
    guess = jnp.clip(guess, 0.0, 1.0)
    ahead = start + scaled
    ahead_image = first + second
    rest = start - guess * ahead
    rest_image = first - guess * ahead_image
    products = (
        start * first,
        first * scaled,
        rest * rest_image,
        rest * ahead_image + ahead * rest_image,
        ahead * ahead_image,
        rest_image * rinv * rest_image,
        2.0 * rest_image * rinv * ahead_image,
        ahead_image * rinv * ahead_image,
        2.0 * rest_image * scaled,
        2.0 * ahead_image * scaled,
        start * rest_image + rest * first,
        start * ahead_image + ahead * first,
    )
    terms[...] = jnp.zeros_like(terms)
    for n, value in enumerate(products):
        terms[n : n + 1] = value
    sums = jnp.sum(terms[...], axis=1, keepdims=True)
    owners = send.shape[0]
    per = LANES // slots
    below, across = iota((16, LANES), 0), iota((16, LANES), 1)
    line = jnp.sum(
        jnp.where(across == below + 2 * slots, sums, 0.0), axis=0, keepdims=True
    )
    spot = iota((owners, LANES), 1)
    source = spot - (iota((owners, LANES), 0) & (per - 1)) * slots
    mine = within(source, slots)
    parts = []
    targets = []
    target = iota((LANES, LANES), 0)
    slot = iota((LANES, LANES), 1) & (slots - 1)
    for n, value in enumerate((first, second)):
        groups = [
            jnp.broadcast_to(value[:, g * LANES : (g + 1) * LANES], (per, LANES))
            for g in range(owners // per)
        ]
        parts += halves(jnp.where(mine, jnp.concatenate(groups, axis=0), 0.0))
        targets += [(target == slot + n * slots).astype(F32).astype(BF16)] * 2
    moved = short_dot(
        jnp.concatenate(parts, axis=1), jnp.concatenate(targets, axis=1), ((1,), (1,))
    )
    tail = jnp.where(spot == 2 * slots + GUESS, guess, line)
    send[...] = jnp.where(spot < 2 * slots, moved, tail)


def to_control(smooth, vert_loc, static_vert, control):
    count, rows_lat, rows_lon, levels = smooth.shape
    blocks = []
    for scale, matrix in ((BETA_ENSEMBLE, vert_loc), (BETA_STATIC, static_vert)):
        high, low = halves(scale * matrix[...])
        upper = jnp.concatenate([high, high], axis=1)
        lower = jnp.concatenate([low, jnp.zeros_like(low)], axis=1)
        blocks.append(jnp.concatenate([upper, lower], axis=0))
    for k in range(count):
        pair = jnp.concatenate(halves(smooth[k].reshape(rows_lat * rows_lon, levels)), axis=1)
        product = short_dot(pair, blocks[k // (count - 1)], ((1,), (1,)))
        product = product[:, :levels] + product[:, levels:]
        control[k] = product.reshape(rows_lat, rows_lon, levels)


def control_kernel(
    kept, vert_hbm, static_hbm,
    control,
    field, powers, smooth, vert_loc, static_vert, sems,
):
    wait_all(fetch((vert_hbm, static_hbm, kept), (vert_loc, static_vert, field), sems))
    smooth_power(field, powers, smooth, 2)
    to_control(smooth, vert_loc, static_vert, control)


def final_kernel(
    recv, early, late, dest_hbm, lane_hbm,
    static_hbm, member_hbm, equivalent_hbm,
    dest, lane, equivalent, result, sems, out_sems,
):
    small = fetch((dest_hbm, lane_hbm), (dest, lane), sems)
    count = early.shape[0]
    owners = recv.shape[0]
    rows = dest.shape[1]
    slots = 2 * rows // owners
    blocks = recv[...]
    sums = jnp.sum(blocks, axis=0, keepdims=True)

    def pick(values, n):
        return values[:, 2 * slots + n : 2 * slots + n + 1]

    norm = pick(sums, 0)
    step = norm / (norm + pick(sums, 1))
    off = pick(blocks, GUESS) - step
    linear = jnp.sum(off * blocks, axis=0, keepdims=True)
    square = jnp.sum(off * off * blocks, axis=0, keepdims=True)
    norm_next = jnp.maximum(pick(sums, 2) + pick(linear, 3) + pick(square, 4), 0.0)
    beta = norm_next / norm
    bend = pick(sums, 5) + pick(linear, 6) + pick(square, 7)
    bend = bend + beta * (pick(sums, 8) + pick(linear, 9)) + beta * beta * pick(sums, 1)
    length = norm_next + beta * (pick(sums, 10) + pick(linear, 11)) + beta * beta * norm
    curve = length + bend
    step_next = jnp.where(curve > 0.0, norm_next / jnp.where(curve > 0.0, curve, 1.0), 0.0)
    step_next = jnp.minimum(step_next, 1.0)
    near = step + step_next * ((1.0 - step) + beta)
    far = -step_next * step
    stores = []
    for k in range(count):
        result[k] = near[None] * early[k] + far[None] * late[k]
        target = member_hbm.at[k] if k < count - 1 else static_hbm
        stores.append(pltpu.make_async_copy(result.at[k], target, out_sems.at[k]))
        stores[k].start()
    wait_all(small)
    chosen = (iota((owners, rows), 0) == dest[...]).astype(F32).astype(BF16)
    table = short_dot(
        jnp.concatenate(halves(blocks), axis=0),
        jnp.concatenate([chosen] * 2, axis=0),
        ((0,), (0,)),
    )
    spot = iota((LANES, rows), 0)
    factor = jnp.where(spot == lane[...], near, 0.0)
    factor = jnp.where(spot == lane[...] + slots, far, factor)
    equivalent[...] = jnp.sum(factor * table, axis=0, keepdims=True)
    stores.append(pltpu.make_async_copy(equivalent, equivalent_hbm, out_sems.at[count]))
    stores[count].start()
    wait_all(stores)


def shape(*dims):
    return jax.ShapeDtypeStruct(dims, F32)


def stay(*values):
    return [pltpu.with_memory_space_constraint(value, pltpu.HBM) for value in values]


def swaps(count, ring):
    inner = [(i, i ^ 1) for i in range(count)]
    outer = []
    for i in range(1, count - 1, 2):
        outer += [(i, i + 1), (i + 1, i)]
    if ring:
        outer += [(count - 1, 0), (0, count - 1)]
    return inner, outer


def body(
    ensemble,
    vert_loc,
    static_vert,
    inst_vert,
    inst_err,
    obs_dest,
    obs_patch,
    obs_window,
    obs_inst,
    obs_hweight,
    innovation,
    obs_count,
):
    members, windows, rows_lat, rows_lon, levels = ensemble.shape
    lat_count = lax.axis_size("lat")
    lon_count = lax.axis_size("lon")
    owners = lat_count * lon_count
    rows = innovation.shape[0]
    slots = 2 * rows // owners
    total = owners * slots
    patches = rows_lat // 2 * (rows_lon // 2)
    count = members + 1
    width = rows_lon + 8
    lat_inner, lat_outer = swaps(lat_count, False)
    lon_inner, lon_outer = swaps(lon_count, True)
    tile = shape(count, rows_lat, rows_lon, levels)
    edge = shape(count, rows_lat, HALO, levels)

    def line(values):
        return values.reshape(1, rows)

    dest = line(obs_dest)
    row_scratch = pltpu.VMEM((1, rows), jnp.int32)
    send, lane = pl.pallas_call(
        functools.partial(pack_kernel, slots, patches),
        out_shape=(shape(owners, LANES), pltpu.HBM((1, rows), jnp.int32)),
        in_specs=[HBM] * 6 + [SMEM],
        out_specs=(VMEM, HBM),
        scratch_shapes=[row_scratch] * 4
        + [
            pltpu.VMEM(obs_hweight.shape, F32),
            pltpu.VMEM((1, rows), F32),
            pltpu.VMEM((8, rows), F32),
            row_scratch,
            pltpu.VMEM((LANES, rows), F32),
            DMA((7,)),
        ],
        compiler_params=PARAMS,
        name="pack",
    )(
        *stay(
            dest,
            line(obs_patch),
            line(obs_window),
            line(obs_inst),
            obs_hweight,
            line(innovation),
        ),
        obs_count,
    )
    squares = pl.pallas_call(
        prepare_kernel,
        out_shape=jax.ShapeDtypeStruct((2, 2 * levels, 2 * levels), BF16),
        compiler_params=PARAMS,
        name="prepare",
    )(vert_loc, static_vert)

    def exchange(blocks):
        return lax.all_to_all(blocks, ("lat", "lon"), split_axis=0, concat_axis=0, tiled=True)

    recv = exchange(send)
    ens_scratch = pltpu.VMEM(ensemble.shape, ensemble.dtype)
    field_scratch = pltpu.VMEM((count, rows_lat + 2 * HALO, width, levels), F32)
    tile_scratch = pltpu.VMEM(tile.shape, F32)
    weight_scratch = pltpu.VMEM((windows * rows_lat * rows_lon, total), F32)
    half_scratch = pltpu.VMEM(weight_scratch.shape, BF16)
    grad_scratch = pltpu.VMEM((windows * rows_lat * rows_lon, levels), F32)

    def powers(order):
        return pltpu.VMEM((order, rows_lat, width, levels), F32)

    feat, ivert, *outs = pl.pallas_call(
        functools.partial(first_kernel, slots),
        out_shape=(shape(8, total), shape(levels, total), tile, edge, edge),
        in_specs=[VMEM, HBM, HBM, HBM],
        out_specs=(VMEM,) * 5,
        scratch_shapes=[
            pltpu.VMEM(inst_vert.shape, F32),
            pltpu.VMEM((1, inst_err.shape[0]), F32),
            ens_scratch,
            weight_scratch,
            half_scratch,
            half_scratch,
            grad_scratch,
            DMA((2 + members,)),
        ],
        compiler_params=PARAMS,
        name="first",
    )(recv, *stay(inst_vert, inst_err.reshape(1, -1), ensemble))

    def sides(part_a, part_b):
        return pl.pallas_call(
            sides_kernel,
            out_shape=(
                shape(count, rows_lat, 8, levels),
                shape(count, 2, 8, levels),
            ),
            in_specs=[VMEM] * 2,
            out_specs=(VMEM,) * 2,
            compiler_params=PARAMS,
            name="sides",
        )(part_a, part_b)

    def halo(fields, edge_a, edge_b):
        lat_b = lax.ppermute(fields, "lat", lat_outer)
        side_a = lax.ppermute(edge_a, "lon", lon_inner)
        side_b = lax.ppermute(edge_b, "lon", lon_outer)
        lat_a = lax.ppermute(fields, "lat", lat_inner)
        cross, folded = sides(side_a, side_b)
        corner_b = lax.ppermute(folded, "lat", lat_outer)
        corner_a = lax.ppermute(cross, "lat", lat_inner)
        return (fields, lat_a, lat_b, cross, corner_a, corner_b)

    parts = halo(*outs)
    matrix_scratch = pltpu.VMEM(vert_loc.shape, F32)
    work = [ens_scratch, field_scratch, powers(4), tile_scratch, tile_scratch, weight_scratch]
    work += [half_scratch] * 2
    sems = [DMA, DMA((8,))]
    kept_shape = pltpu.HBM((count, rows_lat + HALO, width, levels), F32)
    image, kept_early, *outs = pl.pallas_call(
        middle_kernel,
        out_shape=(shape(8, total), kept_shape, tile, edge, edge),
        in_specs=[ANY] * 6 + [HBM] + [VMEM] * 3,
        out_specs=(VMEM, HBM) + (VMEM,) * 3,
        scratch_shapes=work + [grad_scratch] + sems,
        compiler_params=PARAMS,
        name="middle",
    )(*parts, *stay(ensemble), feat, ivert, squares)
    early = pl.pallas_call(
        control_kernel,
        out_shape=tile,
        in_specs=[HBM] * 3,
        out_specs=VMEM,
        scratch_shapes=[
            pltpu.VMEM(kept_shape.shape, F32),
            powers(2),
            tile_scratch,
            matrix_scratch,
            matrix_scratch,
            DMA((3,)),
        ],
        compiler_params=PARAMS,
        name="control",
    )(*stay(kept_early, vert_loc, static_vert))
    parts = halo(*outs)
    send, late = pl.pallas_call(
        functools.partial(last_kernel, slots),
        out_shape=(shape(owners, LANES), tile),
        in_specs=[ANY] * 6 + [HBM] * 3 + [VMEM] * 4,
        out_specs=(VMEM,) * 2,
        scratch_shapes=work
        + [pltpu.VMEM((16, total), F32), tile_scratch, matrix_scratch, matrix_scratch]
        + [DMA, DMA((10,))],
        compiler_params=PARAMS,
        name="last",
    )(*parts, *stay(ensemble, vert_loc, static_vert), feat, ivert, squares, image)
    recv = exchange(send)
    static, member, equivalent = pl.pallas_call(
        final_kernel,
        out_shape=(
            shape(rows_lat, rows_lon, levels),
            shape(members, rows_lat, rows_lon, levels),
            shape(1, rows),
        ),
        in_specs=[VMEM] * 3 + [HBM] * 2,
        out_specs=(HBM,) * 3,
        scratch_shapes=[
            row_scratch,
            row_scratch,
            pltpu.VMEM((1, rows), F32),
            tile_scratch,
            DMA((2,)),
            DMA((count + 1,)),
        ],
        compiler_params=PARAMS,
        name="final",
    )(recv, early, late, *stay(dest, lane))
    return static, member, equivalent.reshape(rows)


def solution(mesh):
    return jax.shard_map(
        body,
        mesh=mesh,
        in_specs=(
            P(None, None, "lat", "lon", None),
            P(),
            P(),
            P(),
            P(),
            P(("lat", "lon"), None),
            P(("lat", "lon")),
            P(("lat", "lon")),
            P(("lat", "lon")),
            P(None, ("lat", "lon")),
            P(("lat", "lon")),
            P(("lat", "lon")),
        ),
        out_specs=(P("lat", "lon", None), P(None, "lat", "lon", None), P(("lat", "lon"))),
        check_vma=False,
    )
```

```python
import functools

import jax
import jax.numpy as jnp
from jax import lax
from jax.experimental import pallas as pl
from jax.experimental.pallas import tpu as pltpu
from jax.sharding import PartitionSpec as P


SMOOTH = 0.15
CENTER = 1.0 - 4.0 * SMOOTH
BETA_STATIC = 0.5
BETA_ENSEMBLE = 0.85
HALO = 4
FOLD = 3
GUESS = 12
LANES = 128
HIGHEST = lax.Precision.HIGHEST
F32 = jnp.float32
BF16 = jnp.bfloat16

HBM = pl.BlockSpec(memory_space=pltpu.HBM)
VMEM = pl.BlockSpec(memory_space=pltpu.VMEM)
SMEM = pl.BlockSpec(memory_space=pltpu.SMEM)
PARAMS = pltpu.CompilerParams(vmem_limit_bytes=32 * 1024 * 1024)
DMA = pltpu.SemaphoreType.DMA


def dot(left, right, dims=((1,), (0,))):
    return lax.dot_general(
        left, right, (dims, ((), ())), precision=HIGHEST, preferred_element_type=F32
    )


def iota(shape, dim):
    return lax.broadcasted_iota(jnp.int32, shape, dim)


def halves(value):
    high = value.astype(BF16)
    return high, (value - high.astype(F32)).astype(BF16)


def thirds(value):
    high = value.astype(BF16)
    rest = value - high.astype(F32)
    middle = rest.astype(BF16)
    return high, middle, (rest - middle.astype(F32)).astype(BF16)


def within(value, length):
    return (value >= 0) & (value < length)


def fetch(sources, targets, sems):
    copies = [
        pltpu.make_async_copy(source, target, sems.at[n])
        for n, (source, target) in enumerate(zip(sources, targets))
    ]
    for copy in copies:
        copy.start()
    return copies


def wait_all(copies):
    for copy in copies:
        copy.wait()


def short_dot(left, right, dims=((1,), (0,))):
    return lax.dot_general(left, right, (dims, ((), ())), preferred_element_type=F32)


def pack_kernel(
    slots, patches,
    dest_hbm, patch_hbm, window_hbm, inst_hbm, hweight_hbm, innov_hbm, count,
    send, lane_hbm,
    dest, patch, window, inst, hweight, innov, feat, lane, table, sems,
):
    wait_all(
        fetch(
            (dest_hbm, patch_hbm, window_hbm, inst_hbm, hweight_hbm, innov_hbm),
            (dest, patch, window, inst, hweight, innov),
            sems,
        )
    )
    owners = send.shape[0]
    rows = dest.shape[1]
    destination = dest[...]
    row, col = iota((rows, rows), 0), iota((rows, rows), 1)
    upright = jnp.sum(
        jnp.where(row == col, destination.astype(F32), 0.0), axis=1, keepdims=True
    ).astype(jnp.int32)
    earlier = (upright == destination) & (row < col)
    ranking = jnp.sum(jnp.where(earlier, 1.0, 0.0), axis=0, keepdims=True).astype(jnp.int32)
    lane[...] = ranking
    lane_copy = pltpu.make_async_copy(lane, lane_hbm, sems.at[6])
    lane_copy.start()
    active = (iota((1, rows), 1) < count[0]).astype(F32)
    feat[0:1] = (window[...] * patches + patch[...]).astype(F32)
    feat[1:2] = inst[...].astype(F32)
    feat[2:6] = hweight[...] * active
    feat[6:7] = innov[...]
    table[...] = jnp.zeros_like(table)
    here = iota((slots, rows), 0) == ranking
    for f in range(7):
        table[f * slots : (f + 1) * slots] = jnp.where(here, feat[f : f + 1], 0.0)
    chosen = (iota((owners, rows), 0) == destination).astype(F32).astype(BF16)
    send[...] = short_dot(
        jnp.concatenate([chosen] * 3, axis=1),
        jnp.concatenate(thirds(table[...]), axis=1),
        ((1,), (1,)),
    )
    lane_copy.wait()


def prepare_kernel(vert_loc, static_vert, squares):
    levels = vert_loc.shape[0]
    squares[...] = jnp.zeros_like(squares)
    for n, (scale, matrix) in enumerate(((BETA_ENSEMBLE, vert_loc), (BETA_STATIC, static_vert))):
        high, low = halves(scale**2 * dot(matrix[...], matrix[...], ((0,), (0,))))
        squares[n, :levels, :levels] = high
        squares[n, :levels, levels:] = low
        squares[n, levels:, :levels] = high


def fill_weights(feat, weights, high_weights, low_weights, windows, rows_lat, rows_lon):
    slots = feat.shape[1]
    cell = feat[0:1].astype(jnp.int32)
    half = iota((rows_lon, slots), 0) >> 1
    odd = (iota((rows_lon, slots), 0) & 1) == 1
    corner = [
        jnp.where(odd, feat[3 + 2 * q : 4 + 2 * q], feat[2 + 2 * q : 3 + 2 * q]) for q in range(2)
    ]
    per_window = rows_lat // 2 * (rows_lon // 2)
    for t in range(windows):
        for a in range(rows_lat):
            first = t * per_window + a // 2 * (rows_lon // 2)
            row = (t * rows_lat + a) * rows_lon
            rows = slice(row, row + rows_lon)
            value = jnp.where(half == cell - first, corner[a % 2], 0.0)
            weights[rows] = value
            high_weights[rows], low_weights[rows] = halves(value)


def adjoint_fields(amount, high_weights, low_weights, ivert, ens, ens_copies, grad, outs):
    fields, edge_a, edge_b = outs
    members, windows, rows_lat, rows_lon, levels = ens.shape
    block = rows_lat * rows_lon
    high, low = halves(ivert[...] * amount)
    both = jnp.concatenate([high, low], axis=0)
    for t in range(windows):
        rows = slice(t * block, (t + 1) * block)
        pair = short_dot(high_weights[rows], both, ((1,), (1,)))
        rest = short_dot(low_weights[rows], high, ((1,), (1,)))
        grad[rows] = pair[:, :levels] + pair[:, levels:] + rest
    even = lax.rem(lax.axis_index("lon"), 2) == 0

    def part(t, a):
        first = (t * rows_lat + a) * rows_lon
        return grad[first : first + rows_lon]

    for k in range(members + 1):
        if k < members and ens_copies:
            ens_copies[k].wait()
        for a in range(rows_lat):
            total = part(0, a) if k == members else ens[k, 0, a].astype(F32) * part(0, a)
            for t in range(1, windows):
                term = part(t, a) if k == members else ens[k, t, a].astype(F32) * part(t, a)
                total = total + term
            fields[k, a] = total
            east = total[rows_lon - HALO :]
            west = total[:HALO]
            edge_a[k, a] = jnp.where(even, east, west)
            edge_b[k, a] = jnp.where(even, west, east)


def first_kernel(
    slots,
    recv, inst_vert_hbm, inst_err_hbm, ens_hbm,
    feat, ivert, ens, weights, high_weights, low_weights, fields, edge_a, edge_b,
    inst_vert, inst_err, grad, sems,
):
    members = ens.shape[0]
    copies = fetch(
        [inst_vert_hbm, inst_err_hbm] + [ens_hbm.at[k] for k in range(members)],
        [inst_vert, inst_err] + [ens.at[k] for k in range(members)],
        sems,
    )
    members, windows, rows_lat, rows_lon, _ = ens.shape
    owners = recv.shape[0]
    total = feat.shape[1]
    source = iota((owners, total), 1) - iota((owners, total), 0) * slots
    mine = within(source, slots).astype(F32).astype(BF16)
    lines = short_dot(
        jnp.concatenate(thirds(recv[...]), axis=0),
        jnp.concatenate([mine] * 3, axis=0),
        ((0,), (0,)),
    )
    same = (iota((LANES, total), 0) & (slots - 1)) == (iota((LANES, total), 1) & (slots - 1))
    lines = jnp.where(same, lines, 0.0)
    for f in range(8):
        feat[f : f + 1] = jnp.sum(lines[f * slots : (f + 1) * slots], axis=0, keepdims=True)
    wait_all(copies[:2])
    instruments = inst_vert.shape[0]
    onehot = (iota((instruments, total), 0) == feat[1:2].astype(jnp.int32)).astype(F32)
    ivert[...] = dot(inst_vert[...].T, onehot)
    inverse = jnp.broadcast_to(1.0 / (inst_err[...] * inst_err[...]), (8, instruments))
    rinv = dot(inverse, onehot)[0:1]
    feat[6:7] = feat[6:7] * rinv
    feat[7:8] = rinv
    fill_weights(feat, weights, high_weights, low_weights, windows, rows_lat, rows_lon)
    outs = (fields, edge_a, edge_b)
    adjoint_fields(feat[6:7], high_weights, low_weights, ivert, ens, copies[2:], grad, outs)


def corner_terms(corner_a, corner_b, k, rows_lat, order):
    odd = lax.rem(lax.axis_index("lat"), 2) == 1
    near = {}
    for r in range(1, HALO):
        tile_a = jnp.where(odd, corner_a[k, rows_lat - r], corner_a[k, r - 1])
        tile_b = corner_b[k, min(r, 2) - 1]
        if r == 3:
            tile_b = pltpu.roll(tile_b, 8 - FOLD, 0)
        near[-r] = jnp.where(odd, tile_a, tile_b)
        near[rows_lat - 1 + r] = jnp.where(odd, tile_b, tile_a)
    none = jnp.zeros_like(near[-1])
    line = {i: near.get(i, none) for i in range(1 - HALO, rows_lat + HALO - 1)}
    powers = []
    for m in range(1, order):
        line = {
            i: line[i - 1] + line[i + 1]
            for i in range(1 - HALO + m, rows_lat + HALO - 1 - m)
        }
        powers.append(line)
    factor = {2: (2.0,), 4: (4.0, 6.0, 4.0)}[order]
    added = []
    for i in range(rows_lat):
        value = None
        for m in range(1, order):
            fresh = (factor[m - 1] * SMOOTH**m) * powers[m - 1][i]
            fresh = jnp.concatenate([none, fresh, none], axis=0)
            value = fresh if value is None else value + fresh
            ring = pltpu.roll(value, 1, 0) + pltpu.roll(value, value.shape[0] - 1, 0)
            value = CENTER * value + SMOOTH * ring
        added.append((value[:8], value[16:]))
    return added


def with_corners(smooth, corner_a, corner_b, k, order):
    rows_lat, rows_lon = smooth.shape[1:3]
    added = corner_terms(corner_a, corner_b, k, rows_lat, order)
    pieces = []
    for i in range(rows_lat):
        last, first = added[i]
        pieces += [
            smooth[k, i, :8] + first,
            smooth[k, i, 8 : rows_lon - 8],
            smooth[k, i, rows_lon - 8 :] + last,
        ]
    return jnp.concatenate(pieces, axis=0)


def sides_kernel(part_a, part_b, cross, folded):
    count, rows_lat, _, levels = part_a.shape
    even = lax.rem(lax.axis_index("lon"), 2) == 0
    odd = lax.rem(lax.axis_index("lat"), 2) == 1
    index = iota((8, levels), 0)
    inner = (index == FOLD - 1) | (index == FOLD)
    for k in range(count):
        rows = []
        for a in range(rows_lat):
            first = jnp.where(even, part_a[k, a], part_b[k, a])
            second = jnp.where(even, part_b[k, a], part_a[k, a])
            rows.append(jnp.concatenate([first, second], axis=0))
            cross[k, a] = rows[a]
        near = [jnp.where(odd, rows[rows_lat - 1 - r], rows[r]) for r in range(HALO - 1)]
        folded[k, 0] = near[0]
        folded[k, 1] = jnp.where(inner, pltpu.roll(near[2], FOLD, 0), near[1])


def smooth_kernel(own, lat_a, lat_b, cross, smooth, twice, powers):
    count, rows_lat, rows_lon, _ = own.shape
    width = rows_lon + 8
    order = HALO
    lat = lax.axis_index("lat")
    odd = lax.rem(lat, 2)
    inside = jnp.where(odd == 1, lat < lax.axis_size("lat") - 1, lat > 0).astype(F32)
    factor = (4.0, 6.0, 4.0, 1.0)

    def turned(row):
        return rows_lat - 1 - row + odd * (2 * row - rows_lat + 1)

    def step(value):
        ring = pltpu.roll(value, 1, 0) + pltpu.roll(value, width - 1, 0)
        return CENTER * value + SMOOTH * ring

    def one(k, carry):
        for c in range(width // 8):
            cols = slice(8 * c, 8 * c + 8)
            if c < rows_lon // 8:
                line = {i: own[k, turned(i), cols] for i in range(rows_lat)}
                for r in range(order):
                    line[-1 - r] = lat_a[k, turned(rows_lat - 1 - r), cols]
                    line[rows_lat + r] = lat_b[k, turned(r), cols]
            else:
                line = {i: cross[k, turned(i)] for i in range(rows_lat)}
                none = jnp.zeros_like(line[0])
                for r in range(order):
                    line[-1 - r] = line[rows_lat + r] = none
            for m in range(1, order + 1):
                fresh = {}
                for i in range(m - order, rows_lat + order - m):
                    value = line[i - 1] + line[i + 1]
                    fresh[i] = value * inside if i >= rows_lat else value
                line = fresh
                for i in range(rows_lat):
                    powers[m - 1, i, cols] = line[i]
        for i in range(rows_lat):
            row = turned(i)
            value = jnp.concatenate([own[k, row], cross[k, row]], axis=0)
            for m in range(1, order + 1):
                value = step(value)
                if m == 1:
                    other = step(value + (2.0 * SMOOTH) * powers[0, i])
                    other = other + SMOOTH**2 * powers[1, i]
                    twice[k, row] = other[:rows_lon]
                value = value + (factor[m - 1] * SMOOTH**m) * powers[m - 1, i]
            smooth[k, row] = value[:rows_lon]
        return carry

    lax.fori_loop(0, count, one, 0, unroll=count)


def observe(smooth, corner_a, corner_b, mixed, squares, ivert, weights, ens):
    members, windows, rows_lat, rows_lon, levels = ens.shape
    block = rows_lat * rows_lon
    shape = (rows_lat, rows_lon, levels)
    for k in range(members + 1):
        square = squares[0] if k < members else squares[1]
        pair = jnp.concatenate(halves(with_corners(smooth, corner_a, corner_b, k, 4)), axis=1)
        product = short_dot(pair, square)
        mixed[k] = (product[:, :levels] + product[:, levels:]).reshape(shape)
    slots = weights.shape[1]
    image = jnp.zeros((8, slots), F32)
    high, low = halves(ivert[...])
    rows_of = jnp.concatenate([high, high, low], axis=0)
    for t in range(windows):
        lines = []
        for a in range(rows_lat):
            total = mixed[members, a]
            for k in range(members):
                total = total + ens[k, t, a].astype(F32) * mixed[k, a]
            lines.append(total)
        increment = jnp.stack(lines).reshape(block, levels)
        high, low = halves(increment)
        seen = short_dot(jnp.concatenate([high, low, high], axis=1), rows_of)
        seen = seen * weights[t * block : (t + 1) * block]
        image = image + jnp.sum(seen.reshape(block // 8, 8, slots), axis=0)
    return jnp.sum(image, axis=0, keepdims=True)


def middle_kernel(
    smooth, corner_a, corner_b, feat, ivert, ens, weights, high_weights, low_weights, squares,
    image, fields, edge_a, edge_b,
    mixed, grad,
):
    seen = observe(smooth, corner_a, corner_b, mixed, squares, ivert, weights, ens)
    scaled = seen * feat[7:8]
    image[...] = jnp.zeros_like(image)
    image[0:1] = seen
    image[1:2] = scaled
    outs = (fields, edge_a, edge_b)
    adjoint_fields(scaled, high_weights, low_weights, ivert, ens, (), grad, outs)


def last_kernel(
    slots,
    smooth, corner_a, corner_b, vert_hbm, static_hbm,
    feat, ivert, ens, weights, squares, image, twice,
    send, late,
    mixed, terms, vert_loc, static_vert, sems,
):
    matrices = fetch((vert_hbm, static_hbm), (vert_loc, static_vert), sems)
    second = observe(smooth, corner_a, corner_b, mixed, squares, ivert, weights, ens)
    wait_all(matrices)
    to_control(twice, corner_a, corner_b, vert_loc, static_vert, late)
    start = feat[6:7]
    rinv = feat[7:8]
    first = image[0:1]
    scaled = image[1:2]
    norm = jnp.sum(start * first, axis=1, keepdims=True)
    curve = norm + jnp.sum(first * scaled, axis=1, keepdims=True)
    guess = jnp.where(curve > 0.0, norm / jnp.where(curve > 0.0, curve, 1.0), 1.0)
    guess = jnp.clip(guess, 0.0, 1.0)
    ahead = start + scaled
    ahead_image = first + second
    rest = start - guess * ahead
    rest_image = first - guess * ahead_image
    products = (
        start * first,
        first * scaled,
        rest * rest_image,
        rest * ahead_image + ahead * rest_image,
        ahead * ahead_image,
        rest_image * rinv * rest_image,
        2.0 * rest_image * rinv * ahead_image,
        ahead_image * rinv * ahead_image,
        2.0 * rest_image * scaled,
        2.0 * ahead_image * scaled,
        start * rest_image + rest * first,
        start * ahead_image + ahead * first,
    )
    terms[...] = jnp.zeros_like(terms)
    for n, value in enumerate(products):
        terms[n : n + 1] = value
    sums = jnp.sum(terms[...], axis=1, keepdims=True)
    owners = send.shape[0]
    per = LANES // slots
    below, across = iota((16, LANES), 0), iota((16, LANES), 1)
    line = jnp.sum(
        jnp.where(across == below + 2 * slots, sums, 0.0), axis=0, keepdims=True
    )
    spot = iota((owners, LANES), 1)
    source = spot - (iota((owners, LANES), 0) & (per - 1)) * slots
    mine = within(source, slots)
    parts = []
    targets = []
    target = iota((LANES, LANES), 0)
    slot = iota((LANES, LANES), 1) & (slots - 1)
    for n, value in enumerate((first, second)):
        groups = [
            jnp.broadcast_to(value[:, g * LANES : (g + 1) * LANES], (per, LANES))
            for g in range(owners // per)
        ]
        parts += halves(jnp.where(mine, jnp.concatenate(groups, axis=0), 0.0))
        targets += [(target == slot + n * slots).astype(F32).astype(BF16)] * 2
    moved = short_dot(
        jnp.concatenate(parts, axis=1), jnp.concatenate(targets, axis=1), ((1,), (1,))
    )
    tail = jnp.where(spot == 2 * slots + GUESS, guess, line)
    send[...] = jnp.where(spot < 2 * slots, moved, tail)


def to_control(smooth, corner_a, corner_b, vert_loc, static_vert, control):
    count, rows_lat, rows_lon, levels = smooth.shape
    blocks = []
    for scale, matrix in ((BETA_ENSEMBLE, vert_loc), (BETA_STATIC, static_vert)):
        high, low = halves(scale * matrix[...])
        upper = jnp.concatenate([high, high], axis=1)
        lower = jnp.concatenate([low, jnp.zeros_like(low)], axis=1)
        blocks.append(jnp.concatenate([upper, lower], axis=0))
    for k in range(count):
        pair = jnp.concatenate(halves(with_corners(smooth, corner_a, corner_b, k, 2)), axis=1)
        product = short_dot(pair, blocks[k // (count - 1)], ((1,), (1,)))
        product = product[:, :levels] + product[:, levels:]
        control[k] = product.reshape(rows_lat, rows_lon, levels)


def control_kernel(
    twice, corner_a, corner_b, vert_hbm, static_hbm, control, vert_loc, static_vert, sems
):
    wait_all(fetch((vert_hbm, static_hbm), (vert_loc, static_vert), sems))
    to_control(twice, corner_a, corner_b, vert_loc, static_vert, control)


def final_kernel(
    recv, early, late, dest_hbm, lane_hbm,
    static_hbm, member_hbm, equivalent_hbm,
    dest, lane, equivalent, result, sems, out_sems,
):
    small = fetch((dest_hbm, lane_hbm), (dest, lane), sems)
    count = early.shape[0]
    owners = recv.shape[0]
    rows = dest.shape[1]
    slots = 2 * rows // owners
    blocks = recv[...]
    sums = jnp.sum(blocks, axis=0, keepdims=True)

    def pick(values, n):
        return values[:, 2 * slots + n : 2 * slots + n + 1]

    norm = pick(sums, 0)
    step = norm / (norm + pick(sums, 1))
    off = pick(blocks, GUESS) - step
    linear = jnp.sum(off * blocks, axis=0, keepdims=True)
    square = jnp.sum(off * off * blocks, axis=0, keepdims=True)
    norm_next = jnp.maximum(pick(sums, 2) + pick(linear, 3) + pick(square, 4), 0.0)
    beta = norm_next / norm
    bend = pick(sums, 5) + pick(linear, 6) + pick(square, 7)
    bend = bend + beta * (pick(sums, 8) + pick(linear, 9)) + beta * beta * pick(sums, 1)
    length = norm_next + beta * (pick(sums, 10) + pick(linear, 11)) + beta * beta * norm
    curve = length + bend
    step_next = jnp.where(curve > 0.0, norm_next / jnp.where(curve > 0.0, curve, 1.0), 0.0)
    step_next = jnp.minimum(step_next, 1.0)
    near = step + step_next * ((1.0 - step) + beta)
    far = -step_next * step
    stores = []
    for k in range(count):
        result[k] = near[None] * early[k] + far[None] * late[k]
        target = member_hbm.at[k] if k < count - 1 else static_hbm
        stores.append(pltpu.make_async_copy(result.at[k], target, out_sems.at[k]))
        stores[k].start()
    wait_all(small)
    chosen = (iota((owners, rows), 0) == dest[...]).astype(F32).astype(BF16)
    table = short_dot(
        jnp.concatenate(halves(blocks), axis=0),
        jnp.concatenate([chosen] * 2, axis=0),
        ((0,), (0,)),
    )
    spot = iota((LANES, rows), 0)
    factor = jnp.where(spot == lane[...], near, 0.0)
    factor = jnp.where(spot == lane[...] + slots, far, factor)
    equivalent[...] = jnp.sum(factor * table, axis=0, keepdims=True)
    stores.append(pltpu.make_async_copy(equivalent, equivalent_hbm, out_sems.at[count]))
    stores[count].start()
    wait_all(stores)


def shape(*dims):
    return jax.ShapeDtypeStruct(dims, F32)


def stay(*values):
    return [pltpu.with_memory_space_constraint(value, pltpu.HBM) for value in values]


def swaps(count, ring):
    inner = [(i, i ^ 1) for i in range(count)]
    outer = []
    for i in range(1, count - 1, 2):
        outer += [(i, i + 1), (i + 1, i)]
    if ring:
        outer += [(count - 1, 0), (0, count - 1)]
    return inner, outer


def body(
    ensemble,
    vert_loc,
    static_vert,
    inst_vert,
    inst_err,
    obs_dest,
    obs_patch,
    obs_window,
    obs_inst,
    obs_hweight,
    innovation,
    obs_count,
):
    members, windows, rows_lat, rows_lon, levels = ensemble.shape
    lat_count = lax.axis_size("lat")
    lon_count = lax.axis_size("lon")
    owners = lat_count * lon_count
    rows = innovation.shape[0]
    slots = 2 * rows // owners
    total = owners * slots
    patches = rows_lat // 2 * (rows_lon // 2)
    count = members + 1
    lat_inner, lat_outer = swaps(lat_count, False)
    lon_inner, lon_outer = swaps(lon_count, True)
    tile = shape(count, rows_lat, rows_lon, levels)
    edge = shape(count, rows_lat, HALO, levels)

    def line(values):
        return values.reshape(1, rows)

    dest = line(obs_dest)
    row_scratch = pltpu.VMEM((1, rows), jnp.int32)
    send, lane = pl.pallas_call(
        functools.partial(pack_kernel, slots, patches),
        out_shape=(shape(owners, LANES), pltpu.HBM((1, rows), jnp.int32)),
        in_specs=[HBM] * 6 + [SMEM],
        out_specs=(VMEM, HBM),
        scratch_shapes=[row_scratch] * 4
        + [
            pltpu.VMEM(obs_hweight.shape, F32),
            pltpu.VMEM((1, rows), F32),
            pltpu.VMEM((8, rows), F32),
            row_scratch,
            pltpu.VMEM((LANES, rows), F32),
            DMA((7,)),
        ],
        compiler_params=PARAMS,
        name="pack",
    )(
        *stay(
            dest,
            line(obs_patch),
            line(obs_window),
            line(obs_inst),
            obs_hweight,
            line(innovation),
        ),
        obs_count,
    )
    squares = pl.pallas_call(
        prepare_kernel,
        out_shape=jax.ShapeDtypeStruct((2, 2 * levels, 2 * levels), BF16),
        compiler_params=PARAMS,
        name="prepare",
    )(vert_loc, static_vert)

    def exchange(blocks):
        return lax.all_to_all(blocks, ("lat", "lon"), split_axis=0, concat_axis=0, tiled=True)

    recv = exchange(send)
    cells = windows * rows_lat * rows_lon
    tile_scratch = pltpu.VMEM(tile.shape, F32)
    grad_scratch = pltpu.VMEM((cells, levels), F32)

    feat, ivert, ens, *weights, fields, edge_a, edge_b = pl.pallas_call(
        functools.partial(first_kernel, slots),
        out_shape=(
            shape(8, total),
            shape(levels, total),
            jax.ShapeDtypeStruct(ensemble.shape, ensemble.dtype),
            shape(cells, total),
            jax.ShapeDtypeStruct((cells, total), BF16),
            jax.ShapeDtypeStruct((cells, total), BF16),
            tile,
            edge,
            edge,
        ),
        in_specs=[VMEM, HBM, HBM, HBM],
        out_specs=(VMEM,) * 9,
        scratch_shapes=[
            pltpu.VMEM(inst_vert.shape, F32),
            pltpu.VMEM((1, inst_err.shape[0]), F32),
            grad_scratch,
            DMA((2 + members,)),
        ],
        compiler_params=PARAMS,
        name="first",
    )(recv, *stay(inst_vert, inst_err.reshape(1, -1), ensemble))

    def sides(part_a, part_b):
        return pl.pallas_call(
            sides_kernel,
            out_shape=(
                shape(count, rows_lat, 8, levels),
                shape(count, 2, 8, levels),
            ),
            in_specs=[VMEM] * 2,
            out_specs=(VMEM,) * 2,
            compiler_params=PARAMS,
            name="sides",
        )(part_a, part_b)

    def halo(fields, edge_a, edge_b):
        lat_b = lax.ppermute(fields, "lat", lat_outer)
        side_a = lax.ppermute(edge_a, "lon", lon_inner)
        side_b = lax.ppermute(edge_b, "lon", lon_outer)
        lat_a = lax.ppermute(fields, "lat", lat_inner)
        cross, folded = sides(side_a, side_b)
        corner_b = lax.ppermute(folded, "lat", lat_outer)
        corner_a = lax.ppermute(cross, "lat", lat_inner)
        smooth, twice = pl.pallas_call(
            smooth_kernel,
            out_shape=(tile, tile),
            in_specs=[VMEM] * 4,
            out_specs=(VMEM,) * 2,
            scratch_shapes=[pltpu.VMEM((HALO, rows_lat, rows_lon + 8, levels), F32)],
            compiler_params=PARAMS,
            name="smooth",
        )(fields, lat_a, lat_b, cross)
        return smooth, twice, corner_a, corner_b


    smooth, twice, corner_a, corner_b = halo(fields, edge_a, edge_b)
    matrix_scratch = pltpu.VMEM(vert_loc.shape, F32)
    image, *outs = pl.pallas_call(
        middle_kernel,
        out_shape=(shape(8, total), tile, edge, edge),
        in_specs=[VMEM] * 10,
        out_specs=(VMEM,) * 4,
        scratch_shapes=[tile_scratch, grad_scratch],
        compiler_params=PARAMS,
        name="middle",
    )(smooth, corner_a, corner_b, feat, ivert, ens, *weights, squares)
    early = pl.pallas_call(
        control_kernel,
        out_shape=tile,
        in_specs=[VMEM] * 3 + [HBM] * 2,
        out_specs=VMEM,
        scratch_shapes=[matrix_scratch, matrix_scratch, DMA((2,))],
        compiler_params=PARAMS,
        name="control",
    )(twice, corner_a, corner_b, *stay(vert_loc, static_vert))
    smooth, twice, corner_a, corner_b = halo(*outs)
    send, late = pl.pallas_call(
        functools.partial(last_kernel, slots),
        out_shape=(shape(owners, LANES), tile),
        in_specs=[VMEM] * 3 + [HBM] * 2 + [VMEM] * 7,
        out_specs=(VMEM,) * 2,
        scratch_shapes=[
            tile_scratch,
            pltpu.VMEM((16, total), F32),
            matrix_scratch,
            matrix_scratch,
            DMA((2,)),
        ],
        compiler_params=PARAMS,
        name="last",
    )(
        smooth,
        corner_a,
        corner_b,
        *stay(vert_loc, static_vert),
        feat,
        ivert,
        ens,
        weights[0],
        squares,
        image,
        twice,
    )
    recv = exchange(send)
    static, member, equivalent = pl.pallas_call(
        final_kernel,
        out_shape=(
            shape(rows_lat, rows_lon, levels),
            shape(members, rows_lat, rows_lon, levels),
            shape(1, rows),
        ),
        in_specs=[VMEM] * 3 + [HBM] * 2,
        out_specs=(HBM,) * 3,
        scratch_shapes=[
            row_scratch,
            row_scratch,
            pltpu.VMEM((1, rows), F32),
            tile_scratch,
            DMA((2,)),
            DMA((count + 1,)),
        ],
        compiler_params=PARAMS,
        name="final",
    )(recv, early, late, *stay(dest, lane))
    return static, member, equivalent.reshape(rows)


def solution(mesh):
    return jax.shard_map(
        body,
        mesh=mesh,
        in_specs=(
            P(None, None, "lat", "lon", None),
            P(),
            P(),
            P(),
            P(),
            P(("lat", "lon"), None),
            P(("lat", "lon")),
            P(("lat", "lon")),
            P(("lat", "lon")),
            P(None, ("lat", "lon")),
            P(("lat", "lon")),
            P(("lat", "lon")),
        ),
        out_specs=(P("lat", "lon", None), P(None, "lat", "lon", None), P(("lat", "lon"))),
        check_vma=False,
    )
```

```python
import functools

import jax
import jax.numpy as jnp
from jax import lax
from jax.experimental import pallas as pl
from jax.experimental.pallas import tpu as pltpu
from jax.sharding import PartitionSpec as P


SMOOTH = 0.15
CENTER = 1.0 - 4.0 * SMOOTH
BETA_STATIC = 0.5
BETA_ENSEMBLE = 0.85
HALO = 4
FOLD = 3
GUESS = 12
LANES = 128
HIGHEST = lax.Precision.HIGHEST
F32 = jnp.float32
BF16 = jnp.bfloat16

HBM = pl.BlockSpec(memory_space=pltpu.HBM)
VMEM = pl.BlockSpec(memory_space=pltpu.VMEM)
SMEM = pl.BlockSpec(memory_space=pltpu.SMEM)
PARAMS = pltpu.CompilerParams(vmem_limit_bytes=32 * 1024 * 1024)
DMA = pltpu.SemaphoreType.DMA


def dot(left, right, dims=((1,), (0,))):
    return lax.dot_general(
        left, right, (dims, ((), ())), precision=HIGHEST, preferred_element_type=F32
    )


def iota(shape, dim):
    return lax.broadcasted_iota(jnp.int32, shape, dim)


def halves(value):
    high = value.astype(BF16)
    return high, (value - high.astype(F32)).astype(BF16)


def thirds(value):
    high = value.astype(BF16)
    rest = value - high.astype(F32)
    middle = rest.astype(BF16)
    return high, middle, (rest - middle.astype(F32)).astype(BF16)


def within(value, length):
    return (value >= 0) & (value < length)


def fetch(sources, targets, sems):
    copies = [
        pltpu.make_async_copy(source, target, sems.at[n])
        for n, (source, target) in enumerate(zip(sources, targets))
    ]
    for copy in copies:
        copy.start()
    return copies


def wait_all(copies):
    for copy in copies:
        copy.wait()


def short_dot(left, right, dims=((1,), (0,))):
    return lax.dot_general(left, right, (dims, ((), ())), preferred_element_type=F32)


def pack_kernel(
    slots, patches,
    dest_hbm, patch_hbm, window_hbm, inst_hbm, hweight_hbm, innov_hbm, count,
    send, lane_hbm,
    dest, patch, window, inst, hweight, innov, feat, lane, table, sems,
):
    wait_all(
        fetch(
            (dest_hbm, patch_hbm, window_hbm, inst_hbm, hweight_hbm, innov_hbm),
            (dest, patch, window, inst, hweight, innov),
            sems,
        )
    )
    owners = send.shape[0]
    rows = dest.shape[1]
    destination = dest[...]
    row, col = iota((rows, rows), 0), iota((rows, rows), 1)
    upright = jnp.sum(
        jnp.where(row == col, destination.astype(F32), 0.0), axis=1, keepdims=True
    ).astype(jnp.int32)
    earlier = (upright == destination) & (row < col)
    ranking = jnp.sum(jnp.where(earlier, 1.0, 0.0), axis=0, keepdims=True).astype(jnp.int32)
    lane[...] = ranking
    lane_copy = pltpu.make_async_copy(lane, lane_hbm, sems.at[6])
    lane_copy.start()
    active = (iota((1, rows), 1) < count[0]).astype(F32)
    feat[0:1] = (window[...] * patches + patch[...]).astype(F32)
    feat[1:2] = inst[...].astype(F32)
    feat[2:6] = hweight[...] * active
    feat[6:7] = innov[...]
    table[...] = jnp.zeros_like(table)
    here = iota((slots, rows), 0) == ranking
    for f in range(7):
        table[f * slots : (f + 1) * slots] = jnp.where(here, feat[f : f + 1], 0.0)
    chosen = (iota((owners, rows), 0) == destination).astype(F32).astype(BF16)
    send[...] = short_dot(
        jnp.concatenate([chosen] * 3, axis=1),
        jnp.concatenate(thirds(table[...]), axis=1),
        ((1,), (1,)),
    )
    lane_copy.wait()


def prepare_kernel(vert_loc, static_vert, squares):
    levels = vert_loc.shape[0]
    squares[...] = jnp.zeros_like(squares)
    for n, (scale, matrix) in enumerate(((BETA_ENSEMBLE, vert_loc), (BETA_STATIC, static_vert))):
        high, low = halves(scale**2 * dot(matrix[...], matrix[...], ((0,), (0,))))
        squares[n, :levels, :levels] = high
        squares[n, :levels, levels:] = low
        squares[n, levels:, :levels] = high


def fill_weights(feat, weights, high_weights, low_weights, windows, rows_lat, rows_lon):
    slots = feat.shape[1]
    cell = feat[0:1].astype(jnp.int32)
    half = iota((rows_lon, slots), 0) >> 1
    odd = (iota((rows_lon, slots), 0) & 1) == 1
    corner = [
        jnp.where(odd, feat[3 + 2 * q : 4 + 2 * q], feat[2 + 2 * q : 3 + 2 * q]) for q in range(2)
    ]
    per_window = rows_lat // 2 * (rows_lon // 2)
    for t in range(windows):
        for a in range(rows_lat):
            first = t * per_window + a // 2 * (rows_lon // 2)
            row = (t * rows_lat + a) * rows_lon
            rows = slice(row, row + rows_lon)
            value = jnp.where(half == cell - first, corner[a % 2], 0.0)
            weights[rows] = value
            high_weights[rows], low_weights[rows] = halves(value)


def adjoint_fields(amount, high_weights, low_weights, ivert, ens, ens_copies, grad, outs):
    fields, edge_a, edge_b = outs
    members, windows, rows_lat, rows_lon, levels = ens.shape
    block = rows_lat * rows_lon
    high, low = halves(ivert[...] * amount)
    both = jnp.concatenate([high, low], axis=0)
    for t in range(windows):
        rows = slice(t * block, (t + 1) * block)
        pair = short_dot(high_weights[rows], both, ((1,), (1,)))
        rest = short_dot(low_weights[rows], high, ((1,), (1,)))
        grad[rows] = pair[:, :levels] + pair[:, levels:] + rest
    even = lax.rem(lax.axis_index("lon"), 2) == 0

    def part(t, a):
        first = (t * rows_lat + a) * rows_lon
        return grad[first : first + rows_lon]

    for k in range(members + 1):
        if k < members and ens_copies:
            ens_copies[k].wait()
        for a in range(rows_lat):
            total = part(0, a) if k == members else ens[k, 0, a].astype(F32) * part(0, a)
            for t in range(1, windows):
                term = part(t, a) if k == members else ens[k, t, a].astype(F32) * part(t, a)
                total = total + term
            fields[k, a] = total
            east = total[rows_lon - HALO :]
            west = total[:HALO]
            edge_a[k, a] = jnp.where(even, east, west)
            edge_b[k, a] = jnp.where(even, west, east)


def first_kernel(
    slots,
    recv, inst_vert_hbm, inst_err_hbm, ens_hbm,
    feat, ivert, ens, weights, high_weights, low_weights, fields, edge_a, edge_b,
    inst_vert, inst_err, grad, sems,
):
    members = ens.shape[0]
    copies = fetch(
        [inst_vert_hbm, inst_err_hbm] + [ens_hbm.at[k] for k in range(members)],
        [inst_vert, inst_err] + [ens.at[k] for k in range(members)],
        sems,
    )
    members, windows, rows_lat, rows_lon, _ = ens.shape
    owners = recv.shape[0]
    total = feat.shape[1]
    source = iota((owners, total), 1) - iota((owners, total), 0) * slots
    mine = within(source, slots).astype(F32).astype(BF16)
    lines = short_dot(
        jnp.concatenate(thirds(recv[...]), axis=0),
        jnp.concatenate([mine] * 3, axis=0),
        ((0,), (0,)),
    )
    same = (iota((LANES, total), 0) & (slots - 1)) == (iota((LANES, total), 1) & (slots - 1))
    lines = jnp.where(same, lines, 0.0)
    for f in range(8):
        feat[f : f + 1] = jnp.sum(lines[f * slots : (f + 1) * slots], axis=0, keepdims=True)
    wait_all(copies[:2])
    instruments = inst_vert.shape[0]
    onehot = (iota((instruments, total), 0) == feat[1:2].astype(jnp.int32)).astype(F32)
    ivert[...] = dot(inst_vert[...].T, onehot)
    inverse = jnp.broadcast_to(1.0 / (inst_err[...] * inst_err[...]), (8, instruments))
    rinv = dot(inverse, onehot)[0:1]
    feat[6:7] = feat[6:7] * rinv
    feat[7:8] = rinv
    fill_weights(feat, weights, high_weights, low_weights, windows, rows_lat, rows_lon)
    outs = (fields, edge_a, edge_b)
    adjoint_fields(feat[6:7], high_weights, low_weights, ivert, ens, copies[2:], grad, outs)


def ring_step(value):
    ring = pltpu.roll(value, 1, 0) + pltpu.roll(value, value.shape[0] - 1, 0)
    return CENTER * value + SMOOTH * ring


def side_terms(cross, corner_a, corner_b, k, order):
    rows_lat = cross.shape[1]
    lat = lax.axis_index("lat")
    odd = lax.rem(lat, 2) == 1
    north = (lat > 0).astype(F32)
    south = (lat < lax.axis_size("lat") - 1).astype(F32)
    line = {i: cross[k, i] for i in range(rows_lat)}
    none = jnp.zeros_like(line[0])
    for r in range(1, HALO):
        tile_a = jnp.where(odd, corner_a[k, rows_lat - r], corner_a[k, r - 1])
        tile_b = corner_b[k, min(r, 2) - 1]
        if r == 3:
            tile_b = pltpu.roll(tile_b, 8 - FOLD, 0)
        line[-r] = jnp.where(odd, tile_a, tile_b)
        line[rows_lat - 1 + r] = jnp.where(odd, tile_b, tile_a)
    powers = [line]
    for m in range(1, order):
        fresh = {}
        for i in range(1 - HALO + m, rows_lat + HALO - 1 - m):
            value = line[i - 1] + line[i + 1]
            fresh[i] = value * north if i < 0 else value * south if i >= rows_lat else value
        line = fresh
        powers.append(line)
    factor = {2: (1.0, 2.0), 4: (1.0, 4.0, 6.0, 4.0)}[order]
    added = []
    for i in range(rows_lat):
        value = None
        for m in range(order):
            fresh = (factor[m] * SMOOTH**m) * powers[m][i]
            fresh = jnp.concatenate([none, fresh, none], axis=0)
            value = ring_step(fresh if value is None else value + fresh)
        added.append((value[:8], value[16:]))
    return added


def with_sides(smooth, cross, corner_a, corner_b, k, order):
    rows_lat, rows_lon = smooth.shape[1:3]
    added = side_terms(cross, corner_a, corner_b, k, order)
    pieces = []
    for i in range(rows_lat):
        last, first = added[i]
        pieces += [
            smooth[k, i, :8] + first,
            smooth[k, i, 8 : rows_lon - 8],
            smooth[k, i, rows_lon - 8 :] + last,
        ]
    return jnp.concatenate(pieces, axis=0)


def sides_kernel(part_a, part_b, cross, folded):
    count, rows_lat, _, levels = part_a.shape
    even = lax.rem(lax.axis_index("lon"), 2) == 0
    odd = lax.rem(lax.axis_index("lat"), 2) == 1
    index = iota((8, levels), 0)
    inner = (index == FOLD - 1) | (index == FOLD)
    for k in range(count):
        rows = []
        for a in range(rows_lat):
            first = jnp.where(even, part_a[k, a], part_b[k, a])
            second = jnp.where(even, part_b[k, a], part_a[k, a])
            rows.append(jnp.concatenate([first, second], axis=0))
            cross[k, a] = rows[a]
        near = [jnp.where(odd, rows[rows_lat - 1 - r], rows[r]) for r in range(HALO - 1)]
        folded[k, 0] = near[0]
        folded[k, 1] = jnp.where(inner, pltpu.roll(near[2], FOLD, 0), near[1])


def row_turner(rows_lat):
    odd = lax.rem(lax.axis_index("lat"), 2)
    return lambda row: rows_lat - 1 - row + odd * (2 * row - rows_lat + 1)


def near_kernel(own, lat_a, smooth, twice, powers):
    count, rows_lat, rows_lon, levels = own.shape
    lat = lax.axis_index("lat")
    odd = lax.rem(lat, 2)
    inside = jnp.where(odd == 1, lat < lax.axis_size("lat") - 1, lat > 0).astype(F32)
    turned = row_turner(rows_lat)
    factor = (4.0, 6.0, 4.0, 1.0)
    powers[:, :, rows_lon:] = jnp.zeros_like(powers[:, :, rows_lon:])
    none = jnp.zeros((8, levels), F32)

    def one(k, carry):
        for c in range(rows_lon // 8):
            cols = slice(8 * c, 8 * c + 8)
            line = {i: own[k, turned(i), cols] for i in range(rows_lat)}
            for r in range(HALO):
                line[-1 - r] = lat_a[k, turned(rows_lat - 1 - r), cols]
            for m in range(1, HALO + 1):
                fresh = {}
                for i in range(m - HALO, rows_lat + min(m, HALO - m)):
                    value = line[i - 1] + line[i + 1] if i + 1 in line else line[i - 1]
                    fresh[i] = value * inside if i >= rows_lat else value
                line = fresh
                for i in range(rows_lat):
                    powers[m - 1, i, cols] = line[i]
        for i in range(rows_lat):
            row = turned(i)
            value = jnp.concatenate([own[k, row], none], axis=0)
            for m in range(1, HALO + 1):
                value = ring_step(value)
                if m == 1:
                    other = ring_step(value + (2.0 * SMOOTH) * powers[0, i])
                    other = other + SMOOTH**2 * powers[1, i]
                    twice[k, row] = other[:rows_lon]
                value = value + (factor[m - 1] * SMOOTH**m) * powers[m - 1, i]
            smooth[k, row] = value[:rows_lon]
        return carry

    lax.fori_loop(0, count, one, 0, unroll=count)


def far_kernel(lat_b, smooth_near, twice_near, smooth, twice, powers):
    count, rows_lat, rows_lon, _ = lat_b.shape
    turned = row_turner(rows_lat)
    factor = (4.0, 6.0, 4.0, 1.0)
    powers[:, :, rows_lon:] = jnp.zeros_like(powers[:, :, rows_lon:])

    def one(k, carry):
        for c in range(rows_lon // 8):
            cols = slice(8 * c, 8 * c + 8)
            line = {rows_lat + r: lat_b[k, turned(r), cols] for r in range(HALO)}
            for m in range(1, HALO + 1):
                fresh = {}
                for i in range(rows_lat - m, rows_lat + HALO - m):
                    terms = [line[n] for n in (i - 1, i + 1) if n in line]
                    fresh[i] = sum(terms[1:], terms[0])
                line = fresh
                for i in range(max(rows_lat - m, 0), rows_lat):
                    powers[m - 1, i, cols] = line[i]
        for i in range(rows_lat):
            row = turned(i)
            value = None
            for m in range(max(rows_lat - i, 1), HALO + 1):
                fresh = (factor[m - 1] * SMOOTH**m) * powers[m - 1, i]
                value = fresh if value is None else ring_step(value) + fresh
            smooth[k, row] = smooth_near[k, row] + value[:rows_lon]
            value = twice_near[k, row]
            if i >= rows_lat - 1:
                value = value + ring_step((2.0 * SMOOTH) * powers[0, i])[:rows_lon]
            if i >= rows_lat - 2:
                value = value + SMOOTH**2 * powers[1, i, :rows_lon]
            twice[k, row] = value
        return carry

    lax.fori_loop(0, count, one, 0, unroll=count)


def observe(smooth, cross, corner_a, corner_b, mixed, squares, ivert, weights, ens):
    members, windows, rows_lat, rows_lon, levels = ens.shape
    block = rows_lat * rows_lon
    shape = (rows_lat, rows_lon, levels)
    for k in range(members + 1):
        square = squares[0] if k < members else squares[1]
        pair = jnp.concatenate(halves(with_sides(smooth, cross, corner_a, corner_b, k, 4)), axis=1)
        product = short_dot(pair, square)
        mixed[k] = (product[:, :levels] + product[:, levels:]).reshape(shape)
    slots = weights.shape[1]
    image = jnp.zeros((8, slots), F32)
    high, low = halves(ivert[...])
    rows_of = jnp.concatenate([high, high, low], axis=0)
    for t in range(windows):
        lines = []
        for a in range(rows_lat):
            total = mixed[members, a]
            for k in range(members):
                total = total + ens[k, t, a].astype(F32) * mixed[k, a]
            lines.append(total)
        increment = jnp.stack(lines).reshape(block, levels)
        high, low = halves(increment)
        seen = short_dot(jnp.concatenate([high, low, high], axis=1), rows_of)
        seen = seen * weights[t * block : (t + 1) * block]
        image = image + jnp.sum(seen.reshape(block // 8, 8, slots), axis=0)
    return jnp.sum(image, axis=0, keepdims=True)


def middle_kernel(
    smooth, cross, corner_a, corner_b, feat, ivert, ens, weights, high_weights, low_weights, squares,
    image, fields, edge_a, edge_b,
    mixed, grad,
):
    seen = observe(smooth, cross, corner_a, corner_b, mixed, squares, ivert, weights, ens)
    scaled = seen * feat[7:8]
    image[...] = jnp.zeros_like(image)
    image[0:1] = seen
    image[1:2] = scaled
    outs = (fields, edge_a, edge_b)
    adjoint_fields(scaled, high_weights, low_weights, ivert, ens, (), grad, outs)


def last_kernel(
    slots,
    smooth, cross, corner_a, corner_b, vert_hbm, static_hbm,
    feat, ivert, ens, weights, squares, image, twice,
    send, late,
    mixed, terms, vert_loc, static_vert, sems,
):
    matrices = fetch((vert_hbm, static_hbm), (vert_loc, static_vert), sems)
    second = observe(smooth, cross, corner_a, corner_b, mixed, squares, ivert, weights, ens)
    wait_all(matrices)
    to_control(twice, cross, corner_a, corner_b, vert_loc, static_vert, late)
    start = feat[6:7]
    rinv = feat[7:8]
    first = image[0:1]
    scaled = image[1:2]
    norm = jnp.sum(start * first, axis=1, keepdims=True)
    curve = norm + jnp.sum(first * scaled, axis=1, keepdims=True)
    guess = jnp.where(curve > 0.0, norm / jnp.where(curve > 0.0, curve, 1.0), 1.0)
    guess = jnp.clip(guess, 0.0, 1.0)
    ahead = start + scaled
    ahead_image = first + second
    rest = start - guess * ahead
    rest_image = first - guess * ahead_image
    products = (
        start * first,
        first * scaled,
        rest * rest_image,
        rest * ahead_image + ahead * rest_image,
        ahead * ahead_image,
        rest_image * rinv * rest_image,
        2.0 * rest_image * rinv * ahead_image,
        ahead_image * rinv * ahead_image,
        2.0 * rest_image * scaled,
        2.0 * ahead_image * scaled,
        start * rest_image + rest * first,
        start * ahead_image + ahead * first,
    )
    terms[...] = jnp.zeros_like(terms)
    for n, value in enumerate(products):
        terms[n : n + 1] = value
    sums = jnp.sum(terms[...], axis=1, keepdims=True)
    owners = send.shape[0]
    per = LANES // slots
    below, across = iota((16, LANES), 0), iota((16, LANES), 1)
    line = jnp.sum(
        jnp.where(across == below + 2 * slots, sums, 0.0), axis=0, keepdims=True
    )
    spot = iota((owners, LANES), 1)
    source = spot - (iota((owners, LANES), 0) & (per - 1)) * slots
    mine = within(source, slots)
    parts = []
    targets = []
    target = iota((LANES, LANES), 0)
    slot = iota((LANES, LANES), 1) & (slots - 1)
    for n, value in enumerate((first, second)):
        groups = [
            jnp.broadcast_to(value[:, g * LANES : (g + 1) * LANES], (per, LANES))
            for g in range(owners // per)
        ]
        parts += halves(jnp.where(mine, jnp.concatenate(groups, axis=0), 0.0))
        targets += [(target == slot + n * slots).astype(F32).astype(BF16)] * 2
    moved = short_dot(
        jnp.concatenate(parts, axis=1), jnp.concatenate(targets, axis=1), ((1,), (1,))
    )
    tail = jnp.where(spot == 2 * slots + GUESS, guess, line)
    send[...] = jnp.where(spot < 2 * slots, moved, tail)


def to_control(smooth, cross, corner_a, corner_b, vert_loc, static_vert, control):
    count, rows_lat, rows_lon, levels = smooth.shape
    blocks = []
    for scale, matrix in ((BETA_ENSEMBLE, vert_loc), (BETA_STATIC, static_vert)):
        high, low = halves(scale * matrix[...])
        upper = jnp.concatenate([high, high], axis=1)
        lower = jnp.concatenate([low, jnp.zeros_like(low)], axis=1)
        blocks.append(jnp.concatenate([upper, lower], axis=0))
    for k in range(count):
        pair = jnp.concatenate(halves(with_sides(smooth, cross, corner_a, corner_b, k, 2)), axis=1)
        product = short_dot(pair, blocks[k // (count - 1)], ((1,), (1,)))
        product = product[:, :levels] + product[:, levels:]
        control[k] = product.reshape(rows_lat, rows_lon, levels)


def control_kernel(
    twice, cross, corner_a, corner_b, vert_hbm, static_hbm, control, vert_loc, static_vert, sems
):
    wait_all(fetch((vert_hbm, static_hbm), (vert_loc, static_vert), sems))
    to_control(twice, cross, corner_a, corner_b, vert_loc, static_vert, control)


def final_kernel(
    recv, early, late, dest_hbm, lane_hbm,
    static_hbm, member_hbm, equivalent_hbm,
    dest, lane, equivalent, result, sems, out_sems,
):
    small = fetch((dest_hbm, lane_hbm), (dest, lane), sems)
    count = early.shape[0]
    owners = recv.shape[0]
    rows = dest.shape[1]
    slots = 2 * rows // owners
    blocks = recv[...]
    sums = jnp.sum(blocks, axis=0, keepdims=True)

    def pick(values, n):
        return values[:, 2 * slots + n : 2 * slots + n + 1]

    norm = pick(sums, 0)
    step = norm / (norm + pick(sums, 1))
    off = pick(blocks, GUESS) - step
    linear = jnp.sum(off * blocks, axis=0, keepdims=True)
    square = jnp.sum(off * off * blocks, axis=0, keepdims=True)
    norm_next = jnp.maximum(pick(sums, 2) + pick(linear, 3) + pick(square, 4), 0.0)
    beta = norm_next / norm
    bend = pick(sums, 5) + pick(linear, 6) + pick(square, 7)
    bend = bend + beta * (pick(sums, 8) + pick(linear, 9)) + beta * beta * pick(sums, 1)
    length = norm_next + beta * (pick(sums, 10) + pick(linear, 11)) + beta * beta * norm
    curve = length + bend
    step_next = jnp.where(curve > 0.0, norm_next / jnp.where(curve > 0.0, curve, 1.0), 0.0)
    step_next = jnp.minimum(step_next, 1.0)
    near = step + step_next * ((1.0 - step) + beta)
    far = -step_next * step
    stores = []
    for k in range(count):
        result[k] = near[None] * early[k] + far[None] * late[k]
        target = member_hbm.at[k] if k < count - 1 else static_hbm
        stores.append(pltpu.make_async_copy(result.at[k], target, out_sems.at[k]))
        stores[k].start()
    wait_all(small)
    chosen = (iota((owners, rows), 0) == dest[...]).astype(F32).astype(BF16)
    table = short_dot(
        jnp.concatenate(halves(blocks), axis=0),
        jnp.concatenate([chosen] * 2, axis=0),
        ((0,), (0,)),
    )
    spot = iota((LANES, rows), 0)
    factor = jnp.where(spot == lane[...], near, 0.0)
    factor = jnp.where(spot == lane[...] + slots, far, factor)
    equivalent[...] = jnp.sum(factor * table, axis=0, keepdims=True)
    stores.append(pltpu.make_async_copy(equivalent, equivalent_hbm, out_sems.at[count]))
    stores[count].start()
    wait_all(stores)


def shape(*dims):
    return jax.ShapeDtypeStruct(dims, F32)


def stay(*values):
    return [pltpu.with_memory_space_constraint(value, pltpu.HBM) for value in values]


def swaps(count, ring):
    inner = [(i, i ^ 1) for i in range(count)]
    outer = []
    for i in range(1, count - 1, 2):
        outer += [(i, i + 1), (i + 1, i)]
    if ring:
        outer += [(count - 1, 0), (0, count - 1)]
    return inner, outer


def body(
    ensemble,
    vert_loc,
    static_vert,
    inst_vert,
    inst_err,
    obs_dest,
    obs_patch,
    obs_window,
    obs_inst,
    obs_hweight,
    innovation,
    obs_count,
):
    members, windows, rows_lat, rows_lon, levels = ensemble.shape
    lat_count = lax.axis_size("lat")
    lon_count = lax.axis_size("lon")
    owners = lat_count * lon_count
    rows = innovation.shape[0]
    slots = 2 * rows // owners
    total = owners * slots
    patches = rows_lat // 2 * (rows_lon // 2)
    count = members + 1
    lat_inner, lat_outer = swaps(lat_count, False)
    lon_inner, lon_outer = swaps(lon_count, True)
    tile = shape(count, rows_lat, rows_lon, levels)
    edge = shape(count, rows_lat, HALO, levels)

    def line(values):
        return values.reshape(1, rows)

    dest = line(obs_dest)
    row_scratch = pltpu.VMEM((1, rows), jnp.int32)
    send, lane = pl.pallas_call(
        functools.partial(pack_kernel, slots, patches),
        out_shape=(shape(owners, LANES), pltpu.HBM((1, rows), jnp.int32)),
        in_specs=[HBM] * 6 + [SMEM],
        out_specs=(VMEM, HBM),
        scratch_shapes=[row_scratch] * 4
        + [
            pltpu.VMEM(obs_hweight.shape, F32),
            pltpu.VMEM((1, rows), F32),
            pltpu.VMEM((8, rows), F32),
            row_scratch,
            pltpu.VMEM((LANES, rows), F32),
            DMA((7,)),
        ],
        compiler_params=PARAMS,
        name="pack",
    )(
        *stay(
            dest,
            line(obs_patch),
            line(obs_window),
            line(obs_inst),
            obs_hweight,
            line(innovation),
        ),
        obs_count,
    )
    squares = pl.pallas_call(
        prepare_kernel,
        out_shape=jax.ShapeDtypeStruct((2, 2 * levels, 2 * levels), BF16),
        compiler_params=PARAMS,
        name="prepare",
    )(vert_loc, static_vert)

    def exchange(blocks):
        return lax.all_to_all(blocks, ("lat", "lon"), split_axis=0, concat_axis=0, tiled=True)

    recv = exchange(send)
    cells = windows * rows_lat * rows_lon
    tile_scratch = pltpu.VMEM(tile.shape, F32)
    grad_scratch = pltpu.VMEM((cells, levels), F32)

    feat, ivert, ens, *weights, fields, edge_a, edge_b = pl.pallas_call(
        functools.partial(first_kernel, slots),
        out_shape=(
            shape(8, total),
            shape(levels, total),
            jax.ShapeDtypeStruct(ensemble.shape, ensemble.dtype),
            shape(cells, total),
            jax.ShapeDtypeStruct((cells, total), BF16),
            jax.ShapeDtypeStruct((cells, total), BF16),
            tile,
            edge,
            edge,
        ),
        in_specs=[VMEM, HBM, HBM, HBM],
        out_specs=(VMEM,) * 9,
        scratch_shapes=[
            pltpu.VMEM(inst_vert.shape, F32),
            pltpu.VMEM((1, inst_err.shape[0]), F32),
            grad_scratch,
            DMA((2 + members,)),
        ],
        compiler_params=PARAMS,
        name="first",
    )(recv, *stay(inst_vert, inst_err.reshape(1, -1), ensemble))

    def sides(part_a, part_b):
        return pl.pallas_call(
            sides_kernel,
            out_shape=(
                shape(count, rows_lat, 8, levels),
                shape(count, 2, 8, levels),
            ),
            in_specs=[VMEM] * 2,
            out_specs=(VMEM,) * 2,
            compiler_params=PARAMS,
            name="sides",
        )(part_a, part_b)

    def halo(fields, edge_a, edge_b):
        lat_b = lax.ppermute(fields, "lat", lat_outer)
        side_a = lax.ppermute(edge_a, "lon", lon_inner)
        side_b = lax.ppermute(edge_b, "lon", lon_outer)
        lat_a = lax.ppermute(fields, "lat", lat_inner)
        cross, folded = sides(side_a, side_b)
        corner_b = lax.ppermute(folded, "lat", lat_outer)
        corner_a = lax.ppermute(cross, "lat", lat_inner)
        powers = pltpu.VMEM((HALO, rows_lat, rows_lon + 8, levels), F32)
        smooth, twice = pl.pallas_call(
            near_kernel,
            out_shape=(tile, tile),
            in_specs=[VMEM] * 2,
            out_specs=(VMEM,) * 2,
            scratch_shapes=[powers],
            compiler_params=PARAMS,
            name="near",
        )(fields, lat_a)
        smooth, twice = pl.pallas_call(
            far_kernel,
            out_shape=(tile, tile),
            in_specs=[VMEM] * 3,
            out_specs=(VMEM,) * 2,
            scratch_shapes=[powers],
            compiler_params=PARAMS,
            name="far",
        )(lat_b, smooth, twice)
        return smooth, twice, cross, corner_a, corner_b


    smooth, twice, cross, corner_a, corner_b = halo(fields, edge_a, edge_b)
    matrix_scratch = pltpu.VMEM(vert_loc.shape, F32)
    image, *outs = pl.pallas_call(
        middle_kernel,
        out_shape=(shape(8, total), tile, edge, edge),
        in_specs=[VMEM] * 11,
        out_specs=(VMEM,) * 4,
        scratch_shapes=[tile_scratch, grad_scratch],
        compiler_params=PARAMS,
        name="middle",
    )(smooth, cross, corner_a, corner_b, feat, ivert, ens, *weights, squares)
    early = pl.pallas_call(
        control_kernel,
        out_shape=tile,
        in_specs=[VMEM] * 4 + [HBM] * 2,
        out_specs=VMEM,
        scratch_shapes=[matrix_scratch, matrix_scratch, DMA((2,))],
        compiler_params=PARAMS,
        name="control",
    )(twice, cross, corner_a, corner_b, *stay(vert_loc, static_vert))
    smooth, twice, cross, corner_a, corner_b = halo(*outs)
    send, late = pl.pallas_call(
        functools.partial(last_kernel, slots),
        out_shape=(shape(owners, LANES), tile),
        in_specs=[VMEM] * 4 + [HBM] * 2 + [VMEM] * 7,
        out_specs=(VMEM,) * 2,
        scratch_shapes=[
            tile_scratch,
            pltpu.VMEM((16, total), F32),
            matrix_scratch,
            matrix_scratch,
            DMA((2,)),
        ],
        compiler_params=PARAMS,
        name="last",
    )(
        smooth,
        cross,
        corner_a,
        corner_b,
        *stay(vert_loc, static_vert),
        feat,
        ivert,
        ens,
        weights[0],
        squares,
        image,
        twice,
    )
    recv = exchange(send)
    static, member, equivalent = pl.pallas_call(
        final_kernel,
        out_shape=(
            shape(rows_lat, rows_lon, levels),
            shape(members, rows_lat, rows_lon, levels),
            shape(1, rows),
        ),
        in_specs=[VMEM] * 3 + [HBM] * 2,
        out_specs=(HBM,) * 3,
        scratch_shapes=[
            row_scratch,
            row_scratch,
            pltpu.VMEM((1, rows), F32),
            tile_scratch,
            DMA((2,)),
            DMA((count + 1,)),
        ],
        compiler_params=PARAMS,
        name="final",
    )(recv, early, late, *stay(dest, lane))
    return static, member, equivalent.reshape(rows)


def solution(mesh):
    return jax.shard_map(
        body,
        mesh=mesh,
        in_specs=(
            P(None, None, "lat", "lon", None),
            P(),
            P(),
            P(),
            P(),
            P(("lat", "lon"), None),
            P(("lat", "lon")),
            P(("lat", "lon")),
            P(("lat", "lon")),
            P(None, ("lat", "lon")),
            P(("lat", "lon")),
            P(("lat", "lon")),
        ),
        out_specs=(P("lat", "lon", None), P(None, "lat", "lon", None), P(("lat", "lon"))),
        check_vma=False,
    )
```

```python
import functools

import jax
import jax.numpy as jnp
from jax import lax
from jax.experimental import pallas as pl
from jax.experimental.pallas import tpu as pltpu
from jax.sharding import PartitionSpec as P


SMOOTH = 0.15
CENTER = 1.0 - 4.0 * SMOOTH
BETA_STATIC = 0.5
BETA_ENSEMBLE = 0.85
HALO = 4
FOLD = 3
GUESS = 12
LANES = 128
HIGHEST = lax.Precision.HIGHEST
F32 = jnp.float32
BF16 = jnp.bfloat16

HBM = pl.BlockSpec(memory_space=pltpu.HBM)
VMEM = pl.BlockSpec(memory_space=pltpu.VMEM)
SMEM = pl.BlockSpec(memory_space=pltpu.SMEM)
PARAMS = pltpu.CompilerParams(vmem_limit_bytes=32 * 1024 * 1024)
DMA = pltpu.SemaphoreType.DMA


def dot(left, right, dims=((1,), (0,))):
    return lax.dot_general(
        left, right, (dims, ((), ())), precision=HIGHEST, preferred_element_type=F32
    )


def iota(shape, dim):
    return lax.broadcasted_iota(jnp.int32, shape, dim)


def halves(value):
    high = value.astype(BF16)
    return high, (value - high.astype(F32)).astype(BF16)


def thirds(value):
    high = value.astype(BF16)
    rest = value - high.astype(F32)
    middle = rest.astype(BF16)
    return high, middle, (rest - middle.astype(F32)).astype(BF16)


def within(value, length):
    return (value >= 0) & (value < length)


def ens_shape(ens):
    head, rest = ens
    return (head.shape[0] + rest.shape[0],) + head.shape[1:]


def member(ens, k):
    head, rest = ens
    return head.at[k] if k < head.shape[0] else rest.at[k - head.shape[0]]


def fetch(sources, targets, sems):
    copies = [
        pltpu.make_async_copy(source, target, sems.at[n])
        for n, (source, target) in enumerate(zip(sources, targets))
    ]
    for copy in copies:
        copy.start()
    return copies


def wait_all(copies):
    for copy in copies:
        copy.wait()


def short_dot(left, right, dims=((1,), (0,))):
    return lax.dot_general(left, right, (dims, ((), ())), preferred_element_type=F32)


def pack_kernel(
    slots, patches,
    dest_hbm, patch_hbm, window_hbm, inst_hbm, hweight_hbm, innov_hbm, count, ens_hbm,
    send, lane_hbm, head,
    dest, patch, window, inst, hweight, innov, feat, lane, table, sems,
):
    copies = fetch(
        (dest_hbm, patch_hbm, window_hbm, inst_hbm, hweight_hbm, innov_hbm),
        (dest, patch, window, inst, hweight, innov),
        sems,
    )
    head_copy = pltpu.make_async_copy(ens_hbm.at[pl.ds(0, head.shape[0])], head, sems.at[7])
    head_copy.start()
    wait_all(copies)
    owners = send.shape[0]
    rows = dest.shape[1]
    destination = dest[...]
    row, col = iota((rows, rows), 0), iota((rows, rows), 1)
    upright = jnp.sum(
        jnp.where(row == col, destination.astype(F32), 0.0), axis=1, keepdims=True
    ).astype(jnp.int32)
    earlier = (upright == destination) & (row < col)
    ranking = jnp.sum(jnp.where(earlier, 1.0, 0.0), axis=0, keepdims=True).astype(jnp.int32)
    lane[...] = ranking
    lane_copy = pltpu.make_async_copy(lane, lane_hbm, sems.at[6])
    lane_copy.start()
    active = (iota((1, rows), 1) < count[0]).astype(F32)
    feat[0:1] = (window[...] * patches + patch[...]).astype(F32)
    feat[1:2] = inst[...].astype(F32)
    feat[2:6] = hweight[...] * active
    feat[6:7] = innov[...]
    table[...] = jnp.zeros_like(table)
    here = iota((slots, rows), 0) == ranking
    for f in range(7):
        table[f * slots : (f + 1) * slots] = jnp.where(here, feat[f : f + 1], 0.0)
    chosen = (iota((owners, rows), 0) == destination).astype(F32).astype(BF16)
    send[...] = short_dot(
        jnp.concatenate([chosen] * 3, axis=1),
        jnp.concatenate(thirds(table[...]), axis=1),
        ((1,), (1,)),
    )
    lane_copy.wait()
    head_copy.wait()


def prepare_kernel(vert_loc, static_vert, squares):
    levels = vert_loc.shape[0]
    squares[...] = jnp.zeros_like(squares)
    for n, (scale, matrix) in enumerate(((BETA_ENSEMBLE, vert_loc), (BETA_STATIC, static_vert))):
        high, low = halves(scale**2 * dot(matrix[...], matrix[...], ((0,), (0,))))
        squares[n, :levels, :levels] = high
        squares[n, :levels, levels:] = low
        squares[n, levels:, :levels] = high


def fill_weights(feat, weights, high_weights, low_weights, windows, rows_lat, rows_lon):
    slots = feat.shape[1]
    cell = feat[0:1].astype(jnp.int32)
    half = iota((rows_lon, slots), 0) >> 1
    odd = (iota((rows_lon, slots), 0) & 1) == 1
    corner = [
        jnp.where(odd, feat[3 + 2 * q : 4 + 2 * q], feat[2 + 2 * q : 3 + 2 * q]) for q in range(2)
    ]
    per_window = rows_lat // 2 * (rows_lon // 2)
    for t in range(windows):
        for a in range(rows_lat):
            first = t * per_window + a // 2 * (rows_lon // 2)
            row = (t * rows_lat + a) * rows_lon
            rows = slice(row, row + rows_lon)
            value = jnp.where(half == cell - first, corner[a % 2], 0.0)
            weights[rows] = value
            high_weights[rows], low_weights[rows] = halves(value)


def adjoint_fields(amount, high_weights, low_weights, ivert, ens, ens_copies, grad, outs):
    fields, edge_a, edge_b = outs
    members, windows, rows_lat, rows_lon, levels = ens_shape(ens)
    block = rows_lat * rows_lon
    high, low = halves(ivert[...] * amount)
    both = jnp.concatenate([high, low], axis=0)
    for t in range(windows):
        rows = slice(t * block, (t + 1) * block)
        pair = short_dot(high_weights[rows], both, ((1,), (1,)))
        rest = short_dot(low_weights[rows], high, ((1,), (1,)))
        grad[rows] = pair[:, :levels] + pair[:, levels:] + rest
    even = lax.rem(lax.axis_index("lon"), 2) == 0

    def part(t, a):
        first = (t * rows_lat + a) * rows_lon
        return grad[first : first + rows_lon]

    for k in range(members + 1):
        if k < members and ens_copies and ens_copies[k] is not None:
            ens_copies[k].wait()
        for a in range(rows_lat):
            total = part(0, a) if k == members else member(ens, k)[0, a].astype(F32) * part(0, a)
            for t in range(1, windows):
                term = part(t, a) if k == members else member(ens, k)[t, a].astype(F32) * part(t, a)
                total = total + term
            fields[k, a] = total
            east = total[rows_lon - HALO :]
            west = total[:HALO]
            edge_a[k, a] = jnp.where(even, east, west)
            edge_b[k, a] = jnp.where(even, west, east)


def first_kernel(
    slots,
    recv, inst_vert_hbm, inst_err_hbm, ens_hbm, head,
    feat, ivert, rest, weights, high_weights, low_weights, fields, edge_a, edge_b,
    inst_vert, inst_err, grad, sems,
):
    ens = (head, rest)
    loaded, missing = head.shape[0], rest.shape[0]
    copies = fetch(
        [inst_vert_hbm, inst_err_hbm] + [ens_hbm.at[loaded + k] for k in range(missing)],
        [inst_vert, inst_err] + [rest.at[k] for k in range(missing)],
        sems,
    )
    _, windows, rows_lat, rows_lon, _ = ens_shape(ens)
    owners = recv.shape[0]
    total = feat.shape[1]
    source = iota((owners, total), 1) - iota((owners, total), 0) * slots
    mine = within(source, slots).astype(F32).astype(BF16)
    lines = short_dot(
        jnp.concatenate(thirds(recv[...]), axis=0),
        jnp.concatenate([mine] * 3, axis=0),
        ((0,), (0,)),
    )
    same = (iota((LANES, total), 0) & (slots - 1)) == (iota((LANES, total), 1) & (slots - 1))
    lines = jnp.where(same, lines, 0.0)
    for f in range(8):
        feat[f : f + 1] = jnp.sum(lines[f * slots : (f + 1) * slots], axis=0, keepdims=True)
    wait_all(copies[:2])
    instruments = inst_vert.shape[0]
    onehot = (iota((instruments, total), 0) == feat[1:2].astype(jnp.int32)).astype(F32)
    ivert[...] = dot(inst_vert[...].T, onehot)
    inverse = jnp.broadcast_to(1.0 / (inst_err[...] * inst_err[...]), (8, instruments))
    rinv = dot(inverse, onehot)[0:1]
    feat[6:7] = feat[6:7] * rinv
    feat[7:8] = rinv
    fill_weights(feat, weights, high_weights, low_weights, windows, rows_lat, rows_lon)
    outs = (fields, edge_a, edge_b)
    copies = [None] * loaded + copies[2:]
    adjoint_fields(feat[6:7], high_weights, low_weights, ivert, ens, copies, grad, outs)


def ring_step(value):
    ring = pltpu.roll(value, 1, 0) + pltpu.roll(value, value.shape[0] - 1, 0)
    return CENTER * value + SMOOTH * ring


def side_terms(cross, corner_a, corner_b, k, order):
    rows_lat = cross.shape[1]
    lat = lax.axis_index("lat")
    odd = lax.rem(lat, 2) == 1
    north = (lat > 0).astype(F32)
    south = (lat < lax.axis_size("lat") - 1).astype(F32)
    line = {i: cross[k, i] for i in range(rows_lat)}
    none = jnp.zeros_like(line[0])
    for r in range(1, HALO):
        tile_a = jnp.where(odd, corner_a[k, rows_lat - r], corner_a[k, r - 1])
        tile_b = corner_b[k, min(r, 2) - 1]
        if r == 3:
            tile_b = pltpu.roll(tile_b, 8 - FOLD, 0)
        line[-r] = jnp.where(odd, tile_a, tile_b)
        line[rows_lat - 1 + r] = jnp.where(odd, tile_b, tile_a)
    powers = [line]
    for m in range(1, order):
        fresh = {}
        for i in range(1 - HALO + m, rows_lat + HALO - 1 - m):
            value = line[i - 1] + line[i + 1]
            fresh[i] = value * north if i < 0 else value * south if i >= rows_lat else value
        line = fresh
        powers.append(line)
    factor = {2: (1.0, 2.0), 4: (1.0, 4.0, 6.0, 4.0)}[order]
    added = []
    for i in range(rows_lat):
        value = None
        for m in range(order):
            fresh = (factor[m] * SMOOTH**m) * powers[m][i]
            fresh = jnp.concatenate([none, fresh, none], axis=0)
            value = ring_step(fresh if value is None else value + fresh)
        added.append((value[:8], value[16:]))
    return added


def with_sides(smooth, cross, corner_a, corner_b, k, order):
    rows_lat, rows_lon = smooth.shape[1:3]
    added = side_terms(cross, corner_a, corner_b, k, order)
    pieces = []
    for i in range(rows_lat):
        last, first = added[i]
        pieces += [
            smooth[k, i, :8] + first,
            smooth[k, i, 8 : rows_lon - 8],
            smooth[k, i, rows_lon - 8 :] + last,
        ]
    return jnp.concatenate(pieces, axis=0)


def sides_kernel(part_a, part_b, cross, folded):
    count, rows_lat, _, levels = part_a.shape
    even = lax.rem(lax.axis_index("lon"), 2) == 0
    odd = lax.rem(lax.axis_index("lat"), 2) == 1
    index = iota((8, levels), 0)
    inner = (index == FOLD - 1) | (index == FOLD)
    for k in range(count):
        rows = []
        for a in range(rows_lat):
            first = jnp.where(even, part_a[k, a], part_b[k, a])
            second = jnp.where(even, part_b[k, a], part_a[k, a])
            rows.append(jnp.concatenate([first, second], axis=0))
            cross[k, a] = rows[a]
        near = [jnp.where(odd, rows[rows_lat - 1 - r], rows[r]) for r in range(HALO - 1)]
        folded[k, 0] = near[0]
        folded[k, 1] = jnp.where(inner, pltpu.roll(near[2], FOLD, 0), near[1])


def row_turner(rows_lat):
    odd = lax.rem(lax.axis_index("lat"), 2)
    return lambda row: rows_lat - 1 - row + odd * (2 * row - rows_lat + 1)


def near_kernel(own, lat_a, smooth, twice, powers):
    count, rows_lat, rows_lon, levels = own.shape
    lat = lax.axis_index("lat")
    odd = lax.rem(lat, 2)
    inside = jnp.where(odd == 1, lat < lax.axis_size("lat") - 1, lat > 0).astype(F32)
    turned = row_turner(rows_lat)
    factor = (4.0, 6.0, 4.0, 1.0)
    powers[:, :, rows_lon:] = jnp.zeros_like(powers[:, :, rows_lon:])
    none = jnp.zeros((8, levels), F32)

    def one(k, carry):
        for c in range(rows_lon // 8):
            cols = slice(8 * c, 8 * c + 8)
            line = {i: own[k, turned(i), cols] for i in range(rows_lat)}
            for r in range(HALO):
                line[-1 - r] = lat_a[k, turned(rows_lat - 1 - r), cols]
            for m in range(1, HALO + 1):
                fresh = {}
                for i in range(m - HALO, rows_lat + min(m, HALO - m)):
                    value = line[i - 1] + line[i + 1] if i + 1 in line else line[i - 1]
                    fresh[i] = value * inside if i >= rows_lat else value
                line = fresh
                for i in range(rows_lat):
                    powers[m - 1, i, cols] = line[i]
        for i in range(rows_lat):
            row = turned(i)
            value = jnp.concatenate([own[k, row], none], axis=0)
            for m in range(1, HALO + 1):
                value = ring_step(value)
                if m == 1:
                    other = ring_step(value + (2.0 * SMOOTH) * powers[0, i])
                    other = other + SMOOTH**2 * powers[1, i]
                    twice[k, row] = other[:rows_lon]
                value = value + (factor[m - 1] * SMOOTH**m) * powers[m - 1, i]
            smooth[k, row] = value[:rows_lon]
        return carry

    lax.fori_loop(0, count, one, 0, unroll=count)


def far_kernel(lat_b, smooth_near, twice_near, smooth, twice, powers):
    count, rows_lat, rows_lon, _ = lat_b.shape
    turned = row_turner(rows_lat)
    factor = (4.0, 6.0, 4.0, 1.0)
    powers[:, :, rows_lon:] = jnp.zeros_like(powers[:, :, rows_lon:])

    def one(k, carry):
        for c in range(rows_lon // 8):
            cols = slice(8 * c, 8 * c + 8)
            line = {rows_lat + r: lat_b[k, turned(r), cols] for r in range(HALO)}
            for m in range(1, HALO + 1):
                fresh = {}
                for i in range(rows_lat - m, rows_lat + HALO - m):
                    terms = [line[n] for n in (i - 1, i + 1) if n in line]
                    fresh[i] = sum(terms[1:], terms[0])
                line = fresh
                for i in range(max(rows_lat - m, 0), rows_lat):
                    powers[m - 1, i, cols] = line[i]
        for i in range(rows_lat):
            row = turned(i)
            value = None
            for m in range(max(rows_lat - i, 1), HALO + 1):
                fresh = (factor[m - 1] * SMOOTH**m) * powers[m - 1, i]
                value = fresh if value is None else ring_step(value) + fresh
            smooth[k, row] = smooth_near[k, row] + value[:rows_lon]
            value = twice_near[k, row]
            if i >= rows_lat - 1:
                value = value + ring_step((2.0 * SMOOTH) * powers[0, i])[:rows_lon]
            if i >= rows_lat - 2:
                value = value + SMOOTH**2 * powers[1, i, :rows_lon]
            twice[k, row] = value
        return carry

    lax.fori_loop(0, count, one, 0, unroll=count)


def observe(smooth, cross, corner_a, corner_b, mixed, squares, ivert, weights, ens):
    members, windows, rows_lat, rows_lon, levels = ens_shape(ens)
    block = rows_lat * rows_lon
    shape = (rows_lat, rows_lon, levels)
    for k in range(members + 1):
        square = squares[0] if k < members else squares[1]
        pair = jnp.concatenate(halves(with_sides(smooth, cross, corner_a, corner_b, k, 4)), axis=1)
        product = short_dot(pair, square)
        mixed[k] = (product[:, :levels] + product[:, levels:]).reshape(shape)
    slots = weights.shape[1]
    image = jnp.zeros((8, slots), F32)
    high, low = halves(ivert[...])
    rows_of = jnp.concatenate([high, high, low], axis=0)
    for t in range(windows):
        lines = []
        for a in range(rows_lat):
            total = mixed[members, a]
            for k in range(members):
                total = total + member(ens, k)[t, a].astype(F32) * mixed[k, a]
            lines.append(total)
        increment = jnp.stack(lines).reshape(block, levels)
        high, low = halves(increment)
        seen = short_dot(jnp.concatenate([high, low, high], axis=1), rows_of)
        seen = seen * weights[t * block : (t + 1) * block]
        image = image + jnp.sum(seen.reshape(block // 8, 8, slots), axis=0)
    return jnp.sum(image, axis=0, keepdims=True)


def middle_kernel(
    smooth, cross, corner_a, corner_b, feat, ivert, head, rest, weights, high_weights, low_weights, squares,
    image, fields, edge_a, edge_b,
    mixed, grad,
):
    ens = (head, rest)
    seen = observe(smooth, cross, corner_a, corner_b, mixed, squares, ivert, weights, ens)
    scaled = seen * feat[7:8]
    image[...] = jnp.zeros_like(image)
    image[0:1] = seen
    image[1:2] = scaled
    outs = (fields, edge_a, edge_b)
    adjoint_fields(scaled, high_weights, low_weights, ivert, ens, (), grad, outs)


def last_kernel(
    slots,
    smooth, cross, corner_a, corner_b, vert_hbm, static_hbm,
    feat, ivert, head, rest, weights, squares, image, twice,
    send, late,
    mixed, terms, vert_loc, static_vert, sems,
):
    matrices = fetch((vert_hbm, static_hbm), (vert_loc, static_vert), sems)
    ens = (head, rest)
    second = observe(smooth, cross, corner_a, corner_b, mixed, squares, ivert, weights, ens)
    wait_all(matrices)
    to_control(twice, cross, corner_a, corner_b, vert_loc, static_vert, late)
    start = feat[6:7]
    rinv = feat[7:8]
    first = image[0:1]
    scaled = image[1:2]
    norm = jnp.sum(start * first, axis=1, keepdims=True)
    curve = norm + jnp.sum(first * scaled, axis=1, keepdims=True)
    guess = jnp.where(curve > 0.0, norm / jnp.where(curve > 0.0, curve, 1.0), 1.0)
    guess = jnp.clip(guess, 0.0, 1.0)
    ahead = start + scaled
    ahead_image = first + second
    rest = start - guess * ahead
    rest_image = first - guess * ahead_image
    products = (
        start * first,
        first * scaled,
        rest * rest_image,
        rest * ahead_image + ahead * rest_image,
        ahead * ahead_image,
        rest_image * rinv * rest_image,
        2.0 * rest_image * rinv * ahead_image,
        ahead_image * rinv * ahead_image,
        2.0 * rest_image * scaled,
        2.0 * ahead_image * scaled,
        start * rest_image + rest * first,
        start * ahead_image + ahead * first,
    )
    terms[...] = jnp.zeros_like(terms)
    for n, value in enumerate(products):
        terms[n : n + 1] = value
    sums = jnp.sum(terms[...], axis=1, keepdims=True)
    owners = send.shape[0]
    per = LANES // slots
    below, across = iota((16, LANES), 0), iota((16, LANES), 1)
    line = jnp.sum(
        jnp.where(across == below + 2 * slots, sums, 0.0), axis=0, keepdims=True
    )
    spot = iota((owners, LANES), 1)
    source = spot - (iota((owners, LANES), 0) & (per - 1)) * slots
    mine = within(source, slots)
    parts = []
    targets = []
    target = iota((LANES, LANES), 0)
    slot = iota((LANES, LANES), 1) & (slots - 1)
    for n, value in enumerate((first, second)):
        groups = [
            jnp.broadcast_to(value[:, g * LANES : (g + 1) * LANES], (per, LANES))
            for g in range(owners // per)
        ]
        parts += halves(jnp.where(mine, jnp.concatenate(groups, axis=0), 0.0))
        targets += [(target == slot + n * slots).astype(F32).astype(BF16)] * 2
    moved = short_dot(
        jnp.concatenate(parts, axis=1), jnp.concatenate(targets, axis=1), ((1,), (1,))
    )
    tail = jnp.where(spot == 2 * slots + GUESS, guess, line)
    send[...] = jnp.where(spot < 2 * slots, moved, tail)


def to_control(smooth, cross, corner_a, corner_b, vert_loc, static_vert, control):
    count, rows_lat, rows_lon, levels = smooth.shape
    blocks = []
    for scale, matrix in ((BETA_ENSEMBLE, vert_loc), (BETA_STATIC, static_vert)):
        high, low = halves(scale * matrix[...])
        upper = jnp.concatenate([high, high], axis=1)
        lower = jnp.concatenate([low, jnp.zeros_like(low)], axis=1)
        blocks.append(jnp.concatenate([upper, lower], axis=0))
    for k in range(count):
        pair = jnp.concatenate(halves(with_sides(smooth, cross, corner_a, corner_b, k, 2)), axis=1)
        product = short_dot(pair, blocks[k // (count - 1)], ((1,), (1,)))
        product = product[:, :levels] + product[:, levels:]
        control[k] = product.reshape(rows_lat, rows_lon, levels)


def control_kernel(
    twice, cross, corner_a, corner_b, vert_hbm, static_hbm, control, vert_loc, static_vert, sems
):
    wait_all(fetch((vert_hbm, static_hbm), (vert_loc, static_vert), sems))
    to_control(twice, cross, corner_a, corner_b, vert_loc, static_vert, control)


def final_kernel(
    recv, early, late, dest_hbm, lane_hbm,
    static_hbm, member_hbm, equivalent_hbm,
    dest, lane, equivalent, result, sems, out_sems,
):
    small = fetch((dest_hbm, lane_hbm), (dest, lane), sems)
    count = early.shape[0]
    owners = recv.shape[0]
    rows = dest.shape[1]
    slots = 2 * rows // owners
    blocks = recv[...]
    sums = jnp.sum(blocks, axis=0, keepdims=True)

    def pick(values, n):
        return values[:, 2 * slots + n : 2 * slots + n + 1]

    norm = pick(sums, 0)
    step = norm / (norm + pick(sums, 1))
    off = pick(blocks, GUESS) - step
    linear = jnp.sum(off * blocks, axis=0, keepdims=True)
    square = jnp.sum(off * off * blocks, axis=0, keepdims=True)
    norm_next = jnp.maximum(pick(sums, 2) + pick(linear, 3) + pick(square, 4), 0.0)
    beta = norm_next / norm
    bend = pick(sums, 5) + pick(linear, 6) + pick(square, 7)
    bend = bend + beta * (pick(sums, 8) + pick(linear, 9)) + beta * beta * pick(sums, 1)
    length = norm_next + beta * (pick(sums, 10) + pick(linear, 11)) + beta * beta * norm
    curve = length + bend
    step_next = jnp.where(curve > 0.0, norm_next / jnp.where(curve > 0.0, curve, 1.0), 0.0)
    step_next = jnp.minimum(step_next, 1.0)
    near = step + step_next * ((1.0 - step) + beta)
    far = -step_next * step
    stores = []
    near, far = jnp.sum(near), jnp.sum(far)
    for k in range(count):
        result[k] = near * early[k] + far * late[k]
        target = member_hbm.at[k] if k < count - 1 else static_hbm
        stores.append(pltpu.make_async_copy(result.at[k], target, out_sems.at[k]))
        stores[k].start()
    wait_all(small)
    chosen = (iota((owners, rows), 0) == dest[...]).astype(F32).astype(BF16)
    table = short_dot(
        jnp.concatenate(halves(blocks), axis=0),
        jnp.concatenate([chosen] * 2, axis=0),
        ((0,), (0,)),
    )
    spot = iota((LANES, rows), 0)
    factor = jnp.where(spot == lane[...], near, 0.0)
    factor = jnp.where(spot == lane[...] + slots, far, factor)
    equivalent[...] = jnp.sum(factor * table, axis=0, keepdims=True)
    stores.append(pltpu.make_async_copy(equivalent, equivalent_hbm, out_sems.at[count]))
    stores[count].start()
    wait_all(stores)


def shape(*dims):
    return jax.ShapeDtypeStruct(dims, F32)


def stay(*values):
    return [pltpu.with_memory_space_constraint(value, pltpu.HBM) for value in values]


def swaps(count, ring):
    inner = [(i, i ^ 1) for i in range(count)]
    outer = []
    for i in range(1, count - 1, 2):
        outer += [(i, i + 1), (i + 1, i)]
    if ring:
        outer += [(count - 1, 0), (0, count - 1)]
    return inner, outer


def body(
    ensemble,
    vert_loc,
    static_vert,
    inst_vert,
    inst_err,
    obs_dest,
    obs_patch,
    obs_window,
    obs_inst,
    obs_hweight,
    innovation,
    obs_count,
):
    members, windows, rows_lat, rows_lon, levels = ensemble.shape
    lat_count = lax.axis_size("lat")
    lon_count = lax.axis_size("lon")
    owners = lat_count * lon_count
    rows = innovation.shape[0]
    slots = 2 * rows // owners
    total = owners * slots
    patches = rows_lat // 2 * (rows_lon // 2)
    count = members + 1
    lat_inner, lat_outer = swaps(lat_count, False)
    lon_inner, lon_outer = swaps(lon_count, True)
    tile = shape(count, rows_lat, rows_lon, levels)
    edge = shape(count, rows_lat, HALO, levels)

    def line(values):
        return values.reshape(1, rows)

    dest = line(obs_dest)
    row_scratch = pltpu.VMEM((1, rows), jnp.int32)
    early_members = members // 2
    send, lane, head = pl.pallas_call(
        functools.partial(pack_kernel, slots, patches),
        out_shape=(
            shape(owners, LANES),
            pltpu.HBM((1, rows), jnp.int32),
            jax.ShapeDtypeStruct((early_members,) + ensemble.shape[1:], ensemble.dtype),
        ),
        in_specs=[HBM] * 6 + [SMEM, HBM],
        out_specs=(VMEM, HBM, VMEM),
        scratch_shapes=[row_scratch] * 4
        + [
            pltpu.VMEM(obs_hweight.shape, F32),
            pltpu.VMEM((1, rows), F32),
            pltpu.VMEM((8, rows), F32),
            row_scratch,
            pltpu.VMEM((LANES, rows), F32),
            DMA((8,)),
        ],
        compiler_params=PARAMS,
        name="pack",
    )(
        *stay(
            dest,
            line(obs_patch),
            line(obs_window),
            line(obs_inst),
            obs_hweight,
            line(innovation),
        ),
        obs_count,
        *stay(ensemble),
    )
    squares = pl.pallas_call(
        prepare_kernel,
        out_shape=jax.ShapeDtypeStruct((2, 2 * levels, 2 * levels), BF16),
        compiler_params=PARAMS,
        name="prepare",
    )(vert_loc, static_vert)

    def exchange(blocks):
        return lax.all_to_all(blocks, ("lat", "lon"), split_axis=0, concat_axis=0, tiled=True)

    recv = exchange(send)
    cells = windows * rows_lat * rows_lon
    tile_scratch = pltpu.VMEM(tile.shape, F32)
    grad_scratch = pltpu.VMEM((cells, levels), F32)

    feat, ivert, rest, *weights, fields, edge_a, edge_b = pl.pallas_call(
        functools.partial(first_kernel, slots),
        out_shape=(
            shape(8, total),
            shape(levels, total),
            jax.ShapeDtypeStruct((members - early_members,) + ensemble.shape[1:], ensemble.dtype),
            shape(cells, total),
            jax.ShapeDtypeStruct((cells, total), BF16),
            jax.ShapeDtypeStruct((cells, total), BF16),
            tile,
            edge,
            edge,
        ),
        in_specs=[VMEM, HBM, HBM, HBM, VMEM],
        out_specs=(VMEM,) * 9,
        scratch_shapes=[
            pltpu.VMEM(inst_vert.shape, F32),
            pltpu.VMEM((1, inst_err.shape[0]), F32),
            grad_scratch,
            DMA((2 + members - early_members,)),
        ],
        compiler_params=PARAMS,
        name="first",
    )(recv, *stay(inst_vert, inst_err.reshape(1, -1), ensemble), head)

    def sides(part_a, part_b):
        return pl.pallas_call(
            sides_kernel,
            out_shape=(
                shape(count, rows_lat, 8, levels),
                shape(count, 2, 8, levels),
            ),
            in_specs=[VMEM] * 2,
            out_specs=(VMEM,) * 2,
            compiler_params=PARAMS,
            name="sides",
        )(part_a, part_b)

    def halo(fields, edge_a, edge_b):
        lat_b = lax.ppermute(fields, "lat", lat_outer)
        side_a = lax.ppermute(edge_a, "lon", lon_inner)
        side_b = lax.ppermute(edge_b, "lon", lon_outer)
        lat_a = lax.ppermute(fields, "lat", lat_inner)
        cross, folded = sides(side_a, side_b)
        corner_b = lax.ppermute(folded, "lat", lat_outer)
        corner_a = lax.ppermute(cross, "lat", lat_inner)
        powers = pltpu.VMEM((HALO, rows_lat, rows_lon + 8, levels), F32)
        smooth, twice = pl.pallas_call(
            near_kernel,
            out_shape=(tile, tile),
            in_specs=[VMEM] * 2,
            out_specs=(VMEM,) * 2,
            scratch_shapes=[powers],
            compiler_params=PARAMS,
            name="near",
        )(fields, lat_a)
        smooth, twice = pl.pallas_call(
            far_kernel,
            out_shape=(tile, tile),
            in_specs=[VMEM] * 3,
            out_specs=(VMEM,) * 2,
            scratch_shapes=[powers],
            compiler_params=PARAMS,
            name="far",
        )(lat_b, smooth, twice)
        return smooth, twice, cross, corner_a, corner_b


    smooth, twice, cross, corner_a, corner_b = halo(fields, edge_a, edge_b)
    matrix_scratch = pltpu.VMEM(vert_loc.shape, F32)
    image, *outs = pl.pallas_call(
        middle_kernel,
        out_shape=(shape(8, total), tile, edge, edge),
        in_specs=[VMEM] * 12,
        out_specs=(VMEM,) * 4,
        scratch_shapes=[tile_scratch, grad_scratch],
        compiler_params=PARAMS,
        name="middle",
    )(smooth, cross, corner_a, corner_b, feat, ivert, head, rest, *weights, squares)
    early = pl.pallas_call(
        control_kernel,
        out_shape=tile,
        in_specs=[VMEM] * 4 + [HBM] * 2,
        out_specs=VMEM,
        scratch_shapes=[matrix_scratch, matrix_scratch, DMA((2,))],
        compiler_params=PARAMS,
        name="control",
    )(twice, cross, corner_a, corner_b, *stay(vert_loc, static_vert))
    smooth, twice, cross, corner_a, corner_b = halo(*outs)
    send, late = pl.pallas_call(
        functools.partial(last_kernel, slots),
        out_shape=(shape(owners, LANES), tile),
        in_specs=[VMEM] * 4 + [HBM] * 2 + [VMEM] * 8,
        out_specs=(VMEM,) * 2,
        scratch_shapes=[
            tile_scratch,
            pltpu.VMEM((16, total), F32),
            matrix_scratch,
            matrix_scratch,
            DMA((2,)),
        ],
        compiler_params=PARAMS,
        name="last",
    )(
        smooth,
        cross,
        corner_a,
        corner_b,
        *stay(vert_loc, static_vert),
        feat,
        ivert,
        head,
        rest,
        weights[0],
        squares,
        image,
        twice,
    )
    recv = exchange(send)
    static, member, equivalent = pl.pallas_call(
        final_kernel,
        out_shape=(
            shape(rows_lat, rows_lon, levels),
            shape(members, rows_lat, rows_lon, levels),
            shape(1, rows),
        ),
        in_specs=[VMEM] * 3 + [HBM] * 2,
        out_specs=(HBM,) * 3,
        scratch_shapes=[
            row_scratch,
            row_scratch,
            pltpu.VMEM((1, rows), F32),
            tile_scratch,
            DMA((2,)),
            DMA((count + 1,)),
        ],
        compiler_params=PARAMS,
        name="final",
    )(recv, early, late, *stay(dest, lane))
    return static, member, equivalent.reshape(rows)


def solution(mesh):
    return jax.shard_map(
        body,
        mesh=mesh,
        in_specs=(
            P(None, None, "lat", "lon", None),
            P(),
            P(),
            P(),
            P(),
            P(("lat", "lon"), None),
            P(("lat", "lon")),
            P(("lat", "lon")),
            P(("lat", "lon")),
            P(None, ("lat", "lon")),
            P(("lat", "lon")),
            P(("lat", "lon")),
        ),
        out_specs=(P("lat", "lon", None), P(None, "lat", "lon", None), P(("lat", "lon"))),
        check_vma=False,
    )
```

```python
import functools

import jax
import jax.numpy as jnp
from jax import lax
from jax.experimental import pallas as pl
from jax.experimental.pallas import tpu as pltpu
from jax.sharding import PartitionSpec as P


SMOOTH = 0.15
CENTER = 1.0 - 4.0 * SMOOTH
BETA_STATIC = 0.5
BETA_ENSEMBLE = 0.85
HALO = 4
FOLD = 3
GUESS = 12
LANES = 128
HIGHEST = lax.Precision.HIGHEST
F32 = jnp.float32
BF16 = jnp.bfloat16

HBM = pl.BlockSpec(memory_space=pltpu.HBM)
VMEM = pl.BlockSpec(memory_space=pltpu.VMEM)
SMEM = pl.BlockSpec(memory_space=pltpu.SMEM)
PARAMS = pltpu.CompilerParams(vmem_limit_bytes=32 * 1024 * 1024)
DMA = pltpu.SemaphoreType.DMA


def dot(left, right, dims=((1,), (0,))):
    return lax.dot_general(
        left, right, (dims, ((), ())), precision=HIGHEST, preferred_element_type=F32
    )


def iota(shape, dim):
    return lax.broadcasted_iota(jnp.int32, shape, dim)


def halves(value):
    high = value.astype(BF16)
    return high, (value - high.astype(F32)).astype(BF16)


def thirds(value):
    high = value.astype(BF16)
    rest = value - high.astype(F32)
    middle = rest.astype(BF16)
    return high, middle, (rest - middle.astype(F32)).astype(BF16)


def within(value, length):
    return (value >= 0) & (value < length)


def ens_shape(ens):
    head, rest = ens
    return (head.shape[0] + rest.shape[0],) + head.shape[1:]


def member(ens, k):
    head, rest = ens
    return head.at[k] if k < head.shape[0] else rest.at[k - head.shape[0]]


def fetch(sources, targets, sems):
    copies = [
        pltpu.make_async_copy(source, target, sems.at[n])
        for n, (source, target) in enumerate(zip(sources, targets))
    ]
    for copy in copies:
        copy.start()
    return copies


def wait_all(copies):
    for copy in copies:
        copy.wait()


def short_dot(left, right, dims=((1,), (0,))):
    return lax.dot_general(left, right, (dims, ((), ())), preferred_element_type=F32)


def pack_kernel(
    slots, patches,
    dest_hbm, patch_hbm, window_hbm, inst_hbm, hweight_hbm, innov_hbm, count, ens_hbm,
    send, lane_hbm, head,
    dest, patch, window, inst, hweight, innov, feat, lane, table, sems,
):
    copies = fetch(
        (dest_hbm, patch_hbm, window_hbm, inst_hbm, hweight_hbm, innov_hbm),
        (dest, patch, window, inst, hweight, innov),
        sems,
    )
    head_copy = pltpu.make_async_copy(ens_hbm.at[pl.ds(0, head.shape[0])], head, sems.at[7])
    head_copy.start()
    wait_all(copies)
    owners = send.shape[0]
    rows = dest.shape[1]
    destination = dest[...]
    row, col = iota((rows, rows), 0), iota((rows, rows), 1)
    upright = jnp.sum(
        jnp.where(row == col, destination.astype(F32), 0.0), axis=1, keepdims=True
    ).astype(jnp.int32)
    earlier = (upright == destination) & (row < col)
    ranking = jnp.sum(jnp.where(earlier, 1.0, 0.0), axis=0, keepdims=True).astype(jnp.int32)
    lane[...] = ranking
    lane_copy = pltpu.make_async_copy(lane, lane_hbm, sems.at[6])
    lane_copy.start()
    active = (iota((1, rows), 1) < count[0]).astype(F32)
    feat[0:1] = (window[...] * patches + patch[...]).astype(F32)
    feat[1:2] = inst[...].astype(F32)
    feat[2:6] = hweight[...] * active
    feat[6:7] = innov[...]
    table[...] = jnp.zeros_like(table)
    here = iota((slots, rows), 0) == ranking
    for f in range(7):
        table[f * slots : (f + 1) * slots] = jnp.where(here, feat[f : f + 1], 0.0)
    chosen = (iota((owners, rows), 0) == destination).astype(F32).astype(BF16)
    send[...] = short_dot(
        jnp.concatenate([chosen] * 3, axis=1),
        jnp.concatenate(thirds(table[...]), axis=1),
        ((1,), (1,)),
    )
    lane_copy.wait()
    head_copy.wait()


def prepare_kernel(vert_loc, static_vert, squares):
    levels = vert_loc.shape[0]
    squares[...] = jnp.zeros_like(squares)
    for n, (scale, matrix) in enumerate(((BETA_ENSEMBLE, vert_loc), (BETA_STATIC, static_vert))):
        high, low = halves(scale**2 * dot(matrix[...], matrix[...], ((0,), (0,))))
        squares[n, :levels, :levels] = high
        squares[n, :levels, levels:] = low
        squares[n, levels:, :levels] = high


def fill_weights(feat, weights, high_weights, low_weights, windows, rows_lat, rows_lon):
    slots = feat.shape[1]
    cell = feat[0:1].astype(jnp.int32)
    half = iota((rows_lon, slots), 0) >> 1
    odd = (iota((rows_lon, slots), 0) & 1) == 1
    corner = [
        jnp.where(odd, feat[3 + 2 * q : 4 + 2 * q], feat[2 + 2 * q : 3 + 2 * q]) for q in range(2)
    ]
    per_window = rows_lat // 2 * (rows_lon // 2)
    for t in range(windows):
        for a in range(rows_lat):
            first = t * per_window + a // 2 * (rows_lon // 2)
            row = (t * rows_lat + a) * rows_lon
            rows = slice(row, row + rows_lon)
            value = jnp.where(half == cell - first, corner[a % 2], 0.0)
            weights[rows] = value
            high_weights[rows], low_weights[rows] = halves(value)


def adjoint_fields(amount, high_weights, low_weights, ivert, ens, ens_copies, grad, outs):
    fields, edge_a, edge_b = outs
    members, windows, rows_lat, rows_lon, levels = ens_shape(ens)
    block = rows_lat * rows_lon
    high, low = halves(ivert[...] * amount)
    both = jnp.concatenate([high, low], axis=0)
    for t in range(windows):
        rows = slice(t * block, (t + 1) * block)
        pair = short_dot(high_weights[rows], both, ((1,), (1,)))
        rest = short_dot(low_weights[rows], high, ((1,), (1,)))
        grad[rows] = pair[:, :levels] + pair[:, levels:] + rest
    even = lax.rem(lax.axis_index("lon"), 2) == 0

    def part(t, a):
        first = (t * rows_lat + a) * rows_lon
        return grad[first : first + rows_lon]

    for k in range(members + 1):
        if k < members and ens_copies and ens_copies[k] is not None:
            ens_copies[k].wait()
        for a in range(rows_lat):
            total = part(0, a) if k == members else member(ens, k)[0, a].astype(F32) * part(0, a)
            for t in range(1, windows):
                term = part(t, a) if k == members else member(ens, k)[t, a].astype(F32) * part(t, a)
                total = total + term
            fields[k, a] = total
            east = total[rows_lon - HALO :]
            west = total[:HALO]
            edge_a[k, a] = jnp.where(even, east, west)
            edge_b[k, a] = jnp.where(even, west, east)


def first_kernel(
    slots,
    recv, inst_vert_hbm, inst_err_hbm, ens_hbm, head,
    feat, ivert, rest, weights, high_weights, low_weights, fields, edge_a, edge_b,
    inst_vert, inst_err, grad, sems,
):
    ens = (head, rest)
    loaded, missing = head.shape[0], rest.shape[0]
    copies = fetch(
        [inst_vert_hbm, inst_err_hbm] + [ens_hbm.at[loaded + k] for k in range(missing)],
        [inst_vert, inst_err] + [rest.at[k] for k in range(missing)],
        sems,
    )
    _, windows, rows_lat, rows_lon, _ = ens_shape(ens)
    owners = recv.shape[0]
    total = feat.shape[1]
    source = iota((owners, total), 1) - iota((owners, total), 0) * slots
    mine = within(source, slots).astype(F32).astype(BF16)
    lines = short_dot(
        jnp.concatenate(thirds(recv[...]), axis=0),
        jnp.concatenate([mine] * 3, axis=0),
        ((0,), (0,)),
    )
    same = (iota((LANES, total), 0) & (slots - 1)) == (iota((LANES, total), 1) & (slots - 1))
    lines = jnp.where(same, lines, 0.0)
    for f in range(8):
        feat[f : f + 1] = jnp.sum(lines[f * slots : (f + 1) * slots], axis=0, keepdims=True)
    wait_all(copies[:2])
    instruments = inst_vert.shape[0]
    onehot = (iota((instruments, total), 0) == feat[1:2].astype(jnp.int32)).astype(F32)
    onehot = jnp.concatenate([onehot.astype(BF16)] * 3, axis=0)
    ivert[...] = short_dot(jnp.concatenate(thirds(inst_vert[...].T), axis=1), onehot)
    inverse = jnp.broadcast_to(1.0 / (inst_err[...] * inst_err[...]), (8, instruments))
    rinv = short_dot(jnp.concatenate(thirds(inverse), axis=1), onehot)[0:1]
    feat[6:7] = feat[6:7] * rinv
    feat[7:8] = rinv
    fill_weights(feat, weights, high_weights, low_weights, windows, rows_lat, rows_lon)
    outs = (fields, edge_a, edge_b)
    copies = [None] * loaded + copies[2:]
    adjoint_fields(feat[6:7], high_weights, low_weights, ivert, ens, copies, grad, outs)


def ring_step(value):
    ring = pltpu.roll(value, 1, 0) + pltpu.roll(value, value.shape[0] - 1, 0)
    return CENTER * value + SMOOTH * ring


def side_terms(cross, corner_a, corner_b, k, order):
    rows_lat = cross.shape[1]
    lat = lax.axis_index("lat")
    odd = lax.rem(lat, 2) == 1
    north = (lat > 0).astype(F32)
    south = (lat < lax.axis_size("lat") - 1).astype(F32)
    line = {i: cross[k, i] for i in range(rows_lat)}
    none = jnp.zeros_like(line[0])
    for r in range(1, HALO):
        tile_a = jnp.where(odd, corner_a[k, rows_lat - r], corner_a[k, r - 1])
        tile_b = corner_b[k, min(r, 2) - 1]
        if r == 3:
            tile_b = pltpu.roll(tile_b, 8 - FOLD, 0)
        line[-r] = jnp.where(odd, tile_a, tile_b)
        line[rows_lat - 1 + r] = jnp.where(odd, tile_b, tile_a)
    powers = [line]
    for m in range(1, order):
        fresh = {}
        for i in range(1 - HALO + m, rows_lat + HALO - 1 - m):
            value = line[i - 1] + line[i + 1]
            fresh[i] = value * north if i < 0 else value * south if i >= rows_lat else value
        line = fresh
        powers.append(line)
    factor = {2: (1.0, 2.0), 4: (1.0, 4.0, 6.0, 4.0)}[order]
    added = []
    for i in range(rows_lat):
        value = None
        for m in range(order):
            fresh = (factor[m] * SMOOTH**m) * powers[m][i]
            fresh = jnp.concatenate([none, fresh, none], axis=0)
            value = ring_step(fresh if value is None else value + fresh)
        added.append((value[:8], value[16:]))
    return added


def with_sides(smooth, cross, corner_a, corner_b, k, order):
    rows_lat, rows_lon = smooth.shape[1:3]
    added = side_terms(cross, corner_a, corner_b, k, order)
    pieces = []
    for i in range(rows_lat):
        last, first = added[i]
        pieces += [
            smooth[k, i, :8] + first,
            smooth[k, i, 8 : rows_lon - 8],
            smooth[k, i, rows_lon - 8 :] + last,
        ]
    return jnp.concatenate(pieces, axis=0)


def sides_kernel(part_a, part_b, cross, folded):
    count, rows_lat, _, levels = part_a.shape
    even = lax.rem(lax.axis_index("lon"), 2) == 0
    odd = lax.rem(lax.axis_index("lat"), 2) == 1
    index = iota((8, levels), 0)
    inner = (index == FOLD - 1) | (index == FOLD)
    for k in range(count):
        rows = []
        for a in range(rows_lat):
            first = jnp.where(even, part_a[k, a], part_b[k, a])
            second = jnp.where(even, part_b[k, a], part_a[k, a])
            rows.append(jnp.concatenate([first, second], axis=0))
            cross[k, a] = rows[a]
        near = [jnp.where(odd, rows[rows_lat - 1 - r], rows[r]) for r in range(HALO - 1)]
        folded[k, 0] = near[0]
        folded[k, 1] = jnp.where(inner, pltpu.roll(near[2], FOLD, 0), near[1])


def row_turner(rows_lat):
    odd = lax.rem(lax.axis_index("lat"), 2)
    return lambda row: rows_lat - 1 - row + odd * (2 * row - rows_lat + 1)


def near_kernel(own, lat_a, smooth, twice, powers):
    count, rows_lat, rows_lon, levels = own.shape
    lat = lax.axis_index("lat")
    odd = lax.rem(lat, 2)
    inside = jnp.where(odd == 1, lat < lax.axis_size("lat") - 1, lat > 0).astype(F32)
    turned = row_turner(rows_lat)
    factor = (4.0, 6.0, 4.0, 1.0)
    powers[:, :, rows_lon:] = jnp.zeros_like(powers[:, :, rows_lon:])
    none = jnp.zeros((8, levels), F32)

    def one(k, carry):
        for c in range(rows_lon // 8):
            cols = slice(8 * c, 8 * c + 8)
            line = {i: own[k, turned(i), cols] for i in range(rows_lat)}
            for r in range(HALO):
                line[-1 - r] = lat_a[k, turned(rows_lat - 1 - r), cols]
            for m in range(1, HALO + 1):
                fresh = {}
                for i in range(m - HALO, rows_lat + min(m, HALO - m)):
                    value = line[i - 1] + line[i + 1] if i + 1 in line else line[i - 1]
                    fresh[i] = value * inside if i >= rows_lat else value
                line = fresh
                for i in range(rows_lat):
                    powers[m - 1, i, cols] = line[i]
        for i in range(rows_lat):
            row = turned(i)
            value = jnp.concatenate([own[k, row], none], axis=0)
            for m in range(1, HALO + 1):
                value = ring_step(value)
                if m == 1:
                    other = ring_step(value + (2.0 * SMOOTH) * powers[0, i])
                    other = other + SMOOTH**2 * powers[1, i]
                    twice[k, row] = other[:rows_lon]
                value = value + (factor[m - 1] * SMOOTH**m) * powers[m - 1, i]
            smooth[k, row] = value[:rows_lon]
        return carry

    lax.fori_loop(0, count, one, 0, unroll=count)


def far_kernel(lat_b, smooth_near, twice_near, smooth, twice, powers):
    count, rows_lat, rows_lon, _ = lat_b.shape
    turned = row_turner(rows_lat)
    factor = (4.0, 6.0, 4.0, 1.0)
    powers[:, :, rows_lon:] = jnp.zeros_like(powers[:, :, rows_lon:])

    def one(k, carry):
        for c in range(rows_lon // 8):
            cols = slice(8 * c, 8 * c + 8)
            line = {rows_lat + r: lat_b[k, turned(r), cols] for r in range(HALO)}
            for m in range(1, HALO + 1):
                fresh = {}
                for i in range(rows_lat - m, rows_lat + HALO - m):
                    terms = [line[n] for n in (i - 1, i + 1) if n in line]
                    fresh[i] = sum(terms[1:], terms[0])
                line = fresh
                for i in range(max(rows_lat - m, 0), rows_lat):
                    powers[m - 1, i, cols] = line[i]
        for i in range(rows_lat):
            row = turned(i)
            value = None
            for m in range(max(rows_lat - i, 1), HALO + 1):
                fresh = (factor[m - 1] * SMOOTH**m) * powers[m - 1, i]
                value = fresh if value is None else ring_step(value) + fresh
            smooth[k, row] = smooth_near[k, row] + value[:rows_lon]
            value = twice_near[k, row]
            if i >= rows_lat - 1:
                value = value + ring_step((2.0 * SMOOTH) * powers[0, i])[:rows_lon]
            if i >= rows_lat - 2:
                value = value + SMOOTH**2 * powers[1, i, :rows_lon]
            twice[k, row] = value
        return carry

    lax.fori_loop(0, count, one, 0, unroll=count)


def observe(smooth, cross, corner_a, corner_b, mixed, squares, ivert, weights, ens):
    members, windows, rows_lat, rows_lon, levels = ens_shape(ens)
    block = rows_lat * rows_lon
    shape = (rows_lat, rows_lon, levels)
    for k in range(members + 1):
        square = squares[0] if k < members else squares[1]
        pair = jnp.concatenate(halves(with_sides(smooth, cross, corner_a, corner_b, k, 4)), axis=1)
        product = short_dot(pair, square)
        mixed[k] = (product[:, :levels] + product[:, levels:]).reshape(shape)
    slots = weights.shape[1]
    image = jnp.zeros((8, slots), F32)
    high, low = halves(ivert[...])
    rows_of = jnp.concatenate([high, high, low], axis=0)
    for t in range(windows):
        lines = []
        for a in range(rows_lat):
            total = mixed[members, a]
            for k in range(members):
                total = total + member(ens, k)[t, a].astype(F32) * mixed[k, a]
            lines.append(total)
        increment = jnp.stack(lines).reshape(block, levels)
        high, low = halves(increment)
        seen = short_dot(jnp.concatenate([high, low, high], axis=1), rows_of)
        seen = seen * weights[t * block : (t + 1) * block]
        image = image + jnp.sum(seen.reshape(block // 8, 8, slots), axis=0)
    return jnp.sum(image, axis=0, keepdims=True)


def middle_kernel(
    smooth, cross, corner_a, corner_b, feat, ivert, head, rest, weights, high_weights, low_weights, squares,
    image, fields, edge_a, edge_b,
    mixed, grad,
):
    ens = (head, rest)
    seen = observe(smooth, cross, corner_a, corner_b, mixed, squares, ivert, weights, ens)
    scaled = seen * feat[7:8]
    image[...] = jnp.zeros_like(image)
    image[0:1] = seen
    image[1:2] = scaled
    outs = (fields, edge_a, edge_b)
    adjoint_fields(scaled, high_weights, low_weights, ivert, ens, (), grad, outs)


def last_kernel(
    slots,
    smooth, cross, corner_a, corner_b, vert_hbm, static_hbm,
    feat, ivert, head, rest, weights, squares, image, twice,
    send, late,
    mixed, terms, vert_loc, static_vert, sems,
):
    matrices = fetch((vert_hbm, static_hbm), (vert_loc, static_vert), sems)
    ens = (head, rest)
    second = observe(smooth, cross, corner_a, corner_b, mixed, squares, ivert, weights, ens)
    wait_all(matrices)
    to_control(twice, cross, corner_a, corner_b, vert_loc, static_vert, late)
    start = feat[6:7]
    rinv = feat[7:8]
    first = image[0:1]
    scaled = image[1:2]
    norm = jnp.sum(start * first, axis=1, keepdims=True)
    curve = norm + jnp.sum(first * scaled, axis=1, keepdims=True)
    guess = jnp.where(curve > 0.0, norm / jnp.where(curve > 0.0, curve, 1.0), 1.0)
    guess = jnp.clip(guess, 0.0, 1.0)
    ahead = start + scaled
    ahead_image = first + second
    rest = start - guess * ahead
    rest_image = first - guess * ahead_image
    products = (
        start * first,
        first * scaled,
        rest * rest_image,
        rest * ahead_image + ahead * rest_image,
        ahead * ahead_image,
        rest_image * rinv * rest_image,
        2.0 * rest_image * rinv * ahead_image,
        ahead_image * rinv * ahead_image,
        2.0 * rest_image * scaled,
        2.0 * ahead_image * scaled,
        start * rest_image + rest * first,
        start * ahead_image + ahead * first,
    )
    terms[...] = jnp.zeros_like(terms)
    for n, value in enumerate(products):
        terms[n : n + 1] = value
    sums = jnp.sum(terms[...], axis=1, keepdims=True)
    owners = send.shape[0]
    per = LANES // slots
    below, across = iota((16, LANES), 0), iota((16, LANES), 1)
    line = jnp.sum(
        jnp.where(across == below + 2 * slots, sums, 0.0), axis=0, keepdims=True
    )
    spot = iota((owners, LANES), 1)
    source = spot - (iota((owners, LANES), 0) & (per - 1)) * slots
    mine = within(source, slots)
    parts = []
    targets = []
    target = iota((LANES, LANES), 0)
    slot = iota((LANES, LANES), 1) & (slots - 1)
    for n, value in enumerate((first, second)):
        groups = [
            jnp.broadcast_to(value[:, g * LANES : (g + 1) * LANES], (per, LANES))
            for g in range(owners // per)
        ]
        parts += halves(jnp.where(mine, jnp.concatenate(groups, axis=0), 0.0))
        targets += [(target == slot + n * slots).astype(F32).astype(BF16)] * 2
    moved = short_dot(
        jnp.concatenate(parts, axis=1), jnp.concatenate(targets, axis=1), ((1,), (1,))
    )
    tail = jnp.where(spot == 2 * slots + GUESS, guess, line)
    send[...] = jnp.where(spot < 2 * slots, moved, tail)


def to_control(smooth, cross, corner_a, corner_b, vert_loc, static_vert, control):
    count, rows_lat, rows_lon, levels = smooth.shape
    blocks = []
    for scale, matrix in ((BETA_ENSEMBLE, vert_loc), (BETA_STATIC, static_vert)):
        high, low = halves(scale * matrix[...])
        upper = jnp.concatenate([high, high], axis=1)
        lower = jnp.concatenate([low, jnp.zeros_like(low)], axis=1)
        blocks.append(jnp.concatenate([upper, lower], axis=0))
    for k in range(count):
        pair = jnp.concatenate(halves(with_sides(smooth, cross, corner_a, corner_b, k, 2)), axis=1)
        product = short_dot(pair, blocks[k // (count - 1)], ((1,), (1,)))
        product = product[:, :levels] + product[:, levels:]
        control[k] = product.reshape(rows_lat, rows_lon, levels)


def control_kernel(
    twice, cross, corner_a, corner_b, vert_hbm, static_hbm, control, vert_loc, static_vert, sems
):
    wait_all(fetch((vert_hbm, static_hbm), (vert_loc, static_vert), sems))
    to_control(twice, cross, corner_a, corner_b, vert_loc, static_vert, control)


def final_kernel(
    recv, early, late, dest_hbm, lane_hbm,
    static_hbm, member_hbm, equivalent_hbm,
    dest, lane, equivalent, result, sems, out_sems,
):
    small = fetch((dest_hbm, lane_hbm), (dest, lane), sems)
    count = early.shape[0]
    owners = recv.shape[0]
    rows = dest.shape[1]
    slots = 2 * rows // owners
    blocks = recv[...]
    sums = jnp.sum(blocks, axis=0, keepdims=True)

    def pick(values, n):
        return values[:, 2 * slots + n : 2 * slots + n + 1]

    norm = pick(sums, 0)
    step = norm / (norm + pick(sums, 1))
    off = pick(blocks, GUESS) - step
    linear = jnp.sum(off * blocks, axis=0, keepdims=True)
    square = jnp.sum(off * off * blocks, axis=0, keepdims=True)
    norm_next = jnp.maximum(pick(sums, 2) + pick(linear, 3) + pick(square, 4), 0.0)
    beta = norm_next / norm
    bend = pick(sums, 5) + pick(linear, 6) + pick(square, 7)
    bend = bend + beta * (pick(sums, 8) + pick(linear, 9)) + beta * beta * pick(sums, 1)
    length = norm_next + beta * (pick(sums, 10) + pick(linear, 11)) + beta * beta * norm
    curve = length + bend
    step_next = jnp.where(curve > 0.0, norm_next / jnp.where(curve > 0.0, curve, 1.0), 0.0)
    step_next = jnp.minimum(step_next, 1.0)
    near = step + step_next * ((1.0 - step) + beta)
    far = -step_next * step
    stores = []
    near, far = jnp.sum(near), jnp.sum(far)
    for k in range(count):
        result[k] = near * early[k] + far * late[k]
        target = member_hbm.at[k] if k < count - 1 else static_hbm
        stores.append(pltpu.make_async_copy(result.at[k], target, out_sems.at[k]))
        stores[k].start()
    wait_all(small)
    chosen = (iota((owners, rows), 0) == dest[...]).astype(F32).astype(BF16)
    table = short_dot(
        jnp.concatenate(halves(blocks), axis=0),
        jnp.concatenate([chosen] * 2, axis=0),
        ((0,), (0,)),
    )
    spot = iota((LANES, rows), 0)
    factor = jnp.where(spot == lane[...], near, 0.0)
    factor = jnp.where(spot == lane[...] + slots, far, factor)
    equivalent[...] = jnp.sum(factor * table, axis=0, keepdims=True)
    stores.append(pltpu.make_async_copy(equivalent, equivalent_hbm, out_sems.at[count]))
    stores[count].start()
    wait_all(stores)


def shape(*dims):
    return jax.ShapeDtypeStruct(dims, F32)


def stay(*values):
    return [pltpu.with_memory_space_constraint(value, pltpu.HBM) for value in values]


def swaps(count, ring):
    inner = [(i, i ^ 1) for i in range(count)]
    outer = []
    for i in range(1, count - 1, 2):
        outer += [(i, i + 1), (i + 1, i)]
    if ring:
        outer += [(count - 1, 0), (0, count - 1)]
    return inner, outer


def body(
    ensemble,
    vert_loc,
    static_vert,
    inst_vert,
    inst_err,
    obs_dest,
    obs_patch,
    obs_window,
    obs_inst,
    obs_hweight,
    innovation,
    obs_count,
):
    members, windows, rows_lat, rows_lon, levels = ensemble.shape
    lat_count = lax.axis_size("lat")
    lon_count = lax.axis_size("lon")
    owners = lat_count * lon_count
    rows = innovation.shape[0]
    slots = 2 * rows // owners
    total = owners * slots
    patches = rows_lat // 2 * (rows_lon // 2)
    count = members + 1
    lat_inner, lat_outer = swaps(lat_count, False)
    lon_inner, lon_outer = swaps(lon_count, True)
    tile = shape(count, rows_lat, rows_lon, levels)
    edge = shape(count, rows_lat, HALO, levels)

    def line(values):
        return values.reshape(1, rows)

    dest = line(obs_dest)
    row_scratch = pltpu.VMEM((1, rows), jnp.int32)
    early_members = members // 2
    send, lane, head = pl.pallas_call(
        functools.partial(pack_kernel, slots, patches),
        out_shape=(
            shape(owners, LANES),
            pltpu.HBM((1, rows), jnp.int32),
            jax.ShapeDtypeStruct((early_members,) + ensemble.shape[1:], ensemble.dtype),
        ),
        in_specs=[HBM] * 6 + [SMEM, HBM],
        out_specs=(VMEM, HBM, VMEM),
        scratch_shapes=[row_scratch] * 4
        + [
            pltpu.VMEM(obs_hweight.shape, F32),
            pltpu.VMEM((1, rows), F32),
            pltpu.VMEM((8, rows), F32),
            row_scratch,
            pltpu.VMEM((LANES, rows), F32),
            DMA((8,)),
        ],
        compiler_params=PARAMS,
        name="pack",
    )(
        *stay(
            dest,
            line(obs_patch),
            line(obs_window),
            line(obs_inst),
            obs_hweight,
            line(innovation),
        ),
        obs_count,
        *stay(ensemble),
    )
    squares = pl.pallas_call(
        prepare_kernel,
        out_shape=jax.ShapeDtypeStruct((2, 2 * levels, 2 * levels), BF16),
        compiler_params=PARAMS,
        name="prepare",
    )(vert_loc, static_vert)

    def exchange(blocks):
        return lax.all_to_all(blocks, ("lat", "lon"), split_axis=0, concat_axis=0, tiled=True)

    recv = exchange(send)
    cells = windows * rows_lat * rows_lon
    tile_scratch = pltpu.VMEM(tile.shape, F32)
    grad_scratch = pltpu.VMEM((cells, levels), F32)

    feat, ivert, rest, *weights, fields, edge_a, edge_b = pl.pallas_call(
        functools.partial(first_kernel, slots),
        out_shape=(
            shape(8, total),
            shape(levels, total),
            jax.ShapeDtypeStruct((members - early_members,) + ensemble.shape[1:], ensemble.dtype),
            shape(cells, total),
            jax.ShapeDtypeStruct((cells, total), BF16),
            jax.ShapeDtypeStruct((cells, total), BF16),
            tile,
            edge,
            edge,
        ),
        in_specs=[VMEM, HBM, HBM, HBM, VMEM],
        out_specs=(VMEM,) * 9,
        scratch_shapes=[
            pltpu.VMEM(inst_vert.shape, F32),
            pltpu.VMEM((1, inst_err.shape[0]), F32),
            grad_scratch,
            DMA((2 + members - early_members,)),
        ],
        compiler_params=PARAMS,
        name="first",
    )(recv, *stay(inst_vert, inst_err.reshape(1, -1), ensemble), head)

    def sides(part_a, part_b):
        return pl.pallas_call(
            sides_kernel,
            out_shape=(
                shape(count, rows_lat, 8, levels),
                shape(count, 2, 8, levels),
            ),
            in_specs=[VMEM] * 2,
            out_specs=(VMEM,) * 2,
            compiler_params=PARAMS,
            name="sides",
        )(part_a, part_b)

    def halo(fields, edge_a, edge_b):
        lat_b = lax.ppermute(fields, "lat", lat_outer)
        side_a = lax.ppermute(edge_a, "lon", lon_inner)
        side_b = lax.ppermute(edge_b, "lon", lon_outer)
        lat_a = lax.ppermute(fields, "lat", lat_inner)
        cross, folded = sides(side_a, side_b)
        corner_b = lax.ppermute(folded, "lat", lat_outer)
        corner_a = lax.ppermute(cross, "lat", lat_inner)
        powers = pltpu.VMEM((HALO, rows_lat, rows_lon + 8, levels), F32)
        smooth, twice = pl.pallas_call(
            near_kernel,
            out_shape=(tile, tile),
            in_specs=[VMEM] * 2,
            out_specs=(VMEM,) * 2,
            scratch_shapes=[powers],
            compiler_params=PARAMS,
            name="near",
        )(fields, lat_a)
        smooth, twice = pl.pallas_call(
            far_kernel,
            out_shape=(tile, tile),
            in_specs=[VMEM] * 3,
            out_specs=(VMEM,) * 2,
            scratch_shapes=[powers],
            compiler_params=PARAMS,
            name="far",
        )(lat_b, smooth, twice)
        return smooth, twice, cross, corner_a, corner_b


    smooth, twice, cross, corner_a, corner_b = halo(fields, edge_a, edge_b)
    matrix_scratch = pltpu.VMEM(vert_loc.shape, F32)
    image, *outs = pl.pallas_call(
        middle_kernel,
        out_shape=(shape(8, total), tile, edge, edge),
        in_specs=[VMEM] * 12,
        out_specs=(VMEM,) * 4,
        scratch_shapes=[tile_scratch, grad_scratch],
        compiler_params=PARAMS,
        name="middle",
    )(smooth, cross, corner_a, corner_b, feat, ivert, head, rest, *weights, squares)
    early = pl.pallas_call(
        control_kernel,
        out_shape=tile,
        in_specs=[VMEM] * 4 + [HBM] * 2,
        out_specs=VMEM,
        scratch_shapes=[matrix_scratch, matrix_scratch, DMA((2,))],
        compiler_params=PARAMS,
        name="control",
    )(twice, cross, corner_a, corner_b, *stay(vert_loc, static_vert))
    smooth, twice, cross, corner_a, corner_b = halo(*outs)
    send, late = pl.pallas_call(
        functools.partial(last_kernel, slots),
        out_shape=(shape(owners, LANES), tile),
        in_specs=[VMEM] * 4 + [HBM] * 2 + [VMEM] * 8,
        out_specs=(VMEM,) * 2,
        scratch_shapes=[
            tile_scratch,
            pltpu.VMEM((16, total), F32),
            matrix_scratch,
            matrix_scratch,
            DMA((2,)),
        ],
        compiler_params=PARAMS,
        name="last",
    )(
        smooth,
        cross,
        corner_a,
        corner_b,
        *stay(vert_loc, static_vert),
        feat,
        ivert,
        head,
        rest,
        weights[0],
        squares,
        image,
        twice,
    )
    recv = exchange(send)
    static, member, equivalent = pl.pallas_call(
        final_kernel,
        out_shape=(
            shape(rows_lat, rows_lon, levels),
            shape(members, rows_lat, rows_lon, levels),
            shape(1, rows),
        ),
        in_specs=[VMEM] * 3 + [HBM] * 2,
        out_specs=(HBM,) * 3,
        scratch_shapes=[
            row_scratch,
            row_scratch,
            pltpu.VMEM((1, rows), F32),
            tile_scratch,
            DMA((2,)),
            DMA((count + 1,)),
        ],
        compiler_params=PARAMS,
        name="final",
    )(recv, early, late, *stay(dest, lane))
    return static, member, equivalent.reshape(rows)


def solution(mesh):
    return jax.shard_map(
        body,
        mesh=mesh,
        in_specs=(
            P(None, None, "lat", "lon", None),
            P(),
            P(),
            P(),
            P(),
            P(("lat", "lon"), None),
            P(("lat", "lon")),
            P(("lat", "lon")),
            P(("lat", "lon")),
            P(None, ("lat", "lon")),
            P(("lat", "lon")),
            P(("lat", "lon")),
        ),
        out_specs=(P("lat", "lon", None), P(None, "lat", "lon", None), P(("lat", "lon"))),
        check_vma=False,
    )
```
